32 devices in a mesh: box: 4 (over y, core), dir: 8 (over z, x).
Axes of the slice: x: 2, y: 2, z: 4, core: 2. Of those that a mesh axis runs over, the one named last changes fastest.
Arguments:
- child_rad: float32 [64, 2, 128, 256], P('box', None, 'dir'), may hold values from -6 to 6
- parent_incoming: float32 [16, 2, 256, 512], P('box', None, 'dir'), may hold values from -6 to 6
- theta_interp: float32 [256, 128], replicated, may hold values from -0.5 to 0.5
- phi_interp: float32 [256, 512], replicated, may hold values from -0.375 to 0.375
- child_ops: float32 [40, 2, 128, 256], P(None, None, 'dir'), may hold values from -2 to 2
- parent_ops: float32 [40, 2, 256, 512], P(None, None, 'dir'), may hold values from -2 to 2
- child_parent: int32 [64], P('box'), may hold values from 0 to 15, as said below
- child_octant: int32 [64], P('box'), may hold values from 0 to 7, as said below
- far_child_src: int32 [64, 16], P('box'), may hold values from 0 to 63, as said below
- far_child_op: int32 [64, 16], P('box'), may hold values from 0 to 39
- far_child_len: int32 [64], P('box'), may hold values from 1 to 16
- far_parent_src: int32 [16, 8], P('box'), may hold values from 0 to 15, as said below
- far_parent_op: int32 [16, 8], P('box'), may hold values from 0 to 39
- far_parent_len: int32 [16], P('box'), may hold values from 1 to 8
Outputs:
- child_local: float32 [64, 2, 128, 256], P('box', None, 'dir')
- parent_local: float32 [16, 2, 256, 512], P('box', None, 'dir')
- parent_rad: float32 [16, 2, 256, 512], P('box', None, 'dir')
The draws below stay inside these ranges and needn't reach their ends.
Inputs may be any that keep to these rules, and one draw needn't show every extreme that they name: child_parent never falls; the children of parents 4 q to 4 q + 3 are exactly children 16 q to 16 q + 15, every parent has 2 to 6 children. `child_octant`: children of one parent have distinct octants. far_child_src[c, k] differs from c, and far_child_src[c, k] // 16 differs from c // 16 by at most 1. far_parent_src[p, k] differs from p, and far_parent_src[p, k] // 4 differs from p // 4 by at most 1.
All inputs are finite; a program needn't handle non-finite values.
Results may differ from the reference program's by a relative error of at most 0.0003.
Values sent between devices are 32-bit elements; how exact they have to be, the bound alone decides.
A program may use at most 64 MiB of HBM per device.

```python
import math
import jax
import jax.numpy as jnp
from jax import lax

THC = 128
PHC = 256
THP = 256
PHP = 512
MF = 16
MFP = 8
NOPS = 40
PB_DEV = 4
CB_DEV = 16
NC = 64
NP = 16


def tree_parts(key):
    subkey = jax.random.fold_in(key, 7)
    first_key, second_key = jax.random.split(subkey)
    offsets = jax.random.randint(first_key, (NP // 2,), -2, 3).astype(jnp.int32)
    counts = jnp.stack([4 + offsets, 4 - offsets], axis=1).reshape(NP)
    ends = jnp.cumsum(counts).astype(jnp.int32)
    starts = ends - counts
    children = jnp.arange(NC, dtype=jnp.int32)
    parent = jnp.sum((ends[None, :] <= children[:, None]).astype(jnp.int32), axis=1).astype(jnp.int32)
    position = children - starts[parent]
    orders = jax.vmap(lambda single: jax.random.permutation(single, 8))(jax.random.split(second_key, NP))
    octant = orders[parent, position].astype(jnp.int32)
    return (parent, octant)


def far_lists(key, per_device, total_boxes, longest, salt_value):
    subkey = jax.random.fold_in(key, salt_value)
    keys = jax.random.split(subkey, 6)
    boxes = jnp.arange(total_boxes, dtype=jnp.int32)
    block_index = boxes // per_device
    block_total = total_boxes // per_device
    window_low = jnp.maximum(block_index - 1, 0) * per_device
    window_high = jnp.minimum(block_index + 2, block_total) * per_device
    window_span = window_high - window_low - 1
    raw_bits = jax.random.randint(keys[0], (total_boxes, longest), 0, 1 << 30)
    candidate = window_low[:, None] + raw_bits % window_span[:, None]
    source = (candidate + (candidate >= boxes[:, None]).astype(jnp.int32)).astype(jnp.int32)
    which_op = jax.random.randint(keys[1], (total_boxes, longest), 0, NOPS).astype(jnp.int32)
    heavy = jax.random.randint(keys[2], (block_total,), 0, 4) == 0
    light_len = 1 + jax.random.randint(keys[3], (total_boxes,), 0, 1 << 30) % max(longest // 4, 1)
    heavy_len = 1 + jax.random.randint(keys[4], (total_boxes,), 0, 1 << 30) % longest
    length = jnp.where(heavy[block_index], heavy_len, light_len)
    chosen_box = jax.random.randint(keys[5], (), 0, total_boxes)
    length = jnp.where(boxes == chosen_box, longest, length).astype(jnp.int32)
    return (source, which_op, length)


def draw_child_parent(key, part):
    return tree_parts(key)[0]


def draw_child_octant(key, part):
    return tree_parts(key)[1]


def draw_far_child_src(key, part):
    return far_lists(key, CB_DEV, NC, MF, 11)[0]


def draw_far_child_op(key, part):
    return far_lists(key, CB_DEV, NC, MF, 11)[1]


def draw_far_child_len(key, part):
    return far_lists(key, CB_DEV, NC, MF, 11)[2]


def draw_far_parent_src(key, part):
    return far_lists(key, PB_DEV, NP, MFP, 23)[0]


def draw_far_parent_op(key, part):
    return far_lists(key, PB_DEV, NP, MFP, 23)[1]


def draw_far_parent_len(key, part):
    return far_lists(key, PB_DEV, NP, MFP, 23)[2]


def shard_levels(own_key, extent, pieces, least, high):
    level = 1.0
    for axis_at, shards_of in pieces:
        heights = jax.random.uniform(jax.random.fold_in(jax.random.fold_in(own_key, 6), axis_at), (shards_of,), jnp.float32, least / len(pieces), high / len(pieces))
        level = level * jnp.repeat(jnp.exp(heights), extent[axis_at] // shards_of).reshape((-1,) + (1,) * (len(extent) - 1 - axis_at))
    return level


def noise(stream_key, extent, width, reach, pieces=(), kind=jnp.bfloat16):
    loudness = shard_levels(stream_key, extent, pieces, -0.22, 0.18) if pieces else 1.0
    array = jax.random.normal(stream_key, extent, jnp.float32) * width * loudness
    return jnp.minimum(jnp.maximum(array, -reach), reach).astype(kind)


def setup_inputs(seed: int = 0) -> dict:
    key_list = jax.random.split(jax.random.key(seed), 15)
    child_rad = noise(key_list[0], (NC, 2, THC, PHC), 1.0, 6.0, ((0, 4), (2, 8)), jnp.float32)
    parent_incoming = noise(key_list[1], (NP, 2, THP, PHP), 1.0, 6.0, ((0, 4), (2, 8)), jnp.float32)
    theta_interp = noise(key_list[2], (THP, THC), THC ** -0.5, 0.5, (), jnp.float32)
    phi_interp = noise(key_list[3], (PHC, PHP), PHC ** -0.5, 0.375, (), jnp.float32)
    child_ops = noise(key_list[4], (NOPS, 2, THC, PHC), 0.3, 2.0, ((2, 8),), jnp.float32)
    parent_ops = noise(key_list[5], (NOPS, 2, THP, PHP), 0.3, 2.0, ((2, 8),), jnp.float32)
    child_parent = draw_child_parent(jax.random.fold_in(key_list[14], 71), 0)
    child_octant = draw_child_octant(jax.random.fold_in(key_list[14], 71), 0)
    far_child_src = draw_far_child_src(jax.random.fold_in(key_list[14], 71), 0)
    far_child_op = draw_far_child_op(jax.random.fold_in(key_list[14], 71), 0)
    far_child_len = draw_far_child_len(jax.random.fold_in(key_list[14], 71), 0)
    far_parent_src = draw_far_parent_src(jax.random.fold_in(key_list[14], 71), 0)
    far_parent_op = draw_far_parent_op(jax.random.fold_in(key_list[14], 71), 0)
    far_parent_len = draw_far_parent_len(jax.random.fold_in(key_list[14], 71), 0)
    return {"child_rad": child_rad, "parent_incoming": parent_incoming, "theta_interp": theta_interp, "phi_interp": phi_interp, "child_ops": child_ops, "parent_ops": parent_ops, "child_parent": child_parent, "child_octant": child_octant, "far_child_src": far_child_src, "far_child_op": far_child_op, "far_child_len": far_child_len, "far_parent_src": far_parent_src, "far_parent_op": far_parent_op, "far_parent_len": far_parent_len}


phase_scale = 6.0
highest = lax.Precision.HIGHEST


def octant_signs(octant):
    first = 1.0 - 2.0 * (octant % 2).astype(jnp.float32)
    second = 1.0 - 2.0 * ((octant // 2) % 2).astype(jnp.float32)
    third = 1.0 - 2.0 * ((octant // 4) % 2).astype(jnp.float32)
    return first, second, third


def phase_parts(octant, row_start, row_count, total_rows, col_count):
    angle_rows = (row_start + jnp.arange(row_count)).astype(jnp.float32)
    theta = math.pi * (angle_rows + 0.5) / total_rows
    azimuth = 2.0 * math.pi * jnp.arange(col_count).astype(jnp.float32) / col_count
    sin_theta = jnp.sin(theta)[:, None]
    along_x = sin_theta * jnp.cos(azimuth)[None, :]
    along_y = sin_theta * jnp.sin(azimuth)[None, :]
    along_z = jnp.cos(theta)[:, None] + 0.0 * azimuth[None, :]
    first, second, third = octant_signs(octant)
    argument = phase_scale * (first[:, None, None] * along_x + second[:, None, None] * along_y + third[:, None, None] * along_z)
    return jnp.cos(argument), jnp.sin(argument)


def translate(patterns, operators, source, which_op, length):
    start = jnp.zeros((source.shape[0],) + patterns.shape[1:], jnp.float32)

    def advance(total, column):
        picked = patterns[source[:, column]]
        chosen = operators[which_op[:, column]]
        live = (column < length).astype(jnp.float32)[:, None, None]
        real_part = chosen[:, 0] * picked[:, 0] - chosen[:, 1] * picked[:, 1]
        imag_part = chosen[:, 0] * picked[:, 1] + chosen[:, 1] * picked[:, 0]
        return total + jnp.stack([live * real_part, live * imag_part], axis=1), None

    result, unused = lax.scan(advance, start, jnp.arange(source.shape[1]))
    return result


def reference(child_rad, parent_incoming, theta_interp, phi_interp, child_ops, parent_ops, child_parent, child_octant, far_child_src, far_child_op, far_child_len, far_parent_src, far_parent_op, far_parent_len):
    along_phi = jnp.einsum("nctf,fg->nctg", child_rad, phi_interp, precision=highest)
    interp = jnp.einsum("jt,nctg->ncjg", theta_interp, along_phi, precision=highest)
    cosine, sine = phase_parts(child_octant, 0, THP, THP, PHP)
    shifted = jnp.stack([cosine * interp[:, 0] - sine * interp[:, 1], sine * interp[:, 0] + cosine * interp[:, 1]], axis=1)
    member = (child_parent[None, :] == jnp.arange(NP)[:, None]).astype(jnp.float32)
    parent_rad = jnp.einsum("pn,ncjg->pcjg", member, shifted, precision=highest)
    parent_local = parent_incoming + translate(parent_rad, parent_ops, far_parent_src, far_parent_op, far_parent_len)
    gathered = parent_local[child_parent]
    unshift = jnp.stack([cosine * gathered[:, 0] + sine * gathered[:, 1], cosine * gathered[:, 1] - sine * gathered[:, 0]], axis=1)
    back_theta = jnp.einsum("jt,ncjg->nctg", theta_interp, unshift, precision=highest)
    anterp = jnp.einsum("nctg,fg->nctf", back_theta, phi_interp, precision=highest)
    child_local = translate(child_rad, child_ops, far_child_src, far_child_op, far_child_len) + anterp
    return child_local, parent_local, parent_rad
```

```python
import functools
import math

import jax
import jax.numpy as jnp
from jax import lax
from jax.experimental import pallas as pl
from jax.experimental.pallas import tpu as pltpu
from jax.sharding import PartitionSpec as P

phase_scale = 6.0
highest = lax.Precision.HIGHEST


def neighbours(array):
    size = lax.axis_size("box")
    up = [(i, i + 1) for i in range(size - 1)]
    down = [(i + 1, i) for i in range(size - 1)]
    return lax.ppermute(array, "box", up), lax.ppermute(array, "box", down)


def octant_signs(octant):
    first = 1.0 - 2.0 * (octant % 2).astype(jnp.float32)
    second = 1.0 - 2.0 * (octant // 2 % 2).astype(jnp.float32)
    third = 1.0 - 2.0 * (octant // 4 % 2).astype(jnp.float32)
    return (first, second, third)


def phase_block(octant, row_start, row_count, total_rows, col_start, col_count, total_cols):
    angle_rows = (row_start + jnp.arange(row_count, dtype=jnp.int32)).astype(jnp.float32)
    theta = math.pi * (angle_rows + 0.5) / total_rows
    angle_cols = (col_start + jnp.arange(col_count, dtype=jnp.int32)).astype(jnp.float32)
    azimuth = 2.0 * math.pi * angle_cols / total_cols
    sin_theta = jnp.sin(theta)[:, None]
    along_x = sin_theta * jnp.cos(azimuth)[None, :]
    along_y = sin_theta * jnp.sin(azimuth)[None, :]
    along_z = jnp.cos(theta)[:, None] + 0.0 * azimuth[None, :]
    first, second, third = octant_signs(octant)
    argument = phase_scale * (
        first[:, None, None] * along_x
        + second[:, None, None] * along_y
        + third[:, None, None] * along_z
    )
    return (jnp.cos(argument), jnp.sin(argument))


def flipped(index, mask):
    result = index
    bit = 1
    while bit <= mask:
        if mask & bit:
            result = result + bit - 2 * bit * lax.rem(lax.div(index, bit), 2)
        bit *= 2
    return result


def exchange_body(count, around, fields, matrix_ref, x_ref, *refs):
    refs = list(refs)
    out_ref = refs.pop(0)
    if around:
        below_ref, above_ref = refs.pop(0), refs.pop(0)
    got, ready, landed, send_sem, recv_sem = refs[:5]
    me = lax.axis_index("dir")
    planes, depth, width = got.shape[1:]
    rows = ready.shape[2]
    mesh_ids = pl.DeviceIdType.MESH
    barrier = pltpu.get_barrier_semaphore()
    steps = range(count - 1, 0, -1)

    def partner(step):
        if count & (count - 1):
            return lax.rem(me + step, count), lax.rem(me + count - step, count)
        peer = flipped(me, step)
        return peer, peer

    for step in steps:
        pl.semaphore_signal(
            barrier, inc=1, device_id={"dir": partner(step)[0]}, device_id_type=mesh_ids
        )
    greeted = count - 1
    if around:
        box = lax.axis_index("box")
        upper = lax.rem(box + 1, fields)
        lower = lax.rem(box + fields - 1, fields)
        for other in (upper, lower):
            pl.semaphore_signal(
                barrier, inc=1, device_id={"box": other}, device_id_type=mesh_ids
            )
        greeted += 2
    pl.semaphore_wait(barrier, greeted)

    def push(source, target, leg, plane):
        for step in steps:
            peer, _ = partner(step)
            copy = pltpu.make_async_remote_copy(
                src_ref=source.at[peer, plane],
                dst_ref=target.at[me, plane],
                send_sem=send_sem.at[leg, plane, step],
                recv_sem=recv_sem.at[leg, plane, step],
                device_id={"dir": peer},
                device_id_type=mesh_ids,
            )
            copy.start()
            started.append(copy)

    def settle(target, leg, plane):
        for step in steps:
            _, origin = partner(step)
            pltpu.make_async_remote_copy(
                src_ref=target.at[origin, plane],
                dst_ref=target.at[origin, plane],
                send_sem=send_sem.at[leg, plane, step],
                recv_sem=recv_sem.at[leg, plane, step],
                device_id={"dir": origin},
                device_id_type=mesh_ids,
            ).wait_recv()

    started = []
    for plane in range(planes):
        push(x_ref, got, 0, plane)
    got[me] = x_ref[me]
    for plane in range(planes):
        settle(got, 0, plane)
        product = lax.dot_general(
            matrix_ref[...],
            got[:, plane].reshape(count * depth, width),
            (((1 if around else 0,), (0,)), ((), ())),
            precision=lax.Precision.HIGH,
            preferred_element_type=jnp.float32,
        )
        ready[:, plane] = product.reshape(count, rows, width)
        push(ready, landed, 1, plane)
    ring = []
    if around:
        box_send, box_recv = refs[5:7]
        for at, (other, target) in enumerate(((upper, below_ref), (lower, above_ref))):
            copy = pltpu.make_async_remote_copy(
                src_ref=x_ref,
                dst_ref=target,
                send_sem=box_send.at[at],
                recv_sem=box_recv.at[at],
                device_id={"box": other},
                device_id_type=mesh_ids,
            )
            copy.start()
            ring.append(copy)
    landed[me] = ready[me]
    for plane in range(planes):
        settle(landed, 1, plane)
    out_ref[...] = landed[...].reshape(out_ref.shape)
    for copy in started:
        copy.wait_send()
    for copy in ring:
        copy.wait()


def exchange(matrix, x, around, which):
    count, planes, depth, width = x.shape
    rows = matrix.shape[0 if around else 1] // count
    operands = (matrix, x)
    vmem = pl.BlockSpec(memory_space=pltpu.VMEM)
    result = jax.ShapeDtypeStruct((count * planes, rows, width), jnp.float32)
    ring = jax.ShapeDtypeStruct(x.shape, jnp.float32)
    scratch = [
        pltpu.VMEM((count, planes, depth, width), jnp.float32),
        pltpu.VMEM((count, planes, rows, width), jnp.float32),
        pltpu.VMEM((count, planes, rows, width), jnp.float32),
        pltpu.SemaphoreType.DMA((2, planes, count)),
        pltpu.SemaphoreType.DMA((2, planes, count)),
    ]
    if around:
        scratch += [pltpu.SemaphoreType.DMA((2,)), pltpu.SemaphoreType.DMA((2,))]
    return pl.pallas_call(
        functools.partial(exchange_body, count, around, lax.axis_size("box")),
        out_shape=(result, ring, ring) if around else result,
        in_specs=[vmem] * len(operands),
        out_specs=(vmem,) * 3 if around else vmem,
        scratch_shapes=scratch,
        compiler_params=pltpu.CompilerParams(
            collective_id=which, has_side_effects=True, vmem_limit_bytes=16 * 1024 * 1024
        ),
        name="exchange_" + str(which),
    )(*operands)


def translate_body(has_base, *refs):
    source_ref, which_ref, length_ref, before, own, after, ops_ref = refs[:7]
    base_ref = refs[7] if has_base else None
    out_ref, wide, sems = refs[-3:]
    boxes, _, rows, width = own.shape
    copies = [
        pltpu.make_async_copy(part, wide.at[pl.ds(at * boxes, boxes)], sems.at[at])
        for at, part in enumerate((before, own, after))
    ]
    for copy in copies:
        copy.start()
    for copy in copies:
        copy.wait()
    offset = (lax.axis_index("box") - 1) * boxes
    tall = rows
    while tall % 16 == 0 and tall * width > 4096:
        tall //= 2

    def one_box(box, carry):
        length = length_ref[box]
        for start in range(0, rows, tall):
            part = slice(start, start + tall)

            def entry(column, totals):
                real, imag = totals
                at = source_ref[box, column] - offset
                op = which_ref[box, column]
                op_real, op_imag = ops_ref[op, 0, part], ops_ref[op, 1, part]
                re, im = wide[at, 0, part], wide[at, 1, part]
                real = real + (op_real * re - op_imag * im)
                imag = imag + (op_real * im + op_imag * re)
                return real, imag

            if has_base:
                initial = (base_ref[box, 0, part], base_ref[box, 1, part])
            else:
                initial = (jnp.zeros((tall, width), jnp.float32),) * 2
            real, imag = lax.fori_loop(0, length, entry, initial)
            out_ref[box, 0, part] = real
            out_ref[box, 1, part] = imag
        return carry

    lax.fori_loop(0, boxes, one_box, 0)


def translate(own, before, after, operators, source, which_op, length, base, name):
    boxes = own.shape[0]
    vmem = pl.BlockSpec(memory_space=pltpu.VMEM)
    smem = pl.BlockSpec(memory_space=pltpu.SMEM)
    anywhere = pl.BlockSpec(memory_space=pltpu.HBM)
    operands = [source, which_op, length, before, own, after, operators]
    specs = [smem] * 3 + [anywhere] * 3 + [vmem]
    if base is not None:
        operands.append(base)
        specs.append(vmem)
    return pl.pallas_call(
        functools.partial(translate_body, base is not None),
        out_shape=jax.ShapeDtypeStruct(own.shape, jnp.float32),
        in_specs=specs,
        out_specs=vmem,
        scratch_shapes=[
            pltpu.VMEM((3 * boxes,) + own.shape[1:], jnp.float32),
            pltpu.SemaphoreType.DMA((3,)),
        ],
        compiler_params=pltpu.CompilerParams(vmem_limit_bytes=20 * 1024 * 1024),
        name=name,
    )(*operands)


def shift_body(parent_ref, octant_ref, cosine_ref, sine_ref, interp_ref, out_ref):
    children = interp_ref.shape[0]
    offset = lax.axis_index("box") * out_ref.shape[0]
    out_ref[...] = jnp.zeros_like(out_ref)

    def one_child(child, carry):
        slot, octant = parent_ref[child] - offset, octant_ref[child]
        mirrored = octant // 4
        held = octant + mirrored * (7 - 2 * octant)
        sign = (1 - 2 * mirrored).astype(jnp.float32)
        cosine, sine = cosine_ref[held], sign * sine_ref[held]
        real, imag = interp_ref[child, 0], interp_ref[child, 1]
        out_ref[slot, 0] += cosine * real - sine * imag
        out_ref[slot, 1] += sine * real + cosine * imag
        return carry

    lax.fori_loop(0, children, one_child, 0)


def unshift_body(parent_ref, octant_ref, cosine_ref, sine_ref, field_ref, out_ref):
    children = out_ref.shape[0]
    offset = lax.axis_index("box") * field_ref.shape[0]

    def one_child(child, carry):
        slot, octant = parent_ref[child] - offset, octant_ref[child]
        mirrored = octant // 4
        held = octant + mirrored * (7 - 2 * octant)
        sign = (1 - 2 * mirrored).astype(jnp.float32)
        cosine, sine = cosine_ref[held], sign * sine_ref[held]
        real, imag = field_ref[slot, 0], field_ref[slot, 1]
        out_ref[child, 0] = cosine * real + sine * imag
        out_ref[child, 1] = cosine * imag - sine * real
        return carry

    lax.fori_loop(0, children, one_child, 0)


def by_child(body, parent, octant, cosine, sine, values, boxes, name):
    vmem = pl.BlockSpec(memory_space=pltpu.VMEM)
    smem = pl.BlockSpec(memory_space=pltpu.SMEM)
    return pl.pallas_call(
        body,
        out_shape=jax.ShapeDtypeStruct((boxes,) + values.shape[1:], jnp.float32),
        in_specs=[smem] * 2 + [vmem] * 3,
        out_specs=vmem,
        compiler_params=pltpu.CompilerParams(vmem_limit_bytes=16 * 1024 * 1024),
        name=name,
    )(parent, octant, cosine, sine, values)


def within(index, size):
    return jnp.minimum(jnp.maximum(index, 0), size - 1)


def precise(lhs, rhs):
    return lax.dot_general(
        lhs,
        rhs,
        (((1,), (0,)), ((), ())),
        precision=lax.Precision.HIGH,
        preferred_element_type=jnp.float32,
    )


def parent_windows(children, parents, least, most):
    windows = []
    for p in range(parents):
        low = max(least * p, children - most * (parents - p))
        high = min(most * (p + 1), children - least * (parents - 1 - p))
        windows.append((low, high))
    return windows


def fused_body(fields, per_chunk, *refs):
    tables_h = refs[:8]
    rad_h, incoming_h, theta_h, phi_h, child_ops_h, parent_ops_h = refs[8:14]
    out_ref, local_ref, parent_rad_ref = refs[14:17]
    (theta, phi, phi_t, theta_t, child_ops, parent_ops, near, gathered, spread, rows_in, wide,
     cosine, sine, back, held_rows, partial, other, total, final) = refs[17:36]
    tables = refs[36:44]
    parent_s, octant_s, child_src_s, child_op_s, child_len_s = tables[:5]
    parent_src_s, parent_op_s, parent_len_s = tables[5:]
    (load_sem, half_sem, pre_send, pre_recv, in_send, in_recv, out_send, out_recv, ring_send,
     ring_recv, parent_send, parent_recv, back_send, back_recv, raw_send, raw_recv, swap_send,
     swap_recv, final_send, final_recv) = refs[44:]
    mesh_ids = pl.DeviceIdType.MESH
    me, box = lax.axis_index("dir"), lax.axis_index("box")
    children = parent_s.shape[0]
    parents, _, rows, width = local_ref.shape
    depth = rad_h.shape[1]
    half = gathered.shape[2]
    group = 2 * per_chunk
    chunks = children // per_chunk
    total_rows, total_cols = theta_h.shape[0], width
    z, x = lax.div(me, 2), lax.rem(me, 2)
    side = lax.div(z, 2)
    inner = z == 1 + side
    outer = z != 1 + side
    partner = {"dir": 2 * z + 1 - x}
    outer_peer = [{"dir": 6 * side + at} for at in range(2)]
    inner_peer = {"dir": 2 * (1 + side) + x}
    across_inner = {"dir": 2 * (2 - side) + x}
    across_outer = {"dir": 6 * (1 - side) + x}
    has_lower, has_upper = box > 0, box < fields - 1
    lower, upper = {"box": box - 1}, {"box": box + 1}

    def remote(source, target, send, recv, device):
        return pltpu.make_async_remote_copy(
            src_ref=source, dst_ref=target, send_sem=send, recv_sem=recv,
            device_id=device, device_id_type=mesh_ids,
        )

    def aligned(value, step):
        return pl.ds(pl.multiple_of(value, step), step)

    def part(k):
        return pl.ds(k * group, group)

    loads = [
        (theta_h, theta), (phi_h, phi), (incoming_h, local_ref), (child_ops_h, child_ops),
        (parent_ops_h, parent_ops), (rad_h, near.at[pl.ds(2 * children, 2 * children)]),
    ]
    loads = [
        pltpu.make_async_copy(source, target, load_sem.at[at])
        for at, (source, target) in enumerate(loads)
    ]
    table_loads = [
        pltpu.make_async_copy(source, target, load_sem.at[6 + at])
        for at, (source, target) in enumerate(zip(tables_h, tables))
    ]
    own_half = pl.ds(pl.multiple_of(x * half, half), half)
    other_half = pl.ds(pl.multiple_of((1 - x) * half, half), half)
    own_depth = aligned(2 * depth * z + depth * x, depth)
    halves = [
        pltpu.make_async_copy(
            rad_h.at[part(k), :, own_half], gathered.at[part(k), own_depth], half_sem.at[k]
        )
        for k in range(chunks)
    ]

    def greet(device):
        pl.semaphore_signal(barrier, inc=1, device_id=device, device_id_type=mesh_ids)

    barrier = pltpu.get_barrier_semaphore()
    greet(partner)

    @pl.when(inner)
    def _():
        for device in (outer_peer[0], outer_peer[1], across_inner, across_outer):
            greet(device)

    @pl.when(outer)
    def _():
        for device in ({"dir": 2 * (1 + side)}, {"dir": 2 * (1 + side) + 1}, across_inner):
            greet(device)

    pl.when(has_lower)(lambda: greet(lower))
    pl.when(has_upper)(lambda: greet(upper))
    for copy in halves:
        copy.start()
    for copy in table_loads + loads:
        copy.start()
    pl.semaphore_wait(
        barrier,
        4 + inner.astype(jnp.int32) + has_lower.astype(jnp.int32) + has_upper.astype(jnp.int32),
    )

    sent, sent_inner, sent_outer = [], [], []

    def launch(record, build):
        record.append(build)
        remote(*build()).start()

    def landed(target, send, recv):
        remote(target, target, send, recv, partner).wait_recv()

    for k in range(chunks):
        launch(sent, lambda k=k: (rad_h.at[part(k), :, other_half], gathered.at[part(k), own_depth], pre_send.at[k], pre_recv.at[k], partner))
    rings = ((has_upper, upper, 0), (has_lower, lower, 4 * children))
    for at, (exists, device, start) in enumerate(rings):
        @pl.when(exists)
        def _():
            remote(
                rad_h, near.at[pl.ds(start, 2 * children)], ring_send.at[at], ring_recv.at[at], device
            ).start()

    partner_depth = aligned(2 * depth * z + depth * (1 - x), depth)
    own_block = aligned(2 * depth * z, 2 * depth)

    def forward(k):
        halves[k].wait()
        landed(gathered.at[part(k), partner_depth], pre_send.at[k], pre_recv.at[k])
        block = gathered.at[part(k), own_block]

        @pl.when(inner)
        def _():
            launch(sent_inner, lambda k=k: (block, block, in_send.at[0, k], in_recv.at[1, k], across_inner))

        @pl.when(outer)
        def _():
            launch(sent_outer, lambda k=k: (block, block, in_send.at[0, k], in_recv.at[0, k], inner_peer))
            launch(sent_outer, lambda k=k: (block, block, in_send.at[1, k], in_recv.at[2, k], across_inner))

    for k in range(chunks):
        forward(k)

    row_at = lax.broadcasted_iota(jnp.int32, (rows, width), 0) + me * rows
    col_at = lax.broadcasted_iota(jnp.int32, (rows, width), 1)
    polar = math.pi * (row_at.astype(jnp.float32) + 0.5) / total_rows
    azimuth = 2.0 * math.pi * col_at.astype(jnp.float32) / total_cols
    sin_polar = jnp.sin(polar)
    along_x = sin_polar * jnp.cos(azimuth)
    along_y = sin_polar * jnp.sin(azimuth)
    along_z = jnp.cos(polar)
    for octant in range(4):
        first, second = 1.0 - 2.0 * (octant % 2), 1.0 - 2.0 * (octant // 2)
        argument = phase_scale * (first * along_x + second * along_y + along_z)
        cosine[octant] = jnp.cos(argument)
        sine[octant] = jnp.sin(argument)
    for copy in table_loads:
        copy.wait()
    loads[0].wait()
    loads[1].wait()
    side_rows = aligned(total_rows // 2 * side, total_rows // 2)
    phi_t[...] = phi[...].T
    theta_t[...] = theta[side_rows].T

    def phases(child):
        octant = octant_s[child]
        mirrored = octant // 4
        held = octant + mirrored * (7 - 2 * octant)
        return held, (1 - 2 * mirrored).astype(jnp.float32)

    def theta_stage(k):
        own, near_z, far_z = 2 * depth * 3 * side, 2 * depth * (2 - side), 2 * depth * 3 * (1 - side)
        for at, start in enumerate((own, near_z, far_z)):
            landed(gathered.at[part(k), aligned(start, 2 * depth)], in_send.at[0, k], in_recv.at[at, k])
        block = jnp.concatenate([gathered[k * group + j] for j in range(group)], axis=1)
        product = precise(theta[side_rows], block)
        for j in range(group):
            spread[k * group + j] = product[:, j * half : (j + 1) * half]
        rows_in[x, part(k)] = spread[part(k), aligned(2 * rows * (1 - side) + rows * x, rows)]
        launch(sent_inner, lambda k=k: (spread.at[part(k), aligned(2 * rows * (1 - side) + rows * (1 - x), rows)], rows_in.at[x, part(k)], out_send.at[0, k], out_recv.at[x, k], partner))
        for at in range(2):
            launch(sent_inner, lambda k=k, at=at: (spread.at[part(k), aligned(2 * rows * side + rows * at, rows)], rows_in.at[x, part(k)], out_send.at[1 + at, k], out_recv.at[x, k], outer_peer[at]))

    windows = parent_windows(children, parents, 2, 6)

    def shift_stage(k):
        @pl.when(inner)
        def _():
            landed(rows_in.at[1 - x, part(k)], out_send.at[0, k], out_recv.at[1 - x, k])

        @pl.when(outer)
        def _():
            for at in range(2):
                landed(rows_in.at[at, part(k)], out_send.at[0, k], out_recv.at[at, k])

        block = jnp.concatenate(
            [rows_in[at, part(k)].reshape(group * rows, half) for at in range(2)], axis=1
        )
        product = precise(block, phi[...])
        for i in range(per_chunk):
            child = k * per_chunk + i
            held, sign = phases(child)
            slot = parent_s[child] - box * parents
            for t in range(0, rows, 8):
                tile = slice(t, t + 8)
                real = product[2 * i * rows + t : 2 * i * rows + t + 8]
                imag = product[(2 * i + 1) * rows + t : (2 * i + 1) * rows + t + 8]
                cos, sin = cosine[held, tile], sign * sine[held, tile]
                moved = (cos * real - sin * imag, sin * real + cos * imag)
                for p, (low, high) in enumerate(windows):
                    if not low <= child < high:
                        continue
                    belongs = (slot == p).astype(jnp.float32)
                    for plane in range(2):
                        term = belongs * moved[plane]
                        if child == low:
                            wide[parents + p, plane, tile] = term
                        else:
                            wide[parents + p, plane, tile] += term
        for p, (low, high) in enumerate(windows):
            if k * per_chunk < high <= (k + 1) * per_chunk:
                for at, (exists, device) in enumerate(((has_upper, upper), (has_lower, lower))):
                    @pl.when(exists)
                    def _():
                        remote(
                            wide.at[parents + p], wide.at[2 * parents * at + p],
                            parent_send.at[at, p], parent_recv.at[at, p], device,
                        ).start()

    for step in range(chunks + 1):
        if step < chunks:
            pl.when(inner)(functools.partial(theta_stage, step))
        if step >= 1:
            shift_stage(step - 1)

    loads[2].wait()
    loads[4].wait()
    for at, exists in enumerate((has_lower, has_upper)):
        @pl.when(exists)
        def _():
            for p in range(parents):
                landed(wide.at[2 * parents * at + p], parent_send.at[at, p], parent_recv.at[at, p])

    tiles = rows // 8

    def translate_tile(step, carry):
        p, t = lax.div(step, tiles), lax.rem(step, tiles)
        tile = pl.ds(pl.multiple_of(t * 8, 8), 8)
        real, imag = local_ref[p, 0, tile], local_ref[p, 1, tile]
        length = parent_len_s[p]
        for column in range(parent_src_s.shape[1]):
            at = within(parent_src_s[p, column] - (box - 1) * parents, 3 * parents)
            op = parent_op_s[p, column]
            live = (column < length).astype(jnp.float32)
            op_real, op_imag = live * parent_ops[op, 0, tile], live * parent_ops[op, 1, tile]
            re, im = wide[at, 0, tile], wide[at, 1, tile]
            real = real + (op_real * re - op_imag * im)
            imag = imag + (op_real * im + op_imag * re)
        local_ref[p, 0, tile] = real
        local_ref[p, 1, tile] = imag
        return carry

    lax.fori_loop(0, parents * tiles, translate_tile, 0)

    z_local = z - 2 * side
    own_rows = aligned(2 * rows * z_local + rows * x, rows)
    partner_rows = aligned(2 * rows * z_local + rows * (1 - x), rows)

    def unshift_stage(k):
        fields_in = []
        for i in range(per_chunk):
            child = k * per_chunk + i
            held, sign = phases(child)
            slot = within(parent_s[child] - box * parents, parents)
            cos, sin = cosine[held], sign * sine[held]
            real, imag = local_ref[slot, 0], local_ref[slot, 1]
            fields_in += [cos * real + sin * imag, cos * imag - sin * real]
        product = precise(jnp.concatenate(fields_in, axis=0), phi_t[...])
        for at in range(2):
            back[at, part(k)] = product[:, at * half : (at + 1) * half].reshape(group, rows, half)
        held_rows[part(k), own_rows] = back[x, part(k)]
        launch(sent, lambda k=k: (back.at[1 - x, part(k)], held_rows.at[part(k), own_rows], back_send.at[k], back_recv.at[k], partner))

    def raise_stage(k):
        landed(held_rows.at[part(k), partner_rows], back_send.at[k], back_recv.at[k])
        launch(sent_outer, lambda k=k: (
            held_rows.at[part(k), aligned(2 * rows * side, 2 * rows)],
            held_rows.at[part(k), aligned(2 * rows * side, 2 * rows)],
            raw_send.at[k], raw_recv.at[k], inner_peer,
        ))

    def gather_stage(k):
        landed(held_rows.at[part(k), partner_rows], back_send.at[k], back_recv.at[k])
        landed(
            held_rows.at[part(k), aligned(2 * rows * side, 2 * rows)], raw_send.at[k], raw_recv.at[k]
        )
        block = jnp.concatenate([held_rows[k * group + j] for j in range(group)], axis=1)
        product = precise(theta_t[...], block)
        for j in range(group):
            partial[k * group + j] = product[:, j * half : (j + 1) * half]
        launch(sent_inner, lambda k=k: (partial.at[part(k), aligned(4 * depth * (1 - side), 4 * depth)], other.at[part(k)], swap_send.at[k], swap_recv.at[k], across_inner))

    def combine_stage(k):
        landed(other.at[part(k)], swap_send.at[k], swap_recv.at[k])
        total[part(k)] = partial[part(k), aligned(4 * depth * side, 4 * depth)] + other[part(k)]
        final[x, part(k)] = total[part(k), aligned(2 * depth * (1 - side) + depth * x, depth)]
        launch(sent_inner, lambda k=k: (total.at[part(k), aligned(2 * depth * (1 - side) + depth * (1 - x), depth)], final.at[x, part(k)], final_send.at[0, k], final_recv.at[x, k], partner))
        for at in range(2):
            launch(sent_inner, lambda k=k, at=at: (total.at[part(k), aligned(2 * depth * side + depth * at, depth)], final.at[x, part(k)], final_send.at[1 + at, k], final_recv.at[x, k], outer_peer[at]))

    def child_translate(child, carry):
        real = jnp.zeros((depth, out_ref.shape[2]), jnp.float32)
        imag = real
        length = child_len_s[child]
        for column in range(child_src_s.shape[1]):
            at = 2 * within(child_src_s[child, column] - (box - 1) * children, 3 * children)
            op = child_op_s[child, column]
            live = (column < length).astype(jnp.float32)
            op_real, op_imag = live * child_ops[op, 0], live * child_ops[op, 1]
            re, im = near[at], near[at + 1]
            real = real + (op_real * re - op_imag * im)
            imag = imag + (op_real * im + op_imag * re)
        out_ref[2 * child] = real
        out_ref[2 * child + 1] = imag
        return carry

    def finish_stage(k):
        @pl.when(inner)
        def _():
            landed(final.at[1 - x, part(k)], final_send.at[0, k], final_recv.at[1 - x, k])

        @pl.when(outer)
        def _():
            for at in range(2):
                landed(final.at[at, part(k)], final_send.at[0, k], final_recv.at[at, k])

        for at in range(2):
            columns = slice(at * half, (at + 1) * half)
            out_ref[part(k), :, columns] += final[at, part(k)]

    lag = 2
    for step in range(chunks + lag + 1):
        if step < chunks:
            unshift_stage(step)
        if 1 <= step <= chunks:
            pl.when(outer)(functools.partial(raise_stage, step - 1))
        if step == lag:
            loads[3].wait()
            loads[5].wait()
            for at, (exists, start) in enumerate(((has_lower, 0), (has_upper, 4 * children))):
                @pl.when(exists)
                def _():
                    landed(near.at[pl.ds(start, 2 * children)], ring_send.at[at], ring_recv.at[at])
            parent_rad_ref[...] = wide[parents : 2 * parents]
        if lag <= step < chunks + lag:
            first = (step - lag) * per_chunk
            lax.fori_loop(first, first + per_chunk, child_translate, 0)
            pl.when(inner)(functools.partial(gather_stage, step - lag))
        if lag + 1 <= step:
            pl.when(inner)(functools.partial(combine_stage, step - lag - 1))
    for k in range(chunks):
        finish_stage(k)

    for build in sent:
        remote(*build()).wait_send()

    @pl.when(inner)
    def _():
        for build in sent_inner:
            remote(*build()).wait_send()

    @pl.when(outer)
    def _():
        for build in sent_outer:
            remote(*build()).wait_send()

    for at, (exists, device, start) in enumerate(rings):
        @pl.when(exists)
        def _():
            remote(
                rad_h, near.at[pl.ds(start, 2 * children)], ring_send.at[at], ring_recv.at[at], device
            ).wait_send()
            for p in range(parents):
                remote(
                    wide.at[parents + p], wide.at[2 * parents * at + p],
                    parent_send.at[at, p], parent_recv.at[at, p], device,
                ).wait_send()


def deliver_body(*refs):
    sems = refs[-1]
    count = (len(refs) - 1) // 2
    copies = [
        pltpu.make_async_copy(refs[at], refs[count + at], sems.at[at]) for at in range(count)
    ]
    for copy in copies:
        copy.start()
    for copy in copies:
        copy.wait()


def deliver(*arrays):
    return pl.pallas_call(
        deliver_body,
        out_shape=tuple(jax.ShapeDtypeStruct(array.shape, array.dtype) for array in arrays),
        in_specs=[pl.BlockSpec(memory_space=pltpu.VMEM)] * len(arrays),
        out_specs=(pl.BlockSpec(memory_space=pltpu.HBM),) * len(arrays),
        scratch_shapes=[pltpu.SemaphoreType.DMA((len(arrays),))],
        compiler_params=pltpu.CompilerParams(vmem_limit_bytes=1024 * 1024),
        name="deliver",
    )(*arrays)


def fused(
    child_rad, parent_incoming, theta_interp, phi_interp, child_ops, parent_ops, *tables
):
    children, _, depth, phi_child = child_rad.shape
    parents, _, rows, width = parent_incoming.shape
    total_rows, total_depth = theta_interp.shape
    per_chunk = 2
    chunks = children // per_chunk
    half = phi_child // 2
    planes = 2 * children
    vmem = pl.BlockSpec(memory_space=pltpu.VMEM)
    hbm = pl.BlockSpec(memory_space=pltpu.HBM)

    def room(*shape):
        return pltpu.VMEM(shape, jnp.float32)

    dma = pltpu.SemaphoreType.DMA
    scratch = [
        room(total_rows, total_depth),
        room(phi_child, width),
        room(width, phi_child),
        room(total_depth, total_rows // 2),
        room(*child_ops.shape),
        room(*parent_ops.shape),
        room(3 * planes, depth, phi_child),
        room(planes, total_depth, half),
        room(planes, total_rows // 2, half),
        room(2, planes, rows, half),
        room(3 * parents, 2, rows, width),
        room(4, rows, width),
        room(4, rows, width),
        room(2, planes, rows, half),
        room(planes, total_rows // 2, half),
        room(planes, total_depth, half),
        room(planes, total_depth // 2, half),
        room(planes, total_depth // 2, half),
        room(2, planes, depth, half),
        *(pltpu.SMEM(table.shape, jnp.int32) for table in tables),
        dma((14,)),
        dma((chunks,)),
        dma((chunks,)),
        dma((chunks,)),
        dma((2, chunks)),
        dma((3, chunks)),
        dma((3, chunks)),
        dma((2, chunks)),
        dma((2,)),
        dma((2,)),
        dma((2, parents)),
        dma((2, parents)),
        dma((chunks,)),
        dma((chunks,)),
        dma((chunks,)),
        dma((chunks,)),
        dma((chunks,)),
        dma((chunks,)),
        dma((3, chunks)),
        dma((2, chunks)),
    ]
    operands = (
        *tables, child_rad.reshape(planes, depth, phi_child), parent_incoming, theta_interp,
        phi_interp, child_ops, parent_ops,
    )
    anterp, local, rad = pl.pallas_call(
        functools.partial(fused_body, lax.axis_size("box"), per_chunk),
        out_shape=(
            jax.ShapeDtypeStruct((planes, depth, phi_child), jnp.float32),
            jax.ShapeDtypeStruct(parent_incoming.shape, jnp.float32),
            jax.ShapeDtypeStruct(parent_incoming.shape, jnp.float32),
        ),
        in_specs=[hbm] * len(operands),
        out_specs=(vmem,) * 3,
        scratch_shapes=scratch,
        compiler_params=pltpu.CompilerParams(
            collective_id=0, has_side_effects=True, vmem_limit_bytes=40 * 1024 * 1024
        ),
        name="level_pass",
    )(*(pltpu.with_memory_space_constraint(operand, pltpu.HBM) for operand in operands))
    anterp, local, rad = deliver(anterp, local, rad)
    return anterp.reshape(child_rad.shape), local, rad


def per_device(
    child_rad,
    parent_incoming,
    theta_interp,
    phi_interp,
    child_ops,
    parent_ops,
    child_parent,
    child_octant,
    far_child_src,
    far_child_op,
    far_child_len,
    far_parent_src,
    far_parent_op,
    far_parent_len,
):
    child_count, _, theta_child, phi_child = child_rad.shape
    parent_count, _, theta_parent, phi_parent = parent_incoming.shape
    theta_total = theta_interp.shape[0]
    dir_count = lax.axis_size("dir")
    if dir_count == 8 and theta_child % 8 == 0 and phi_child % 256 == 0 and child_count % 2 == 0:
        return fused(
            child_rad, parent_incoming, theta_interp, phi_interp, child_ops, parent_ops, child_parent,
            child_octant, far_child_src, far_child_op, far_child_len, far_parent_src, far_parent_op,
            far_parent_len,
        )
    planes = child_count * 2 // dir_count
    padded = -(-theta_child // 8) * 8
    dir_index = lax.axis_index("dir")
    grow = ((0, 0), (0, 0), (0, padded - theta_child), (0, 0))
    spread = jnp.pad(
        theta_interp.reshape(theta_total, dir_count, theta_child),
        ((0, 0), (0, 0), (0, padded - theta_child)),
    ).reshape(theta_total, dir_count * padded)
    grown = jnp.pad(child_rad, grow)
    theta_done, before, after = exchange(
        spread, grown.reshape(dir_count, planes, padded, phi_child), True, 0
    )
    before = before.reshape(grown.shape)[:, :, :theta_child]
    after = after.reshape(grown.shape)[:, :, :theta_child]
    child_trans = translate(
        child_rad, before, after, child_ops, far_child_src, far_child_op, far_child_len, None,
        "child_translate",
    )
    theta_done = theta_done.reshape(child_count, 2, theta_parent, phi_child)
    interp = jnp.einsum("ncjf,fg->ncjg", theta_done, phi_interp, precision=lax.Precision.HIGH)
    cosine, sine = phase_block(
        jnp.arange(4, dtype=jnp.int32), dir_index * theta_parent, theta_parent, theta_total,
        0, phi_parent, phi_parent,
    )
    parent_rad = by_child(
        shift_body, child_parent, child_octant, cosine, sine, interp, parent_count, "shift"
    )
    before, after = neighbours(parent_rad)
    parent_local = translate(
        parent_rad, before, after, parent_ops, far_parent_src, far_parent_op, far_parent_len,
        parent_incoming, "parent_translate",
    )
    unshift = by_child(
        unshift_body, child_parent, child_octant, cosine, sine, parent_local, child_count, "unshift"
    )
    back_phi = jnp.einsum("ncjg,fg->ncjf", unshift, phi_interp, precision=lax.Precision.HIGH)
    anterp = exchange(
        spread, back_phi.reshape(dir_count, planes, theta_parent, phi_child), False, 1
    )
    anterp = anterp.reshape(child_count, 2, padded, phi_child)[:, :, :theta_child]
    child_local = child_trans + anterp
    return (child_local, parent_local, parent_rad)


def solution(mesh):
    in_specs = (
        P("box", None, "dir", None),
        P("box", None, "dir", None),
        P(),
        P(),
        P(None, None, "dir", None),
        P(None, None, "dir", None),
        P("box"),
        P("box"),
        P("box", None),
        P("box", None),
        P("box"),
        P("box", None),
        P("box", None),
        P("box"),
    )
    out_specs = (
        P("box", None, "dir", None),
        P("box", None, "dir", None),
        P("box", None, "dir", None),
    )
    return jax.shard_map(
        per_device, mesh=mesh, in_specs=in_specs, out_specs=out_specs, check_vma=False
    )
```

```python
import functools
import math

import jax
import jax.numpy as jnp
from jax import lax
from jax.experimental import pallas as pl
from jax.experimental.pallas import tpu as pltpu
from jax.sharding import PartitionSpec as P

phase_scale = 6.0
highest = lax.Precision.HIGHEST


def neighbours(array):
    size = lax.axis_size("box")
    up = [(i, i + 1) for i in range(size - 1)]
    down = [(i + 1, i) for i in range(size - 1)]
    return lax.ppermute(array, "box", up), lax.ppermute(array, "box", down)


def octant_signs(octant):
    first = 1.0 - 2.0 * (octant % 2).astype(jnp.float32)
    second = 1.0 - 2.0 * (octant // 2 % 2).astype(jnp.float32)
    third = 1.0 - 2.0 * (octant // 4 % 2).astype(jnp.float32)
    return (first, second, third)


def phase_block(octant, row_start, row_count, total_rows, col_start, col_count, total_cols):
    angle_rows = (row_start + jnp.arange(row_count, dtype=jnp.int32)).astype(jnp.float32)
    theta = math.pi * (angle_rows + 0.5) / total_rows
    angle_cols = (col_start + jnp.arange(col_count, dtype=jnp.int32)).astype(jnp.float32)
    azimuth = 2.0 * math.pi * angle_cols / total_cols
    sin_theta = jnp.sin(theta)[:, None]
    along_x = sin_theta * jnp.cos(azimuth)[None, :]
    along_y = sin_theta * jnp.sin(azimuth)[None, :]
    along_z = jnp.cos(theta)[:, None] + 0.0 * azimuth[None, :]
    first, second, third = octant_signs(octant)
    argument = phase_scale * (
        first[:, None, None] * along_x
        + second[:, None, None] * along_y
        + third[:, None, None] * along_z
    )
    return (jnp.cos(argument), jnp.sin(argument))


def flipped(index, mask):
    result = index
    bit = 1
    while bit <= mask:
        if mask & bit:
            result = result + bit - 2 * bit * lax.rem(lax.div(index, bit), 2)
        bit *= 2
    return result


def exchange_body(count, around, fields, matrix_ref, x_ref, *refs):
    refs = list(refs)
    out_ref = refs.pop(0)
    if around:
        below_ref, above_ref = refs.pop(0), refs.pop(0)
    got, ready, landed, send_sem, recv_sem = refs[:5]
    me = lax.axis_index("dir")
    planes, depth, width = got.shape[1:]
    rows = ready.shape[2]
    mesh_ids = pl.DeviceIdType.MESH
    barrier = pltpu.get_barrier_semaphore()
    steps = range(count - 1, 0, -1)

    def partner(step):
        if count & (count - 1):
            return lax.rem(me + step, count), lax.rem(me + count - step, count)
        peer = flipped(me, step)
        return peer, peer

    for step in steps:
        pl.semaphore_signal(
            barrier, inc=1, device_id={"dir": partner(step)[0]}, device_id_type=mesh_ids
        )
    greeted = count - 1
    if around:
        box = lax.axis_index("box")
        upper = lax.rem(box + 1, fields)
        lower = lax.rem(box + fields - 1, fields)
        for other in (upper, lower):
            pl.semaphore_signal(
                barrier, inc=1, device_id={"box": other}, device_id_type=mesh_ids
            )
        greeted += 2
    pl.semaphore_wait(barrier, greeted)

    def push(source, target, leg, plane):
        for step in steps:
            peer, _ = partner(step)
            copy = pltpu.make_async_remote_copy(
                src_ref=source.at[peer, plane],
                dst_ref=target.at[me, plane],
                send_sem=send_sem.at[leg, plane, step],
                recv_sem=recv_sem.at[leg, plane, step],
                device_id={"dir": peer},
                device_id_type=mesh_ids,
            )
            copy.start()
            started.append(copy)

    def settle(target, leg, plane):
        for step in steps:
            _, origin = partner(step)
            pltpu.make_async_remote_copy(
                src_ref=target.at[origin, plane],
                dst_ref=target.at[origin, plane],
                send_sem=send_sem.at[leg, plane, step],
                recv_sem=recv_sem.at[leg, plane, step],
                device_id={"dir": origin},
                device_id_type=mesh_ids,
            ).wait_recv()

    started = []
    for plane in range(planes):
        push(x_ref, got, 0, plane)
    got[me] = x_ref[me]
    for plane in range(planes):
        settle(got, 0, plane)
        product = lax.dot_general(
            matrix_ref[...],
            got[:, plane].reshape(count * depth, width),
            (((1 if around else 0,), (0,)), ((), ())),
            precision=lax.Precision.HIGH,
            preferred_element_type=jnp.float32,
        )
        ready[:, plane] = product.reshape(count, rows, width)
        push(ready, landed, 1, plane)
    ring = []
    if around:
        box_send, box_recv = refs[5:7]
        for at, (other, target) in enumerate(((upper, below_ref), (lower, above_ref))):
            copy = pltpu.make_async_remote_copy(
                src_ref=x_ref,
                dst_ref=target,
                send_sem=box_send.at[at],
                recv_sem=box_recv.at[at],
                device_id={"box": other},
                device_id_type=mesh_ids,
            )
            copy.start()
            ring.append(copy)
    landed[me] = ready[me]
    for plane in range(planes):
        settle(landed, 1, plane)
    out_ref[...] = landed[...].reshape(out_ref.shape)
    for copy in started:
        copy.wait_send()
    for copy in ring:
        copy.wait()


def exchange(matrix, x, around, which):
    count, planes, depth, width = x.shape
    rows = matrix.shape[0 if around else 1] // count
    operands = (matrix, x)
    vmem = pl.BlockSpec(memory_space=pltpu.VMEM)
    result = jax.ShapeDtypeStruct((count * planes, rows, width), jnp.float32)
    ring = jax.ShapeDtypeStruct(x.shape, jnp.float32)
    scratch = [
        pltpu.VMEM((count, planes, depth, width), jnp.float32),
        pltpu.VMEM((count, planes, rows, width), jnp.float32),
        pltpu.VMEM((count, planes, rows, width), jnp.float32),
        pltpu.SemaphoreType.DMA((2, planes, count)),
        pltpu.SemaphoreType.DMA((2, planes, count)),
    ]
    if around:
        scratch += [pltpu.SemaphoreType.DMA((2,)), pltpu.SemaphoreType.DMA((2,))]
    return pl.pallas_call(
        functools.partial(exchange_body, count, around, lax.axis_size("box")),
        out_shape=(result, ring, ring) if around else result,
        in_specs=[vmem] * len(operands),
        out_specs=(vmem,) * 3 if around else vmem,
        scratch_shapes=scratch,
        compiler_params=pltpu.CompilerParams(
            collective_id=which, has_side_effects=True, vmem_limit_bytes=16 * 1024 * 1024
        ),
        name="exchange_" + str(which),
    )(*operands)


def translate_body(has_base, *refs):
    source_ref, which_ref, length_ref, before, own, after, ops_ref = refs[:7]
    base_ref = refs[7] if has_base else None
    out_ref, wide, sems = refs[-3:]
    boxes, _, rows, width = own.shape
    copies = [
        pltpu.make_async_copy(part, wide.at[pl.ds(at * boxes, boxes)], sems.at[at])
        for at, part in enumerate((before, own, after))
    ]
    for copy in copies:
        copy.start()
    for copy in copies:
        copy.wait()
    offset = (lax.axis_index("box") - 1) * boxes
    tall = rows
    while tall % 16 == 0 and tall * width > 4096:
        tall //= 2

    def one_box(box, carry):
        length = length_ref[box]
        for start in range(0, rows, tall):
            part = slice(start, start + tall)

            def entry(column, totals):
                real, imag = totals
                at = source_ref[box, column] - offset
                op = which_ref[box, column]
                op_real, op_imag = ops_ref[op, 0, part], ops_ref[op, 1, part]
                re, im = wide[at, 0, part], wide[at, 1, part]
                real = real + (op_real * re - op_imag * im)
                imag = imag + (op_real * im + op_imag * re)
                return real, imag

            if has_base:
                initial = (base_ref[box, 0, part], base_ref[box, 1, part])
            else:
                initial = (jnp.zeros((tall, width), jnp.float32),) * 2
            real, imag = lax.fori_loop(0, length, entry, initial)
            out_ref[box, 0, part] = real
            out_ref[box, 1, part] = imag
        return carry

    lax.fori_loop(0, boxes, one_box, 0)


def translate(own, before, after, operators, source, which_op, length, base, name):
    boxes = own.shape[0]
    vmem = pl.BlockSpec(memory_space=pltpu.VMEM)
    smem = pl.BlockSpec(memory_space=pltpu.SMEM)
    anywhere = pl.BlockSpec(memory_space=pltpu.HBM)
    operands = [source, which_op, length, before, own, after, operators]
    specs = [smem] * 3 + [anywhere] * 3 + [vmem]
    if base is not None:
        operands.append(base)
        specs.append(vmem)
    return pl.pallas_call(
        functools.partial(translate_body, base is not None),
        out_shape=jax.ShapeDtypeStruct(own.shape, jnp.float32),
        in_specs=specs,
        out_specs=vmem,
        scratch_shapes=[
            pltpu.VMEM((3 * boxes,) + own.shape[1:], jnp.float32),
            pltpu.SemaphoreType.DMA((3,)),
        ],
        compiler_params=pltpu.CompilerParams(vmem_limit_bytes=20 * 1024 * 1024),
        name=name,
    )(*operands)


def shift_body(parent_ref, octant_ref, cosine_ref, sine_ref, interp_ref, out_ref):
    children = interp_ref.shape[0]
    offset = lax.axis_index("box") * out_ref.shape[0]
    out_ref[...] = jnp.zeros_like(out_ref)

    def one_child(child, carry):
        slot, octant = parent_ref[child] - offset, octant_ref[child]
        mirrored = octant // 4
        held = octant + mirrored * (7 - 2 * octant)
        sign = (1 - 2 * mirrored).astype(jnp.float32)
        cosine, sine = cosine_ref[held], sign * sine_ref[held]
        real, imag = interp_ref[child, 0], interp_ref[child, 1]
        out_ref[slot, 0] += cosine * real - sine * imag
        out_ref[slot, 1] += sine * real + cosine * imag
        return carry

    lax.fori_loop(0, children, one_child, 0)


def unshift_body(parent_ref, octant_ref, cosine_ref, sine_ref, field_ref, out_ref):
    children = out_ref.shape[0]
    offset = lax.axis_index("box") * field_ref.shape[0]

    def one_child(child, carry):
        slot, octant = parent_ref[child] - offset, octant_ref[child]
        mirrored = octant // 4
        held = octant + mirrored * (7 - 2 * octant)
        sign = (1 - 2 * mirrored).astype(jnp.float32)
        cosine, sine = cosine_ref[held], sign * sine_ref[held]
        real, imag = field_ref[slot, 0], field_ref[slot, 1]
        out_ref[child, 0] = cosine * real + sine * imag
        out_ref[child, 1] = cosine * imag - sine * real
        return carry

    lax.fori_loop(0, children, one_child, 0)


def by_child(body, parent, octant, cosine, sine, values, boxes, name):
    vmem = pl.BlockSpec(memory_space=pltpu.VMEM)
    smem = pl.BlockSpec(memory_space=pltpu.SMEM)
    return pl.pallas_call(
        body,
        out_shape=jax.ShapeDtypeStruct((boxes,) + values.shape[1:], jnp.float32),
        in_specs=[smem] * 2 + [vmem] * 3,
        out_specs=vmem,
        compiler_params=pltpu.CompilerParams(vmem_limit_bytes=16 * 1024 * 1024),
        name=name,
    )(parent, octant, cosine, sine, values)


def within(index, size):
    return jnp.minimum(jnp.maximum(index, 0), size - 1)


def precise(lhs, rhs):
    return lax.dot_general(
        lhs,
        rhs,
        (((1,), (0,)), ((), ())),
        precision=lax.Precision.HIGH,
        preferred_element_type=jnp.float32,
    )


def parent_windows(children, parents, least, most):
    windows = []
    for p in range(parents):
        low = max(least * p, children - most * (parents - p))
        high = min(most * (p + 1), children - least * (parents - 1 - p))
        windows.append((low, high))
    return windows


def fused_body(fields, sizes, *refs):
    tables_h = refs[:8]
    rad_h, incoming_h, theta_h, phi_h, child_ops_h, parent_ops_h = refs[8:14]
    out_ref, local_ref, parent_rad_ref = refs[14:17]
    (theta, phi, phi_t, theta_t, child_ops, parent_ops, near, gathered, spread, rows_in, wide,
     cosine, sine, back, held_rows, partial, other, total, final) = refs[17:36]
    tables = refs[36:44]
    parent_s, octant_s, child_src_s, child_op_s, child_len_s = tables[:5]
    parent_src_s, parent_op_s, parent_len_s = tables[5:]
    (load_sem, pre_send, pre_recv, in_send, in_recv, out_send, out_recv, ring_send,
     ring_recv, parent_send, parent_recv, back_send, back_recv, raw_send, raw_recv, swap_send,
     swap_recv, final_send, final_recv) = refs[44:]
    mesh_ids = pl.DeviceIdType.MESH
    me, box = lax.axis_index("dir"), lax.axis_index("box")
    children = parent_s.shape[0]
    parents, _, rows, width = local_ref.shape
    depth = rad_h.shape[1]
    half = gathered.shape[2]
    chunks, direct, early = len(sizes), 2, 2
    starts = [sum(sizes[:k]) for k in range(chunks)]
    total_rows, total_cols = theta_h.shape[0], width
    z, x = lax.div(me, 2), lax.rem(me, 2)
    side = lax.div(z, 2)
    inner = z == 1 + side
    outer = z != 1 + side

    def at_place(place):
        return {"box": box, "dir": place}

    partner = at_place(2 * z + 1 - x)
    outer_peer = [at_place(6 * side + at) for at in range(2)]
    inner_peers = [at_place(2 * (1 + side) + at) for at in range(2)]
    inner_peer = at_place(2 * (1 + side) + x)
    across_inner = at_place(2 * (2 - side) + x)
    across_inners = [at_place(2 * (2 - side) + at) for at in range(2)]
    across_outers = [at_place(6 * (1 - side) + at) for at in range(2)]
    inner_diagonal = at_place(2 * (1 + side) + 1 - x)
    across_diagonal = at_place(2 * (2 - side) + 1 - x)
    has_lower, has_upper = box > 0, box < fields - 1
    lower, upper = {"box": box - 1, "dir": me}, {"box": box + 1, "dir": me}

    def remote(source, target, send, recv, device):
        return pltpu.make_async_remote_copy(
            src_ref=source, dst_ref=target, send_sem=send, recv_sem=recv,
            device_id=device, device_id_type=mesh_ids,
        )

    def aligned(value, step):
        return pl.ds(pl.multiple_of(value, step), step)

    def part(k):
        return pl.ds(2 * starts[k], 2 * sizes[k])

    own_near = pl.ds(2 * children, 2 * children)
    loads = [
        (rad_h, near.at[own_near]), (theta_h, theta), (phi_h, phi), (incoming_h, local_ref),
        (child_ops_h, child_ops), (parent_ops_h, parent_ops),
    ]
    near_load, theta_load, phi_load, incoming_load, child_load, parent_load = (
        pltpu.make_async_copy(source, target, load_sem.at[at])
        for at, (source, target) in enumerate(loads)
    )
    table_loads = [
        pltpu.make_async_copy(source, target, load_sem.at[6 + at])
        for at, (source, target) in enumerate(zip(tables_h, tables))
    ]
    own_half = pl.ds(pl.multiple_of(x * half, half), half)
    other_half = pl.ds(pl.multiple_of((1 - x) * half, half), half)
    own_depth = aligned(2 * depth * z + depth * x, depth)
    def fill_phases():
        row_at = lax.broadcasted_iota(jnp.int32, (rows, width), 0) + me * rows
        col_at = lax.broadcasted_iota(jnp.int32, (rows, width), 1)
        polar = math.pi * (row_at.astype(jnp.float32) + 0.5) / total_rows
        azimuth = 2.0 * math.pi * col_at.astype(jnp.float32) / total_cols
        sin_polar = jnp.sin(polar)
        along_x = sin_polar * jnp.cos(azimuth)
        along_y = sin_polar * jnp.sin(azimuth)
        along_z = jnp.cos(polar)
        for octant in range(4):
            first, second = 1.0 - 2.0 * (octant % 2), 1.0 - 2.0 * (octant // 2)
            argument = phase_scale * (first * along_x + second * along_y + along_z)
            cosine[octant] = jnp.cos(argument)
            sine[octant] = jnp.sin(argument)

    def greet(device):
        pl.semaphore_signal(barrier, inc=1, device_id=device, device_id_type=mesh_ids)

    barrier = pltpu.get_barrier_semaphore()
    greet(partner)

    @pl.when(inner)
    def _():
        for device in outer_peer + across_inners + across_outers:
            greet(device)

    @pl.when(outer)
    def _():
        for device in inner_peers + across_inners:
            greet(device)

    pl.when(has_lower)(lambda: greet(lower))
    pl.when(has_upper)(lambda: greet(upper))
    for copy in (near_load, *table_loads, theta_load, phi_load):
        copy.start()
    fill_phases()
    near_load.wait()
    pl.semaphore_wait(
        barrier,
        5 + 2 * inner.astype(jnp.int32) + has_lower.astype(jnp.int32) + has_upper.astype(jnp.int32),
    )

    def landed(target, send, recv):
        remote(target, target, send, recv, partner).wait_recv()

    def each(first, count, body):
        for k in range(first, count):
            body(k)

    partner_depth = aligned(2 * depth * z + depth * (1 - x), depth)

    def mine(k, columns):
        return near.at[pl.ds(2 * (children + starts[k]), 2 * sizes[k]), :, columns]

    def trade(k):
        return remote(
            mine(k, other_half), gathered.at[part(k), own_depth], pre_send.at[0], pre_recv.at[k],
            partner,
        )

    def supply(k, relayed, devices):
        target = gathered.at[part(k), own_depth]
        source, device = mine(k, own_half), devices[0]
        if relayed and k < direct:
            source, device = mine(k, other_half), devices[1]
        elif relayed:
            source = target = gathered.at[part(k), partner_depth]
        return remote(source, target, in_send.at[0], in_recv.at[k], device)

    def inner_supply(k, relayed):
        return [supply(k, relayed, (across_inner, across_diagonal))]

    def outer_supply(k, relayed):
        return [
            supply(k, relayed, (inner_peer, inner_diagonal)),
            supply(k, relayed, (across_inner, across_diagonal)),
        ]

    def start(copies):
        for copy in copies:
            copy.start()

    def traded(k):
        landed(gathered.at[part(k), partner_depth], pre_send.at[0], pre_recv.at[k])

    def advance(k, copies):
        traded(k)
        start(copies(k, 1))
        if k + early < chunks:
            trade(k + early).start()
            start(copies(k + early, 0))

    def open_supply(copies):
        for k in range(direct):
            start(copies(k, 0))
            start(copies(k, 1))
        for k in range(direct, direct + early):
            start(copies(k, 0))

    pl.when(inner)(lambda: start([trade(k) for k in range(direct)]))
    start([trade(k) for k in range(direct, direct + early)])
    pl.when(inner)(lambda: open_supply(inner_supply))
    pl.when(outer)(lambda: open_supply(outer_supply))
    rings = ((has_upper, upper, 0), (has_lower, lower, 4 * children))

    def ring_copy(at):
        exists, device, begin = rings[at]
        return remote(
            near.at[own_near], near.at[pl.ds(begin, 2 * children)], ring_send.at[at],
            ring_recv.at[at], device,
        )

    for at in range(2):
        pl.when(rings[at][0])(lambda: ring_copy(at).start())
    pl.when(outer)(lambda: each(direct, chunks, lambda k: advance(k, outer_supply)))
    for copy in (incoming_load, child_load, parent_load):
        copy.start()
    for copy in table_loads:
        copy.wait()
    theta_load.wait()
    phi_load.wait()
    side_rows = aligned(total_rows // 2 * side, total_rows // 2)
    phi_t[...] = phi[...].T
    theta_t[...] = theta[side_rows].T

    def phases(child):
        octant = octant_s[child]
        mirrored = lax.shift_right_logical(octant, 2)
        held = octant + mirrored * (7 - 2 * octant)
        return held, (1 - 2 * mirrored).astype(jnp.float32)

    def out_copy(k, at):
        if at == 0:
            begin, device = 2 * rows * (1 - side) + rows * (1 - x), partner
        else:
            begin, device = 2 * rows * side + rows * (at - 1), outer_peer[at - 1]
        return remote(
            spread.at[part(k), aligned(begin, rows)], rows_in.at[x, part(k)], out_send.at[0],
            out_recv.at[k], device,
        )

    def theta_stage(k):
        if k < direct:
            traded(k)
        if direct <= k + early < chunks:
            advance(k + early, inner_supply)
        gathered[part(k), own_depth] = near[
            pl.ds(2 * (children + starts[k]), 2 * sizes[k]), :, own_half
        ]
        landed(gathered.at[part(k), pl.ds(0, 6 * depth)], in_send.at[0], in_recv.at[k])
        planes = range(2 * starts[k], 2 * (starts[k] + sizes[k]))
        block = jnp.concatenate([gathered[j] for j in planes], axis=1)
        product = precise(theta[side_rows], block)
        for at, j in enumerate(planes):
            spread[j] = product[:, at * half : (at + 1) * half]
        for at in (1, 2, 0):
            out_copy(k, at).start()
        rows_in[x, part(k)] = spread[
            part(k), aligned(2 * rows * (1 - side) + rows * x, rows)
        ]

    windows = parent_windows(children, parents, 2, 6)

    def parent_copy(at, p):
        return remote(
            wide.at[parents + p], wide.at[2 * parents * at + p], parent_send.at[at, p],
            parent_recv.at[at, p], (upper, lower)[at],
        )

    def shift_stage(k):
        pl.when(inner)(
            lambda: landed(rows_in.at[1 - x, part(k)], out_send.at[0], out_recv.at[k])
        )
        pl.when(outer)(lambda: landed(rows_in.at[:, part(k)], out_send.at[0], out_recv.at[k]))
        block = jnp.concatenate(
            [rows_in[at, part(k)].reshape(2 * sizes[k] * rows, half) for at in range(2)], axis=1
        )
        product = precise(block, phi[...])
        members = range(starts[k], starts[k] + sizes[k])
        angles = [phases(child) for child in members]
        slots = [parent_s[child] - box * parents for child in members]
        belongs = [[(slot == p).astype(jnp.float32) for slot in slots] for p in range(parents)]
        for t in range(0, rows, 8):
            tile = slice(t, t + 8)
            moved = []
            for i, (held, sign) in enumerate(angles):
                real = product[2 * i * rows + t : 2 * i * rows + t + 8]
                imag = product[(2 * i + 1) * rows + t : (2 * i + 1) * rows + t + 8]
                cos, sin = cosine[held, tile], sign * sine[held, tile]
                moved.append((cos * real - sin * imag, sin * real + cos * imag))
            for p, (low, high) in enumerate(windows):
                for plane in range(2):
                    terms = [
                        belongs[p][i] * moved[i][plane]
                        for i, child in enumerate(members) if low <= child < high
                    ]
                    if not terms:
                        continue
                    if low not in members:
                        terms.insert(0, wide[parents + p, plane, tile])
                    wide[parents + p, plane, tile] = functools.reduce(jnp.add, terms)
        for p, (low, high) in enumerate(windows):
            if high - 1 in members:
                for at in range(2):
                    pl.when(rings[at][0])(lambda: parent_copy(at, p).start())

    shift_lag = 1

    def up_step(step):
        if step < chunks:
            pl.when(inner)(lambda: theta_stage(step))
        if step >= shift_lag:
            shift_stage(step - shift_lag)

    each(0, chunks + shift_lag, up_step)

    incoming_load.wait()
    parent_load.wait()
    for at, exists in enumerate((has_lower, has_upper)):
        @pl.when(exists)
        def _():
            for p in range(parents):
                landed(wide.at[2 * parents * at + p], parent_send.at[at, p], parent_recv.at[at, p])

    def translate_parent(p):
        length = parent_len_s[p]
        entries = []
        for column in range(parent_src_s.shape[1]):
            at = within(parent_src_s[p, column] - (box - 1) * parents, 3 * parents)
            entries.append((at, parent_op_s[p, column], (column < length).astype(jnp.float32)))
        for t in range(0, rows, 8):
            tile = slice(t, t + 8)
            real, imag = local_ref[p, 0, tile], local_ref[p, 1, tile]
            for at, op, live in entries:
                op_real, op_imag = live * parent_ops[op, 0, tile], live * parent_ops[op, 1, tile]
                re, im = wide[at, 0, tile], wide[at, 1, tile]
                real = real + (op_real * re - op_imag * im)
                imag = imag + (op_real * im + op_imag * re)
            local_ref[p, 0, tile] = real
            local_ref[p, 1, tile] = imag

    def translate_step(p, carry):
        translate_parent(p)
        return carry

    lax.fori_loop(0, parents, translate_step, 0)

    z_local = z - 2 * side
    own_rows = aligned(2 * rows * z_local + rows * x, rows)
    partner_rows = aligned(2 * rows * z_local + rows * (1 - x), rows)

    def back_copy(k):
        return remote(
            back.at[1 - x, part(k)], held_rows.at[part(k), own_rows], back_send.at[0],
            back_recv.at[k], partner,
        )

    def raw_copy(k, relayed):
        source, target, device = back.at[x, part(k)], held_rows.at[part(k), own_rows], inner_peer
        if relayed and k < direct:
            source, device = back.at[1 - x, part(k)], inner_diagonal
        elif relayed:
            source = target = held_rows.at[part(k), partner_rows]
        return remote(source, target, raw_send.at[0], raw_recv.at[k], device)

    def unshift_stage(k):
        fields_in = []
        for child in range(starts[k], starts[k] + sizes[k]):
            held, sign = phases(child)
            slot = within(parent_s[child] - box * parents, parents)
            cos, sin = cosine[held], sign * sine[held]
            real, imag = local_ref[slot, 0], local_ref[slot, 1]
            fields_in += [cos * real + sin * imag, cos * imag - sin * real]
        product = precise(jnp.concatenate(fields_in, axis=0), phi_t[...])
        for at in range(2):
            back[at, part(k)] = product[:, at * half : (at + 1) * half].reshape(
                2 * sizes[k], rows, half
            )
        if k >= direct:
            back_copy(k).start()

        @pl.when(inner)
        def _():
            if k < direct:
                back_copy(k).start()
            held_rows[part(k), own_rows] = back[x, part(k)]

        @pl.when(outer)
        def _():
            raw_copy(k, 0).start()
            if k < direct:
                raw_copy(k, 1).start()

    def raise_stage(k):
        if k >= direct:
            landed(held_rows.at[part(k), partner_rows], back_send.at[0], back_recv.at[k])
            raw_copy(k, 1).start()

    def swap_copy(k):
        return remote(
            partial.at[part(k), aligned(4 * depth * (1 - side), 4 * depth)], other.at[part(k)],
            swap_send.at[0], swap_recv.at[k], across_inner,
        )

    def gather_stage(k):
        landed(held_rows.at[part(k), partner_rows], back_send.at[0], back_recv.at[k])
        landed(
            held_rows.at[part(k), aligned(2 * rows * side, 2 * rows)], raw_send.at[0],
            raw_recv.at[k],
        )
        planes = range(2 * starts[k], 2 * (starts[k] + sizes[k]))
        block = jnp.concatenate([held_rows[j] for j in planes], axis=1)
        product = precise(theta_t[...], block)
        for at, j in enumerate(planes):
            partial[j] = product[:, at * half : (at + 1) * half]
        swap_copy(k).start()

    def final_copy(k, at):
        if at == 0:
            begin, device = 2 * depth * (1 - side) + depth * (1 - x), partner
        else:
            begin, device = 2 * depth * side + depth * (at - 1), outer_peer[at - 1]
        return remote(
            total.at[part(k), aligned(begin, depth)], final.at[x, part(k)], final_send.at[0],
            final_recv.at[k], device,
        )

    def combine_stage(k):
        landed(other.at[part(k)], swap_send.at[0], swap_recv.at[k])
        total[part(k)] = partial[part(k), aligned(4 * depth * side, 4 * depth)] + other[part(k)]
        for at in (1, 2, 0):
            final_copy(k, at).start()
        final[x, part(k)] = total[
            part(k), aligned(2 * depth * (1 - side) + depth * x, depth)
        ]

    def child_translate(child, carry):
        real = jnp.zeros((depth, out_ref.shape[2]), jnp.float32)
        imag = real
        length = child_len_s[child]
        for column in range(child_src_s.shape[1]):
            at = 2 * within(child_src_s[child, column] - (box - 1) * children, 3 * children)
            op = child_op_s[child, column]
            live = (column < length).astype(jnp.float32)
            op_real, op_imag = live * child_ops[op, 0], live * child_ops[op, 1]
            re, im = near[at], near[at + 1]
            real = real + (op_real * re - op_imag * im)
            imag = imag + (op_real * im + op_imag * re)
        out_ref[2 * child] = real
        out_ref[2 * child + 1] = imag
        return carry

    def finish_stage(k):
        pl.when(inner)(
            lambda: landed(final.at[1 - x, part(k)], final_send.at[0], final_recv.at[k])
        )
        pl.when(outer)(lambda: landed(final.at[:, part(k)], final_send.at[0], final_recv.at[k]))
        for at in range(2):
            columns = slice(at * half, (at + 1) * half)
            out_ref[part(k), :, columns] += final[at, part(k)]

    child_load.wait()
    for at, (exists, start) in enumerate(((has_lower, 0), (has_upper, 4 * children))):
        @pl.when(exists)
        def _():
            landed(near.at[pl.ds(start, 2 * children)], ring_send.at[at], ring_recv.at[at])

    lag, wait_lag, end_lag = 3, 2, 2

    def down_step(step):
        if step < chunks:
            unshift_stage(step)
        if 1 <= step <= chunks:
            pl.when(outer)(lambda: raise_stage(step - 1))
        if lag <= step < chunks + lag:
            pl.when(inner)(lambda: gather_stage(step - lag))
            first = starts[step - lag]
            lax.fori_loop(first, first + sizes[step - lag], child_translate, 0)
        if step >= lag + wait_lag:
            pl.when(inner)(lambda: combine_stage(step - lag - wait_lag))
        if step >= lag + wait_lag + end_lag:
            finish_stage(step - lag - wait_lag - end_lag)

    each(0, chunks + lag + wait_lag, down_step)
    parent_rad_ref[...] = wide[parents : 2 * parents]
    each(chunks - end_lag, chunks, finish_stage)

    def settled(target, send):
        remote(target, target, send, final_recv.at[0], partner).wait_send()

    everything = pl.ds(0, 2 * children)
    later = pl.ds(2 * starts[direct], 2 * (children - starts[direct]))

    def settle_inner():
        settled(gathered.at[everything, pl.ds(0, depth)], pre_send.at[0])
        settled(gathered.at[everything, pl.ds(0, 2 * depth)], in_send.at[0])
        settled(spread.at[everything, pl.ds(0, 3 * rows)], out_send.at[0])
        settled(held_rows.at[everything, pl.ds(0, rows)], back_send.at[0])
        settled(partial.at[everything, pl.ds(0, 4 * depth)], swap_send.at[0])
        settled(total.at[everything, pl.ds(0, 3 * depth)], final_send.at[0])

    def settle_outer():
        settled(gathered.at[later, pl.ds(0, depth)], pre_send.at[0])
        settled(gathered.at[everything, pl.ds(0, 4 * depth)], in_send.at[0])
        settled(held_rows.at[later, pl.ds(0, rows)], back_send.at[0])
        settled(held_rows.at[everything, pl.ds(0, 2 * rows)], raw_send.at[0])

    pl.when(inner)(settle_inner)
    pl.when(outer)(settle_outer)
    for at, (exists, device, start) in enumerate(rings):
        @pl.when(exists)
        def _():
            ring_copy(at).wait_send()
            for p in range(parents):
                parent_copy(at, p).wait_send()


def deliver_body(*refs):
    sems = refs[-1]
    count = (len(refs) - 1) // 2
    copies = [
        pltpu.make_async_copy(refs[at], refs[count + at], sems.at[at]) for at in range(count)
    ]
    for copy in copies:
        copy.start()
    for copy in copies:
        copy.wait()


def deliver(*arrays):
    return pl.pallas_call(
        deliver_body,
        out_shape=tuple(jax.ShapeDtypeStruct(array.shape, array.dtype) for array in arrays),
        in_specs=[pl.BlockSpec(memory_space=pltpu.VMEM)] * len(arrays),
        out_specs=(pl.BlockSpec(memory_space=pltpu.HBM),) * len(arrays),
        scratch_shapes=[pltpu.SemaphoreType.DMA((len(arrays),))],
        compiler_params=pltpu.CompilerParams(vmem_limit_bytes=1024 * 1024),
        name="deliver",
    )(*arrays)


def fused(
    child_rad, parent_incoming, theta_interp, phi_interp, child_ops, parent_ops, *tables
):
    children, _, depth, phi_child = child_rad.shape
    parents, _, rows, width = parent_incoming.shape
    total_rows, total_depth = theta_interp.shape
    sizes = (2,) * (children // 2)
    chunks = len(sizes)
    half = phi_child // 2
    planes = 2 * children
    vmem = pl.BlockSpec(memory_space=pltpu.VMEM)
    hbm = pl.BlockSpec(memory_space=pltpu.HBM)

    def room(*shape):
        return pltpu.VMEM(shape, jnp.float32)

    dma = pltpu.SemaphoreType.DMA
    scratch = [
        room(total_rows, total_depth),
        room(phi_child, width),
        room(width, phi_child),
        room(total_depth, total_rows // 2),
        room(*child_ops.shape),
        room(*parent_ops.shape),
        room(3 * planes, depth, phi_child),
        room(planes, total_depth, half),
        room(planes, total_rows // 2, half),
        room(2, planes, rows, half),
        room(3 * parents, 2, rows, width),
        room(4, rows, width),
        room(4, rows, width),
        room(2, planes, rows, half),
        room(planes, total_rows // 2, half),
        room(planes, total_depth, half),
        room(planes, total_depth // 2, half),
        room(planes, total_depth // 2, half),
        room(2, planes, depth, half),
        *(pltpu.SMEM(table.shape, jnp.int32) for table in tables),
        dma((14,)),
        dma((1,)),
        dma((chunks,)),
        dma((1,)),
        dma((chunks,)),
        dma((1,)),
        dma((chunks,)),
        dma((2,)),
        dma((2,)),
        dma((2, parents)),
        dma((2, parents)),
        dma((1,)),
        dma((chunks,)),
        dma((1,)),
        dma((chunks,)),
        dma((1,)),
        dma((chunks,)),
        dma((1,)),
        dma((chunks,)),
    ]
    operands = (
        *tables, child_rad.reshape(planes, depth, phi_child), parent_incoming, theta_interp,
        phi_interp, child_ops, parent_ops,
    )
    anterp, local, rad = pl.pallas_call(
        functools.partial(fused_body, lax.axis_size("box"), sizes),
        out_shape=(
            jax.ShapeDtypeStruct((planes, depth, phi_child), jnp.float32),
            jax.ShapeDtypeStruct(parent_incoming.shape, jnp.float32),
            jax.ShapeDtypeStruct(parent_incoming.shape, jnp.float32),
        ),
        in_specs=[hbm] * len(operands),
        out_specs=(vmem,) * 3,
        scratch_shapes=scratch,
        compiler_params=pltpu.CompilerParams(
            collective_id=0, has_side_effects=True, vmem_limit_bytes=40 * 1024 * 1024
        ),
        name="level_pass",
    )(*(pltpu.with_memory_space_constraint(operand, pltpu.HBM) for operand in operands))
    anterp, local, rad = deliver(anterp, local, rad)
    return anterp.reshape(child_rad.shape), local, rad


def per_device(
    child_rad,
    parent_incoming,
    theta_interp,
    phi_interp,
    child_ops,
    parent_ops,
    child_parent,
    child_octant,
    far_child_src,
    far_child_op,
    far_child_len,
    far_parent_src,
    far_parent_op,
    far_parent_len,
):
    child_count, _, theta_child, phi_child = child_rad.shape
    parent_count, _, theta_parent, phi_parent = parent_incoming.shape
    theta_total = theta_interp.shape[0]
    dir_count = lax.axis_size("dir")
    if dir_count == 8 and theta_child % 8 == 0 and phi_child % 256 == 0 and child_count % 2 == 0 and child_count >= 8:
        return fused(
            child_rad, parent_incoming, theta_interp, phi_interp, child_ops, parent_ops, child_parent,
            child_octant, far_child_src, far_child_op, far_child_len, far_parent_src, far_parent_op,
            far_parent_len,
        )
    planes = child_count * 2 // dir_count
    padded = -(-theta_child // 8) * 8
    dir_index = lax.axis_index("dir")
    grow = ((0, 0), (0, 0), (0, padded - theta_child), (0, 0))
    spread = jnp.pad(
        theta_interp.reshape(theta_total, dir_count, theta_child),
        ((0, 0), (0, 0), (0, padded - theta_child)),
    ).reshape(theta_total, dir_count * padded)
    grown = jnp.pad(child_rad, grow)
    theta_done, before, after = exchange(
        spread, grown.reshape(dir_count, planes, padded, phi_child), True, 0
    )
    before = before.reshape(grown.shape)[:, :, :theta_child]
    after = after.reshape(grown.shape)[:, :, :theta_child]
    child_trans = translate(
        child_rad, before, after, child_ops, far_child_src, far_child_op, far_child_len, None,
        "child_translate",
    )
    theta_done = theta_done.reshape(child_count, 2, theta_parent, phi_child)
    interp = jnp.einsum("ncjf,fg->ncjg", theta_done, phi_interp, precision=lax.Precision.HIGH)
    cosine, sine = phase_block(
        jnp.arange(4, dtype=jnp.int32), dir_index * theta_parent, theta_parent, theta_total,
        0, phi_parent, phi_parent,
    )
    parent_rad = by_child(
        shift_body, child_parent, child_octant, cosine, sine, interp, parent_count, "shift"
    )
    before, after = neighbours(parent_rad)
    parent_local = translate(
        parent_rad, before, after, parent_ops, far_parent_src, far_parent_op, far_parent_len,
        parent_incoming, "parent_translate",
    )
    unshift = by_child(
        unshift_body, child_parent, child_octant, cosine, sine, parent_local, child_count, "unshift"
    )
    back_phi = jnp.einsum("ncjg,fg->ncjf", unshift, phi_interp, precision=lax.Precision.HIGH)
    anterp = exchange(
        spread, back_phi.reshape(dir_count, planes, theta_parent, phi_child), False, 1
    )
    anterp = anterp.reshape(child_count, 2, padded, phi_child)[:, :, :theta_child]
    child_local = child_trans + anterp
    return (child_local, parent_local, parent_rad)


def solution(mesh):
    in_specs = (
        P("box", None, "dir", None),
        P("box", None, "dir", None),
        P(),
        P(),
        P(None, None, "dir", None),
        P(None, None, "dir", None),
        P("box"),
        P("box"),
        P("box", None),
        P("box", None),
        P("box"),
        P("box", None),
        P("box", None),
        P("box"),
    )
    out_specs = (
        P("box", None, "dir", None),
        P("box", None, "dir", None),
        P("box", None, "dir", None),
    )
    return jax.shard_map(
        per_device, mesh=mesh, in_specs=in_specs, out_specs=out_specs, check_vma=False
    )
```

```python
import functools
import math

import jax
import jax.numpy as jnp
from jax import lax
from jax.experimental import pallas as pl
from jax.experimental.pallas import tpu as pltpu
from jax.sharding import PartitionSpec as P

phase_scale = 6.0
highest = lax.Precision.HIGHEST


def neighbours(array):
    size = lax.axis_size("box")
    up = [(i, i + 1) for i in range(size - 1)]
    down = [(i + 1, i) for i in range(size - 1)]
    return lax.ppermute(array, "box", up), lax.ppermute(array, "box", down)


def octant_signs(octant):
    first = 1.0 - 2.0 * (octant % 2).astype(jnp.float32)
    second = 1.0 - 2.0 * (octant // 2 % 2).astype(jnp.float32)
    third = 1.0 - 2.0 * (octant // 4 % 2).astype(jnp.float32)
    return (first, second, third)


def phase_block(octant, row_start, row_count, total_rows, col_start, col_count, total_cols):
    angle_rows = (row_start + jnp.arange(row_count, dtype=jnp.int32)).astype(jnp.float32)
    theta = math.pi * (angle_rows + 0.5) / total_rows
    angle_cols = (col_start + jnp.arange(col_count, dtype=jnp.int32)).astype(jnp.float32)
    azimuth = 2.0 * math.pi * angle_cols / total_cols
    sin_theta = jnp.sin(theta)[:, None]
    along_x = sin_theta * jnp.cos(azimuth)[None, :]
    along_y = sin_theta * jnp.sin(azimuth)[None, :]
    along_z = jnp.cos(theta)[:, None] + 0.0 * azimuth[None, :]
    first, second, third = octant_signs(octant)
    argument = phase_scale * (
        first[:, None, None] * along_x
        + second[:, None, None] * along_y
        + third[:, None, None] * along_z
    )
    return (jnp.cos(argument), jnp.sin(argument))


def flipped(index, mask):
    result = index
    bit = 1
    while bit <= mask:
        if mask & bit:
            result = result + bit - 2 * bit * lax.rem(lax.div(index, bit), 2)
        bit *= 2
    return result


def exchange_body(count, around, fields, matrix_ref, x_ref, *refs):
    refs = list(refs)
    out_ref = refs.pop(0)
    if around:
        below_ref, above_ref = refs.pop(0), refs.pop(0)
    got, ready, landed, send_sem, recv_sem = refs[:5]
    me = lax.axis_index("dir")
    planes, depth, width = got.shape[1:]
    rows = ready.shape[2]
    mesh_ids = pl.DeviceIdType.MESH
    barrier = pltpu.get_barrier_semaphore()
    steps = range(count - 1, 0, -1)

    def partner(step):
        if count & (count - 1):
            return lax.rem(me + step, count), lax.rem(me + count - step, count)
        peer = flipped(me, step)
        return peer, peer

    for step in steps:
        pl.semaphore_signal(
            barrier, inc=1, device_id={"dir": partner(step)[0]}, device_id_type=mesh_ids
        )
    greeted = count - 1
    if around:
        box = lax.axis_index("box")
        upper = lax.rem(box + 1, fields)
        lower = lax.rem(box + fields - 1, fields)
        for other in (upper, lower):
            pl.semaphore_signal(
                barrier, inc=1, device_id={"box": other}, device_id_type=mesh_ids
            )
        greeted += 2
    pl.semaphore_wait(barrier, greeted)

    def push(source, target, leg, plane):
        for step in steps:
            peer, _ = partner(step)
            copy = pltpu.make_async_remote_copy(
                src_ref=source.at[peer, plane],
                dst_ref=target.at[me, plane],
                send_sem=send_sem.at[leg, plane, step],
                recv_sem=recv_sem.at[leg, plane, step],
                device_id={"dir": peer},
                device_id_type=mesh_ids,
            )
            copy.start()
            started.append(copy)

    def settle(target, leg, plane):
        for step in steps:
            _, origin = partner(step)
            pltpu.make_async_remote_copy(
                src_ref=target.at[origin, plane],
                dst_ref=target.at[origin, plane],
                send_sem=send_sem.at[leg, plane, step],
                recv_sem=recv_sem.at[leg, plane, step],
                device_id={"dir": origin},
                device_id_type=mesh_ids,
            ).wait_recv()

    started = []
    for plane in range(planes):
        push(x_ref, got, 0, plane)
    got[me] = x_ref[me]
    for plane in range(planes):
        settle(got, 0, plane)
        product = lax.dot_general(
            matrix_ref[...],
            got[:, plane].reshape(count * depth, width),
            (((1 if around else 0,), (0,)), ((), ())),
            precision=lax.Precision.HIGH,
            preferred_element_type=jnp.float32,
        )
        ready[:, plane] = product.reshape(count, rows, width)
        push(ready, landed, 1, plane)
    ring = []
    if around:
        box_send, box_recv = refs[5:7]
        for at, (other, target) in enumerate(((upper, below_ref), (lower, above_ref))):
            copy = pltpu.make_async_remote_copy(
                src_ref=x_ref,
                dst_ref=target,
                send_sem=box_send.at[at],
                recv_sem=box_recv.at[at],
                device_id={"box": other},
                device_id_type=mesh_ids,
            )
            copy.start()
            ring.append(copy)
    landed[me] = ready[me]
    for plane in range(planes):
        settle(landed, 1, plane)
    out_ref[...] = landed[...].reshape(out_ref.shape)
    for copy in started:
        copy.wait_send()
    for copy in ring:
        copy.wait()


def exchange(matrix, x, around, which):
    count, planes, depth, width = x.shape
    rows = matrix.shape[0 if around else 1] // count
    operands = (matrix, x)
    vmem = pl.BlockSpec(memory_space=pltpu.VMEM)
    result = jax.ShapeDtypeStruct((count * planes, rows, width), jnp.float32)
    ring = jax.ShapeDtypeStruct(x.shape, jnp.float32)
    scratch = [
        pltpu.VMEM((count, planes, depth, width), jnp.float32),
        pltpu.VMEM((count, planes, rows, width), jnp.float32),
        pltpu.VMEM((count, planes, rows, width), jnp.float32),
        pltpu.SemaphoreType.DMA((2, planes, count)),
        pltpu.SemaphoreType.DMA((2, planes, count)),
    ]
    if around:
        scratch += [pltpu.SemaphoreType.DMA((2,)), pltpu.SemaphoreType.DMA((2,))]
    return pl.pallas_call(
        functools.partial(exchange_body, count, around, lax.axis_size("box")),
        out_shape=(result, ring, ring) if around else result,
        in_specs=[vmem] * len(operands),
        out_specs=(vmem,) * 3 if around else vmem,
        scratch_shapes=scratch,
        compiler_params=pltpu.CompilerParams(
            collective_id=which, has_side_effects=True, vmem_limit_bytes=16 * 1024 * 1024
        ),
        name="exchange_" + str(which),
    )(*operands)


def translate_body(has_base, *refs):
    source_ref, which_ref, length_ref, before, own, after, ops_ref = refs[:7]
    base_ref = refs[7] if has_base else None
    out_ref, wide, sems = refs[-3:]
    boxes, _, rows, width = own.shape
    copies = [
        pltpu.make_async_copy(part, wide.at[pl.ds(at * boxes, boxes)], sems.at[at])
        for at, part in enumerate((before, own, after))
    ]
    for copy in copies:
        copy.start()
    for copy in copies:
        copy.wait()
    offset = (lax.axis_index("box") - 1) * boxes
    tall = rows
    while tall % 16 == 0 and tall * width > 4096:
        tall //= 2

    def one_box(box, carry):
        length = length_ref[box]
        for start in range(0, rows, tall):
            part = slice(start, start + tall)

            def entry(column, totals):
                real, imag = totals
                at = source_ref[box, column] - offset
                op = which_ref[box, column]
                op_real, op_imag = ops_ref[op, 0, part], ops_ref[op, 1, part]
                re, im = wide[at, 0, part], wide[at, 1, part]
                real = real + (op_real * re - op_imag * im)
                imag = imag + (op_real * im + op_imag * re)
                return real, imag

            if has_base:
                initial = (base_ref[box, 0, part], base_ref[box, 1, part])
            else:
                initial = (jnp.zeros((tall, width), jnp.float32),) * 2
            real, imag = lax.fori_loop(0, length, entry, initial)
            out_ref[box, 0, part] = real
            out_ref[box, 1, part] = imag
        return carry

    lax.fori_loop(0, boxes, one_box, 0)


def translate(own, before, after, operators, source, which_op, length, base, name):
    boxes = own.shape[0]
    vmem = pl.BlockSpec(memory_space=pltpu.VMEM)
    smem = pl.BlockSpec(memory_space=pltpu.SMEM)
    anywhere = pl.BlockSpec(memory_space=pltpu.HBM)
    operands = [source, which_op, length, before, own, after, operators]
    specs = [smem] * 3 + [anywhere] * 3 + [vmem]
    if base is not None:
        operands.append(base)
        specs.append(vmem)
    return pl.pallas_call(
        functools.partial(translate_body, base is not None),
        out_shape=jax.ShapeDtypeStruct(own.shape, jnp.float32),
        in_specs=specs,
        out_specs=vmem,
        scratch_shapes=[
            pltpu.VMEM((3 * boxes,) + own.shape[1:], jnp.float32),
            pltpu.SemaphoreType.DMA((3,)),
        ],
        compiler_params=pltpu.CompilerParams(vmem_limit_bytes=20 * 1024 * 1024),
        name=name,
    )(*operands)


def shift_body(parent_ref, octant_ref, cosine_ref, sine_ref, interp_ref, out_ref):
    children = interp_ref.shape[0]
    offset = lax.axis_index("box") * out_ref.shape[0]
    out_ref[...] = jnp.zeros_like(out_ref)

    def one_child(child, carry):
        slot, octant = parent_ref[child] - offset, octant_ref[child]
        mirrored = octant // 4
        held = octant + mirrored * (7 - 2 * octant)
        sign = (1 - 2 * mirrored).astype(jnp.float32)
        cosine, sine = cosine_ref[held], sign * sine_ref[held]
        real, imag = interp_ref[child, 0], interp_ref[child, 1]
        out_ref[slot, 0] += cosine * real - sine * imag
        out_ref[slot, 1] += sine * real + cosine * imag
        return carry

    lax.fori_loop(0, children, one_child, 0)


def unshift_body(parent_ref, octant_ref, cosine_ref, sine_ref, field_ref, out_ref):
    children = out_ref.shape[0]
    offset = lax.axis_index("box") * field_ref.shape[0]

    def one_child(child, carry):
        slot, octant = parent_ref[child] - offset, octant_ref[child]
        mirrored = octant // 4
        held = octant + mirrored * (7 - 2 * octant)
        sign = (1 - 2 * mirrored).astype(jnp.float32)
        cosine, sine = cosine_ref[held], sign * sine_ref[held]
        real, imag = field_ref[slot, 0], field_ref[slot, 1]
        out_ref[child, 0] = cosine * real + sine * imag
        out_ref[child, 1] = cosine * imag - sine * real
        return carry

    lax.fori_loop(0, children, one_child, 0)


def by_child(body, parent, octant, cosine, sine, values, boxes, name):
    vmem = pl.BlockSpec(memory_space=pltpu.VMEM)
    smem = pl.BlockSpec(memory_space=pltpu.SMEM)
    return pl.pallas_call(
        body,
        out_shape=jax.ShapeDtypeStruct((boxes,) + values.shape[1:], jnp.float32),
        in_specs=[smem] * 2 + [vmem] * 3,
        out_specs=vmem,
        compiler_params=pltpu.CompilerParams(vmem_limit_bytes=16 * 1024 * 1024),
        name=name,
    )(parent, octant, cosine, sine, values)


def within(index, size):
    return jnp.minimum(jnp.maximum(index, 0), size - 1)


def precise(lhs, rhs):
    return lax.dot_general(
        lhs,
        rhs,
        (((1,), (0,)), ((), ())),
        precision=lax.Precision.HIGH,
        preferred_element_type=jnp.float32,
    )


def parent_windows(children, parents, least, most):
    windows = []
    for p in range(parents):
        low = max(least * p, children - most * (parents - p))
        high = min(most * (p + 1), children - least * (parents - 1 - p))
        windows.append((low, high))
    return windows


def fused_body(fields, sizes, *refs):
    tables_h = refs[:8]
    rad_h, incoming_h, theta_h, phi_h, child_ops_h, parent_ops_h = refs[8:14]
    out_ref, local_ref, parent_rad_ref = refs[14:17]
    (theta, phi, phi_t, theta_t, child_ops, parent_ops, near, gathered, spread, rows_in, wide,
     cosine, sine, back, held_rows, partial, other, total, final) = refs[17:36]
    tables = refs[36:44]
    parent_s, octant_s, child_src_s, child_op_s, child_len_s = tables[:5]
    parent_src_s, parent_op_s, parent_len_s = tables[5:]
    (load_sem, pre_send, pre_recv, in_send, in_recv, out_send, out_recv, ring_send,
     ring_recv, parent_send, parent_recv, back_send, back_recv, raw_send, raw_recv, swap_send,
     swap_recv, final_send, final_recv) = refs[44:]
    mesh_ids = pl.DeviceIdType.MESH
    me, box = lax.axis_index("dir"), lax.axis_index("box")
    children = parent_s.shape[0]
    parents, _, rows, width = local_ref.shape
    depth = rad_h.shape[1]
    half = gathered.shape[2]
    chunks, direct, early = len(sizes), 2, 2
    starts = [sum(sizes[:k]) for k in range(chunks)]
    total_rows, total_cols = theta_h.shape[0], width
    z, x = lax.div(me, 2), lax.rem(me, 2)
    side = lax.div(z, 2)
    inner = z == 1 + side
    outer = z != 1 + side

    def at_place(place):
        return {"box": box, "dir": place}

    partner = at_place(2 * z + 1 - x)
    outer_peer = [at_place(6 * side + at) for at in range(2)]
    inner_peers = [at_place(2 * (1 + side) + at) for at in range(2)]
    inner_peer = at_place(2 * (1 + side) + x)
    across_inner = at_place(2 * (2 - side) + x)
    across_inners = [at_place(2 * (2 - side) + at) for at in range(2)]
    across_outers = [at_place(6 * (1 - side) + at) for at in range(2)]
    inner_diagonal = at_place(2 * (1 + side) + 1 - x)
    across_diagonal = at_place(2 * (2 - side) + 1 - x)
    has_lower, has_upper = box > 0, box < fields - 1
    lower, upper = {"box": box - 1, "dir": me}, {"box": box + 1, "dir": me}

    def remote(source, target, send, recv, device):
        return pltpu.make_async_remote_copy(
            src_ref=source, dst_ref=target, send_sem=send, recv_sem=recv,
            device_id=device, device_id_type=mesh_ids,
        )

    def aligned(value, step):
        return pl.ds(pl.multiple_of(value, step), step)

    def part(k):
        return pl.ds(2 * starts[k], 2 * sizes[k])

    own_near = pl.ds(2 * children, 2 * children)
    loads = [
        (rad_h, near.at[own_near]), (theta_h, theta), (phi_h, phi), (incoming_h, local_ref),
        (child_ops_h, child_ops), (parent_ops_h, parent_ops),
    ]
    near_load, theta_load, phi_load, incoming_load, child_load, parent_load = (
        pltpu.make_async_copy(source, target, load_sem.at[at])
        for at, (source, target) in enumerate(loads)
    )
    table_loads = [
        pltpu.make_async_copy(source, target, load_sem.at[6 + at])
        for at, (source, target) in enumerate(zip(tables_h, tables))
    ]
    own_half = pl.ds(pl.multiple_of(x * half, half), half)
    other_half = pl.ds(pl.multiple_of((1 - x) * half, half), half)
    own_depth = aligned(2 * depth * z + depth * x, depth)
    def fill_phases():
        row_at = lax.broadcasted_iota(jnp.int32, (rows, width), 0) + me * rows
        col_at = lax.broadcasted_iota(jnp.int32, (rows, width), 1)
        polar = math.pi * (row_at.astype(jnp.float32) + 0.5) / total_rows
        azimuth = 2.0 * math.pi * col_at.astype(jnp.float32) / total_cols
        sin_polar = jnp.sin(polar)
        along_x = sin_polar * jnp.cos(azimuth)
        along_y = sin_polar * jnp.sin(azimuth)
        along_z = jnp.cos(polar)
        for octant in range(4):
            first, second = 1.0 - 2.0 * (octant % 2), 1.0 - 2.0 * (octant // 2)
            argument = phase_scale * (first * along_x + second * along_y + along_z)
            cosine[octant] = jnp.cos(argument)
            sine[octant] = jnp.sin(argument)

    def greet(device):
        pl.semaphore_signal(barrier, inc=1, device_id=device, device_id_type=mesh_ids)

    barrier = pltpu.get_barrier_semaphore()
    greet(partner)

    @pl.when(inner)
    def _():
        for device in outer_peer + across_inners + across_outers:
            greet(device)

    @pl.when(outer)
    def _():
        for device in inner_peers + across_inners:
            greet(device)

    pl.when(has_lower)(lambda: greet(lower))
    pl.when(has_upper)(lambda: greet(upper))
    for copy in (near_load, *table_loads, theta_load, phi_load):
        copy.start()
    fill_phases()
    near_load.wait()
    pl.semaphore_wait(
        barrier,
        5 + 2 * inner.astype(jnp.int32) + has_lower.astype(jnp.int32) + has_upper.astype(jnp.int32),
    )

    def landed(target, send, recv):
        remote(target, target, send, recv, partner).wait_recv()

    def each(first, count, body):
        for k in range(first, count):
            body(k)

    partner_depth = aligned(2 * depth * z + depth * (1 - x), depth)

    def mine(k, columns):
        return near.at[pl.ds(2 * (children + starts[k]), 2 * sizes[k]), :, columns]

    def trade(k):
        return remote(
            mine(k, other_half), gathered.at[part(k), own_depth], pre_send.at[0], pre_recv.at[k],
            partner,
        )

    def supply(k, relayed, devices):
        target = gathered.at[part(k), own_depth]
        source, device = mine(k, own_half), devices[0]
        if relayed and k < direct:
            source, device = mine(k, other_half), devices[1]
        elif relayed:
            source = target = gathered.at[part(k), partner_depth]
        return remote(source, target, in_send.at[0], in_recv.at[k], device)

    def inner_supply(k, relayed):
        return [supply(k, relayed, (across_inner, across_diagonal))]

    def outer_supply(k, relayed):
        return [
            supply(k, relayed, (inner_peer, inner_diagonal)),
            supply(k, relayed, (across_inner, across_diagonal)),
        ]

    def start(copies):
        for copy in copies:
            copy.start()

    def traded(k):
        landed(gathered.at[part(k), partner_depth], pre_send.at[0], pre_recv.at[k])

    def advance(k, copies):
        traded(k)
        start(copies(k, 1))
        if k + early < chunks:
            trade(k + early).start()
            start(copies(k + early, 0))

    def open_supply(copies):
        for k in range(direct):
            start(copies(k, 0))
            start(copies(k, 1))
        for k in range(direct, direct + early):
            start(copies(k, 0))

    pl.when(inner)(lambda: start([trade(k) for k in range(direct)]))
    start([trade(k) for k in range(direct, direct + early)])
    pl.when(inner)(lambda: open_supply(inner_supply))
    pl.when(outer)(lambda: open_supply(outer_supply))
    rings = ((has_upper, upper, 0), (has_lower, lower, 4 * children))

    def ring_copy(at):
        exists, device, begin = rings[at]
        return remote(
            near.at[own_near], near.at[pl.ds(begin, 2 * children)], ring_send.at[at],
            ring_recv.at[at], device,
        )

    for at in range(2):
        pl.when(rings[at][0])(lambda: ring_copy(at).start())
    pl.when(outer)(lambda: each(direct, chunks, lambda k: advance(k, outer_supply)))
    for copy in (incoming_load, child_load, parent_load):
        copy.start()
    for copy in table_loads:
        copy.wait()
    theta_load.wait()
    phi_load.wait()
    side_rows = aligned(total_rows // 2 * side, total_rows // 2)
    phi_t[...] = phi[...].T
    theta_t[...] = theta[side_rows].T

    def phases(child):
        octant = octant_s[child]
        mirrored = lax.shift_right_logical(octant, 2)
        held = octant + mirrored * (7 - 2 * octant)
        return held, (1 - 2 * mirrored).astype(jnp.float32)

    def out_copy(k, at):
        if at == 0:
            begin, device = 2 * rows * (1 - side) + rows * (1 - x), partner
        else:
            begin, device = 2 * rows * side + rows * (at - 1), outer_peer[at - 1]
        return remote(
            spread.at[part(k), aligned(begin, rows)], rows_in.at[x, part(k)], out_send.at[0],
            out_recv.at[k], device,
        )

    def theta_stage(k):
        if k < direct:
            traded(k)
        if direct <= k + early < chunks:
            advance(k + early, inner_supply)
        gathered[part(k), own_depth] = near[
            pl.ds(2 * (children + starts[k]), 2 * sizes[k]), :, own_half
        ]
        landed(gathered.at[part(k), pl.ds(0, 6 * depth)], in_send.at[0], in_recv.at[k])
        planes = range(2 * starts[k], 2 * (starts[k] + sizes[k]))
        block = jnp.concatenate([gathered[j] for j in planes], axis=1)
        product = precise(theta[side_rows], block)
        for at, j in enumerate(planes):
            spread[j] = product[:, at * half : (at + 1) * half]
        for at in (1, 2, 0):
            out_copy(k, at).start()
        rows_in[x, part(k)] = spread[
            part(k), aligned(2 * rows * (1 - side) + rows * x, rows)
        ]

    windows = parent_windows(children, parents, 2, 6)

    def parent_copy(at, p):
        return remote(
            wide.at[parents + p], wide.at[2 * parents * at + p], parent_send.at[at, p],
            parent_recv.at[at, p], (upper, lower)[at],
        )

    def shift_stage(k):
        pl.when(inner)(
            lambda: landed(rows_in.at[1 - x, part(k)], out_send.at[0], out_recv.at[k])
        )
        pl.when(outer)(lambda: landed(rows_in.at[:, part(k)], out_send.at[0], out_recv.at[k]))
        block = jnp.concatenate(
            [rows_in[at, part(k)].reshape(2 * sizes[k] * rows, half) for at in range(2)], axis=1
        )
        product = precise(block, phi[...])
        members = range(starts[k], starts[k] + sizes[k])
        angles = [phases(child) for child in members]
        slots = [parent_s[child] - box * parents for child in members]
        belongs = [[(slot == p).astype(jnp.float32) for slot in slots] for p in range(parents)]
        for t in range(0, rows, 8):
            tile = slice(t, t + 8)
            moved = []
            for i, (held, sign) in enumerate(angles):
                real = product[2 * i * rows + t : 2 * i * rows + t + 8]
                imag = product[(2 * i + 1) * rows + t : (2 * i + 1) * rows + t + 8]
                cos, sin = cosine[held, tile], sign * sine[held, tile]
                moved.append((cos * real - sin * imag, sin * real + cos * imag))
            for p, (low, high) in enumerate(windows):
                for plane in range(2):
                    terms = [
                        belongs[p][i] * moved[i][plane]
                        for i, child in enumerate(members) if low <= child < high
                    ]
                    if not terms:
                        continue
                    if low not in members:
                        terms.insert(0, wide[parents + p, plane, tile])
                    wide[parents + p, plane, tile] = functools.reduce(jnp.add, terms)
        for p, (low, high) in enumerate(windows):
            if high - 1 in members:
                for at in range(2):
                    pl.when(rings[at][0])(lambda: parent_copy(at, p).start())

    shift_lag = 1

    def up_step(step):
        if step < chunks:
            pl.when(inner)(lambda: theta_stage(step))
        if step >= shift_lag:
            shift_stage(step - shift_lag)

    each(0, chunks + shift_lag, up_step)

    incoming_load.wait()
    parent_load.wait()
    for at, exists in enumerate((has_lower, has_upper)):
        @pl.when(exists)
        def _():
            for p in range(parents):
                landed(wide.at[2 * parents * at + p], parent_send.at[at, p], parent_recv.at[at, p])

    def translate_parent(p):
        length = parent_len_s[p]
        entries = []
        for column in range(parent_src_s.shape[1]):
            at = within(parent_src_s[p, column] - (box - 1) * parents, 3 * parents)
            entries.append((at, parent_op_s[p, column], (column < length).astype(jnp.float32)))
        for t in range(0, rows, 8):
            tile = slice(t, t + 8)
            real, imag = local_ref[p, 0, tile], local_ref[p, 1, tile]
            for at, op, live in entries:
                op_real, op_imag = live * parent_ops[op, 0, tile], live * parent_ops[op, 1, tile]
                re, im = wide[at, 0, tile], wide[at, 1, tile]
                real = real + (op_real * re - op_imag * im)
                imag = imag + (op_real * im + op_imag * re)
            local_ref[p, 0, tile] = real
            local_ref[p, 1, tile] = imag


    z_local = z - 2 * side
    own_rows = aligned(2 * rows * z_local + rows * x, rows)
    partner_rows = aligned(2 * rows * z_local + rows * (1 - x), rows)

    def back_copy(k):
        return remote(
            back.at[1 - x, part(k)], held_rows.at[part(k), own_rows], back_send.at[0],
            back_recv.at[k], partner,
        )

    def raw_copy(k, relayed):
        source, target, device = back.at[x, part(k)], held_rows.at[part(k), own_rows], inner_peer
        if relayed and k < direct:
            source, device = back.at[1 - x, part(k)], inner_diagonal
        elif relayed:
            source = target = held_rows.at[part(k), partner_rows]
        return remote(source, target, raw_send.at[0], raw_recv.at[k], device)

    def unshift_stage(k):
        fields_in = []
        for child in range(starts[k], starts[k] + sizes[k]):
            held, sign = phases(child)
            slot = within(parent_s[child] - box * parents, parents)
            cos, sin = cosine[held], sign * sine[held]
            real, imag = local_ref[slot, 0], local_ref[slot, 1]
            fields_in += [cos * real + sin * imag, cos * imag - sin * real]
        product = precise(jnp.concatenate(fields_in, axis=0), phi_t[...])
        for at in range(2):
            back[at, part(k)] = product[:, at * half : (at + 1) * half].reshape(
                2 * sizes[k], rows, half
            )
        if k >= direct:
            back_copy(k).start()

        @pl.when(inner)
        def _():
            if k < direct:
                back_copy(k).start()
            held_rows[part(k), own_rows] = back[x, part(k)]

        @pl.when(outer)
        def _():
            raw_copy(k, 0).start()
            if k < direct:
                raw_copy(k, 1).start()

    def raise_stage(k):
        if k >= direct:
            landed(held_rows.at[part(k), partner_rows], back_send.at[0], back_recv.at[k])
            raw_copy(k, 1).start()

    def swap_copy(k):
        return remote(
            partial.at[part(k), aligned(4 * depth * (1 - side), 4 * depth)], other.at[part(k)],
            swap_send.at[0], swap_recv.at[k], across_inner,
        )

    def gather_stage(k):
        landed(held_rows.at[part(k), partner_rows], back_send.at[0], back_recv.at[k])
        landed(
            held_rows.at[part(k), aligned(2 * rows * side, 2 * rows)], raw_send.at[0],
            raw_recv.at[k],
        )
        planes = range(2 * starts[k], 2 * (starts[k] + sizes[k]))
        block = jnp.concatenate([held_rows[j] for j in planes], axis=1)
        product = precise(theta_t[...], block)
        for at, j in enumerate(planes):
            partial[j] = product[:, at * half : (at + 1) * half]
        swap_copy(k).start()

    def final_copy(k, at):
        if at == 0:
            begin, device = 2 * depth * (1 - side) + depth * (1 - x), partner
        else:
            begin, device = 2 * depth * side + depth * (at - 1), outer_peer[at - 1]
        return remote(
            total.at[part(k), aligned(begin, depth)], final.at[x, part(k)], final_send.at[0],
            final_recv.at[k], device,
        )

    def combine_stage(k):
        landed(other.at[part(k)], swap_send.at[0], swap_recv.at[k])
        total[part(k)] = partial[part(k), aligned(4 * depth * side, 4 * depth)] + other[part(k)]
        for at in (1, 2, 0):
            final_copy(k, at).start()
        final[x, part(k)] = total[
            part(k), aligned(2 * depth * (1 - side) + depth * x, depth)
        ]

    def child_translate(child, carry):
        real = jnp.zeros((depth, out_ref.shape[2]), jnp.float32)
        imag = real
        length = child_len_s[child]
        for column in range(child_src_s.shape[1]):
            at = 2 * within(child_src_s[child, column] - (box - 1) * children, 3 * children)
            op = child_op_s[child, column]
            live = (column < length).astype(jnp.float32)
            op_real, op_imag = live * child_ops[op, 0], live * child_ops[op, 1]
            re, im = near[at], near[at + 1]
            real = real + (op_real * re - op_imag * im)
            imag = imag + (op_real * im + op_imag * re)
        out_ref[2 * child] = real
        out_ref[2 * child + 1] = imag
        return carry

    def finish_stage(k):
        pl.when(inner)(
            lambda: landed(final.at[1 - x, part(k)], final_send.at[0], final_recv.at[k])
        )
        pl.when(outer)(lambda: landed(final.at[:, part(k)], final_send.at[0], final_recv.at[k]))
        for at in range(2):
            columns = slice(at * half, (at + 1) * half)
            out_ref[part(k), :, columns] += final[at, part(k)]

    child_load.wait()
    for at, (exists, start) in enumerate(((has_lower, 0), (has_upper, 4 * children))):
        @pl.when(exists)
        def _():
            landed(near.at[pl.ds(start, 2 * children)], ring_send.at[at], ring_recv.at[at])

    lag, wait_lag, end_lag = 2, 2, 2

    def down_step(step):
        if step < chunks:
            reached = starts[step] + sizes[step]
            for p, (low, high) in enumerate(windows):
                if starts[step] <= low < reached:
                    translate_parent(p)
            unshift_stage(step)
        if 1 <= step <= chunks:
            pl.when(outer)(lambda: raise_stage(step - 1))
        if lag <= step < chunks + lag:
            pl.when(inner)(lambda: gather_stage(step - lag))
            if step == lag:
                parent_rad_ref[...] = wide[parents : 2 * parents]
            first = starts[step - lag]
            lax.fori_loop(first, first + sizes[step - lag], child_translate, 0)
        if step >= lag + wait_lag:
            pl.when(inner)(lambda: combine_stage(step - lag - wait_lag))
        if step >= lag + wait_lag + end_lag:
            finish_stage(step - lag - wait_lag - end_lag)

    each(0, chunks + lag + wait_lag, down_step)
    each(chunks - end_lag, chunks, finish_stage)

    def settled(target, send):
        remote(target, target, send, final_recv.at[0], partner).wait_send()

    everything = pl.ds(0, 2 * children)
    later = pl.ds(2 * starts[direct], 2 * (children - starts[direct]))

    def settle_inner():
        settled(gathered.at[everything, pl.ds(0, depth)], pre_send.at[0])
        settled(gathered.at[everything, pl.ds(0, 2 * depth)], in_send.at[0])
        settled(spread.at[everything, pl.ds(0, 3 * rows)], out_send.at[0])
        settled(held_rows.at[everything, pl.ds(0, rows)], back_send.at[0])
        settled(partial.at[everything, pl.ds(0, 4 * depth)], swap_send.at[0])
        settled(total.at[everything, pl.ds(0, 3 * depth)], final_send.at[0])

    def settle_outer():
        settled(gathered.at[later, pl.ds(0, depth)], pre_send.at[0])
        settled(gathered.at[everything, pl.ds(0, 4 * depth)], in_send.at[0])
        settled(held_rows.at[later, pl.ds(0, rows)], back_send.at[0])
        settled(held_rows.at[everything, pl.ds(0, 2 * rows)], raw_send.at[0])

    pl.when(inner)(settle_inner)
    pl.when(outer)(settle_outer)
    for at, (exists, device, start) in enumerate(rings):
        @pl.when(exists)
        def _():
            ring_copy(at).wait_send()
            for p in range(parents):
                parent_copy(at, p).wait_send()


def deliver_body(*refs):
    sems = refs[-1]
    count = (len(refs) - 1) // 2
    copies = [
        pltpu.make_async_copy(refs[at], refs[count + at], sems.at[at]) for at in range(count)
    ]
    for copy in copies:
        copy.start()
    for copy in copies:
        copy.wait()


def deliver(*arrays):
    return pl.pallas_call(
        deliver_body,
        out_shape=tuple(jax.ShapeDtypeStruct(array.shape, array.dtype) for array in arrays),
        in_specs=[pl.BlockSpec(memory_space=pltpu.VMEM)] * len(arrays),
        out_specs=(pl.BlockSpec(memory_space=pltpu.HBM),) * len(arrays),
        scratch_shapes=[pltpu.SemaphoreType.DMA((len(arrays),))],
        compiler_params=pltpu.CompilerParams(vmem_limit_bytes=1024 * 1024),
        name="deliver",
    )(*arrays)


def fused(
    child_rad, parent_incoming, theta_interp, phi_interp, child_ops, parent_ops, *tables
):
    children, _, depth, phi_child = child_rad.shape
    parents, _, rows, width = parent_incoming.shape
    total_rows, total_depth = theta_interp.shape
    sizes = (2,) * (children // 2 - 1) + (1, 1)
    chunks = len(sizes)
    half = phi_child // 2
    planes = 2 * children
    vmem = pl.BlockSpec(memory_space=pltpu.VMEM)
    hbm = pl.BlockSpec(memory_space=pltpu.HBM)

    def room(*shape):
        return pltpu.VMEM(shape, jnp.float32)

    dma = pltpu.SemaphoreType.DMA
    scratch = [
        room(total_rows, total_depth),
        room(phi_child, width),
        room(width, phi_child),
        room(total_depth, total_rows // 2),
        room(*child_ops.shape),
        room(*parent_ops.shape),
        room(3 * planes, depth, phi_child),
        room(planes, total_depth, half),
        room(planes, total_rows // 2, half),
        room(2, planes, rows, half),
        room(3 * parents, 2, rows, width),
        room(4, rows, width),
        room(4, rows, width),
        room(2, planes, rows, half),
        room(planes, total_rows // 2, half),
        room(planes, total_depth, half),
        room(planes, total_depth // 2, half),
        room(planes, total_depth // 2, half),
        room(2, planes, depth, half),
        *(pltpu.SMEM(table.shape, jnp.int32) for table in tables),
        dma((14,)),
        dma((1,)),
        dma((chunks,)),
        dma((1,)),
        dma((chunks,)),
        dma((1,)),
        dma((chunks,)),
        dma((2,)),
        dma((2,)),
        dma((2, parents)),
        dma((2, parents)),
        dma((1,)),
        dma((chunks,)),
        dma((1,)),
        dma((chunks,)),
        dma((1,)),
        dma((chunks,)),
        dma((1,)),
        dma((chunks,)),
    ]
    operands = (
        *tables, child_rad.reshape(planes, depth, phi_child), parent_incoming, theta_interp,
        phi_interp, child_ops, parent_ops,
    )
    anterp, local, rad = pl.pallas_call(
        functools.partial(fused_body, lax.axis_size("box"), sizes),
        out_shape=(
            jax.ShapeDtypeStruct((planes, depth, phi_child), jnp.float32),
            jax.ShapeDtypeStruct(parent_incoming.shape, jnp.float32),
            jax.ShapeDtypeStruct(parent_incoming.shape, jnp.float32),
        ),
        in_specs=[hbm] * len(operands),
        out_specs=(vmem,) * 3,
        scratch_shapes=scratch,
        compiler_params=pltpu.CompilerParams(
            collective_id=0, has_side_effects=True, vmem_limit_bytes=40 * 1024 * 1024
        ),
        name="level_pass",
    )(*(pltpu.with_memory_space_constraint(operand, pltpu.HBM) for operand in operands))
    anterp, local, rad = deliver(anterp, local, rad)
    return anterp.reshape(child_rad.shape), local, rad


def per_device(
    child_rad,
    parent_incoming,
    theta_interp,
    phi_interp,
    child_ops,
    parent_ops,
    child_parent,
    child_octant,
    far_child_src,
    far_child_op,
    far_child_len,
    far_parent_src,
    far_parent_op,
    far_parent_len,
):
    child_count, _, theta_child, phi_child = child_rad.shape
    parent_count, _, theta_parent, phi_parent = parent_incoming.shape
    theta_total = theta_interp.shape[0]
    dir_count = lax.axis_size("dir")
    if dir_count == 8 and theta_child % 8 == 0 and phi_child % 256 == 0 and child_count % 2 == 0 and child_count >= 8:
        return fused(
            child_rad, parent_incoming, theta_interp, phi_interp, child_ops, parent_ops, child_parent,
            child_octant, far_child_src, far_child_op, far_child_len, far_parent_src, far_parent_op,
            far_parent_len,
        )
    planes = child_count * 2 // dir_count
    padded = -(-theta_child // 8) * 8
    dir_index = lax.axis_index("dir")
    grow = ((0, 0), (0, 0), (0, padded - theta_child), (0, 0))
    spread = jnp.pad(
        theta_interp.reshape(theta_total, dir_count, theta_child),
        ((0, 0), (0, 0), (0, padded - theta_child)),
    ).reshape(theta_total, dir_count * padded)
    grown = jnp.pad(child_rad, grow)
    theta_done, before, after = exchange(
        spread, grown.reshape(dir_count, planes, padded, phi_child), True, 0
    )
    before = before.reshape(grown.shape)[:, :, :theta_child]
    after = after.reshape(grown.shape)[:, :, :theta_child]
    child_trans = translate(
        child_rad, before, after, child_ops, far_child_src, far_child_op, far_child_len, None,
        "child_translate",
    )
    theta_done = theta_done.reshape(child_count, 2, theta_parent, phi_child)
    interp = jnp.einsum("ncjf,fg->ncjg", theta_done, phi_interp, precision=lax.Precision.HIGH)
    cosine, sine = phase_block(
        jnp.arange(4, dtype=jnp.int32), dir_index * theta_parent, theta_parent, theta_total,
        0, phi_parent, phi_parent,
    )
    parent_rad = by_child(
        shift_body, child_parent, child_octant, cosine, sine, interp, parent_count, "shift"
    )
    before, after = neighbours(parent_rad)
    parent_local = translate(
        parent_rad, before, after, parent_ops, far_parent_src, far_parent_op, far_parent_len,
        parent_incoming, "parent_translate",
    )
    unshift = by_child(
        unshift_body, child_parent, child_octant, cosine, sine, parent_local, child_count, "unshift"
    )
    back_phi = jnp.einsum("ncjg,fg->ncjf", unshift, phi_interp, precision=lax.Precision.HIGH)
    anterp = exchange(
        spread, back_phi.reshape(dir_count, planes, theta_parent, phi_child), False, 1
    )
    anterp = anterp.reshape(child_count, 2, padded, phi_child)[:, :, :theta_child]
    child_local = child_trans + anterp
    return (child_local, parent_local, parent_rad)


def solution(mesh):
    in_specs = (
        P("box", None, "dir", None),
        P("box", None, "dir", None),
        P(),
        P(),
        P(None, None, "dir", None),
        P(None, None, "dir", None),
        P("box"),
        P("box"),
        P("box", None),
        P("box", None),
        P("box"),
        P("box", None),
        P("box", None),
        P("box"),
    )
    out_specs = (
        P("box", None, "dir", None),
        P("box", None, "dir", None),
        P("box", None, "dir", None),
    )
    return jax.shard_map(
        per_device, mesh=mesh, in_specs=in_specs, out_specs=out_specs, check_vma=False
    )
```

```python
import functools
import math

import jax
import jax.numpy as jnp
from jax import lax
from jax.experimental import pallas as pl
from jax.experimental.pallas import tpu as pltpu
from jax.sharding import PartitionSpec as P

phase_scale = 6.0
highest = lax.Precision.HIGHEST


def neighbours(array):
    size = lax.axis_size("box")
    up = [(i, i + 1) for i in range(size - 1)]
    down = [(i + 1, i) for i in range(size - 1)]
    return lax.ppermute(array, "box", up), lax.ppermute(array, "box", down)


def octant_signs(octant):
    first = 1.0 - 2.0 * (octant % 2).astype(jnp.float32)
    second = 1.0 - 2.0 * (octant // 2 % 2).astype(jnp.float32)
    third = 1.0 - 2.0 * (octant // 4 % 2).astype(jnp.float32)
    return (first, second, third)


def phase_block(octant, row_start, row_count, total_rows, col_start, col_count, total_cols):
    angle_rows = (row_start + jnp.arange(row_count, dtype=jnp.int32)).astype(jnp.float32)
    theta = math.pi * (angle_rows + 0.5) / total_rows
    angle_cols = (col_start + jnp.arange(col_count, dtype=jnp.int32)).astype(jnp.float32)
    azimuth = 2.0 * math.pi * angle_cols / total_cols
    sin_theta = jnp.sin(theta)[:, None]
    along_x = sin_theta * jnp.cos(azimuth)[None, :]
    along_y = sin_theta * jnp.sin(azimuth)[None, :]
    along_z = jnp.cos(theta)[:, None] + 0.0 * azimuth[None, :]
    first, second, third = octant_signs(octant)
    argument = phase_scale * (
        first[:, None, None] * along_x
        + second[:, None, None] * along_y
        + third[:, None, None] * along_z
    )
    return (jnp.cos(argument), jnp.sin(argument))


def flipped(index, mask):
    result = index
    bit = 1
    while bit <= mask:
        if mask & bit:
            result = result + bit - 2 * bit * lax.rem(lax.div(index, bit), 2)
        bit *= 2
    return result


def exchange_body(count, around, fields, matrix_ref, x_ref, *refs):
    refs = list(refs)
    out_ref = refs.pop(0)
    if around:
        below_ref, above_ref = refs.pop(0), refs.pop(0)
    got, ready, landed, send_sem, recv_sem = refs[:5]
    me = lax.axis_index("dir")
    planes, depth, width = got.shape[1:]
    rows = ready.shape[2]
    mesh_ids = pl.DeviceIdType.MESH
    barrier = pltpu.get_barrier_semaphore()
    steps = range(count - 1, 0, -1)

    def partner(step):
        if count & (count - 1):
            return lax.rem(me + step, count), lax.rem(me + count - step, count)
        peer = flipped(me, step)
        return peer, peer

    for step in steps:
        pl.semaphore_signal(
            barrier, inc=1, device_id={"dir": partner(step)[0]}, device_id_type=mesh_ids
        )
    greeted = count - 1
    if around:
        box = lax.axis_index("box")
        upper = lax.rem(box + 1, fields)
        lower = lax.rem(box + fields - 1, fields)
        for other in (upper, lower):
            pl.semaphore_signal(
                barrier, inc=1, device_id={"box": other}, device_id_type=mesh_ids
            )
        greeted += 2
    pl.semaphore_wait(barrier, greeted)

    def push(source, target, leg, plane):
        for step in steps:
            peer, _ = partner(step)
            copy = pltpu.make_async_remote_copy(
                src_ref=source.at[peer, plane],
                dst_ref=target.at[me, plane],
                send_sem=send_sem.at[leg, plane, step],
                recv_sem=recv_sem.at[leg, plane, step],
                device_id={"dir": peer},
                device_id_type=mesh_ids,
            )
            copy.start()
            started.append(copy)

    def settle(target, leg, plane):
        for step in steps:
            _, origin = partner(step)
            pltpu.make_async_remote_copy(
                src_ref=target.at[origin, plane],
                dst_ref=target.at[origin, plane],
                send_sem=send_sem.at[leg, plane, step],
                recv_sem=recv_sem.at[leg, plane, step],
                device_id={"dir": origin},
                device_id_type=mesh_ids,
            ).wait_recv()

    started = []
    for plane in range(planes):
        push(x_ref, got, 0, plane)
    got[me] = x_ref[me]
    for plane in range(planes):
        settle(got, 0, plane)
        product = lax.dot_general(
            matrix_ref[...],
            got[:, plane].reshape(count * depth, width),
            (((1 if around else 0,), (0,)), ((), ())),
            precision=lax.Precision.HIGH,
            preferred_element_type=jnp.float32,
        )
        ready[:, plane] = product.reshape(count, rows, width)
        push(ready, landed, 1, plane)
    ring = []
    if around:
        box_send, box_recv = refs[5:7]
        for at, (other, target) in enumerate(((upper, below_ref), (lower, above_ref))):
            copy = pltpu.make_async_remote_copy(
                src_ref=x_ref,
                dst_ref=target,
                send_sem=box_send.at[at],
                recv_sem=box_recv.at[at],
                device_id={"box": other},
                device_id_type=mesh_ids,
            )
            copy.start()
            ring.append(copy)
    landed[me] = ready[me]
    for plane in range(planes):
        settle(landed, 1, plane)
    out_ref[...] = landed[...].reshape(out_ref.shape)
    for copy in started:
        copy.wait_send()
    for copy in ring:
        copy.wait()


def exchange(matrix, x, around, which):
    count, planes, depth, width = x.shape
    rows = matrix.shape[0 if around else 1] // count
    operands = (matrix, x)
    vmem = pl.BlockSpec(memory_space=pltpu.VMEM)
    result = jax.ShapeDtypeStruct((count * planes, rows, width), jnp.float32)
    ring = jax.ShapeDtypeStruct(x.shape, jnp.float32)
    scratch = [
        pltpu.VMEM((count, planes, depth, width), jnp.float32),
        pltpu.VMEM((count, planes, rows, width), jnp.float32),
        pltpu.VMEM((count, planes, rows, width), jnp.float32),
        pltpu.SemaphoreType.DMA((2, planes, count)),
        pltpu.SemaphoreType.DMA((2, planes, count)),
    ]
    if around:
        scratch += [pltpu.SemaphoreType.DMA((2,)), pltpu.SemaphoreType.DMA((2,))]
    return pl.pallas_call(
        functools.partial(exchange_body, count, around, lax.axis_size("box")),
        out_shape=(result, ring, ring) if around else result,
        in_specs=[vmem] * len(operands),
        out_specs=(vmem,) * 3 if around else vmem,
        scratch_shapes=scratch,
        compiler_params=pltpu.CompilerParams(
            collective_id=which, has_side_effects=True, vmem_limit_bytes=16 * 1024 * 1024
        ),
        name="exchange_" + str(which),
    )(*operands)


def translate_body(has_base, *refs):
    source_ref, which_ref, length_ref, before, own, after, ops_ref = refs[:7]
    base_ref = refs[7] if has_base else None
    out_ref, wide, sems = refs[-3:]
    boxes, _, rows, width = own.shape
    copies = [
        pltpu.make_async_copy(part, wide.at[pl.ds(at * boxes, boxes)], sems.at[at])
        for at, part in enumerate((before, own, after))
    ]
    for copy in copies:
        copy.start()
    for copy in copies:
        copy.wait()
    offset = (lax.axis_index("box") - 1) * boxes
    tall = rows
    while tall % 16 == 0 and tall * width > 4096:
        tall //= 2

    def one_box(box, carry):
        length = length_ref[box]
        for start in range(0, rows, tall):
            part = slice(start, start + tall)

            def entry(column, totals):
                real, imag = totals
                at = source_ref[box, column] - offset
                op = which_ref[box, column]
                op_real, op_imag = ops_ref[op, 0, part], ops_ref[op, 1, part]
                re, im = wide[at, 0, part], wide[at, 1, part]
                real = real + (op_real * re - op_imag * im)
                imag = imag + (op_real * im + op_imag * re)
                return real, imag

            if has_base:
                initial = (base_ref[box, 0, part], base_ref[box, 1, part])
            else:
                initial = (jnp.zeros((tall, width), jnp.float32),) * 2
            real, imag = lax.fori_loop(0, length, entry, initial)
            out_ref[box, 0, part] = real
            out_ref[box, 1, part] = imag
        return carry

    lax.fori_loop(0, boxes, one_box, 0)


def translate(own, before, after, operators, source, which_op, length, base, name):
    boxes = own.shape[0]
    vmem = pl.BlockSpec(memory_space=pltpu.VMEM)
    smem = pl.BlockSpec(memory_space=pltpu.SMEM)
    anywhere = pl.BlockSpec(memory_space=pltpu.HBM)
    operands = [source, which_op, length, before, own, after, operators]
    specs = [smem] * 3 + [anywhere] * 3 + [vmem]
    if base is not None:
        operands.append(base)
        specs.append(vmem)
    return pl.pallas_call(
        functools.partial(translate_body, base is not None),
        out_shape=jax.ShapeDtypeStruct(own.shape, jnp.float32),
        in_specs=specs,
        out_specs=vmem,
        scratch_shapes=[
            pltpu.VMEM((3 * boxes,) + own.shape[1:], jnp.float32),
            pltpu.SemaphoreType.DMA((3,)),
        ],
        compiler_params=pltpu.CompilerParams(vmem_limit_bytes=20 * 1024 * 1024),
        name=name,
    )(*operands)


def shift_body(parent_ref, octant_ref, cosine_ref, sine_ref, interp_ref, out_ref):
    children = interp_ref.shape[0]
    offset = lax.axis_index("box") * out_ref.shape[0]
    out_ref[...] = jnp.zeros_like(out_ref)

    def one_child(child, carry):
        slot, octant = parent_ref[child] - offset, octant_ref[child]
        mirrored = octant // 4
        held = octant + mirrored * (7 - 2 * octant)
        sign = (1 - 2 * mirrored).astype(jnp.float32)
        cosine, sine = cosine_ref[held], sign * sine_ref[held]
        real, imag = interp_ref[child, 0], interp_ref[child, 1]
        out_ref[slot, 0] += cosine * real - sine * imag
        out_ref[slot, 1] += sine * real + cosine * imag
        return carry

    lax.fori_loop(0, children, one_child, 0)


def unshift_body(parent_ref, octant_ref, cosine_ref, sine_ref, field_ref, out_ref):
    children = out_ref.shape[0]
    offset = lax.axis_index("box") * field_ref.shape[0]

    def one_child(child, carry):
        slot, octant = parent_ref[child] - offset, octant_ref[child]
        mirrored = octant // 4
        held = octant + mirrored * (7 - 2 * octant)
        sign = (1 - 2 * mirrored).astype(jnp.float32)
        cosine, sine = cosine_ref[held], sign * sine_ref[held]
        real, imag = field_ref[slot, 0], field_ref[slot, 1]
        out_ref[child, 0] = cosine * real + sine * imag
        out_ref[child, 1] = cosine * imag - sine * real
        return carry

    lax.fori_loop(0, children, one_child, 0)


def by_child(body, parent, octant, cosine, sine, values, boxes, name):
    vmem = pl.BlockSpec(memory_space=pltpu.VMEM)
    smem = pl.BlockSpec(memory_space=pltpu.SMEM)
    return pl.pallas_call(
        body,
        out_shape=jax.ShapeDtypeStruct((boxes,) + values.shape[1:], jnp.float32),
        in_specs=[smem] * 2 + [vmem] * 3,
        out_specs=vmem,
        compiler_params=pltpu.CompilerParams(vmem_limit_bytes=16 * 1024 * 1024),
        name=name,
    )(parent, octant, cosine, sine, values)


def within(index, size):
    return jnp.minimum(jnp.maximum(index, 0), size - 1)


def precise(lhs, rhs):
    return lax.dot_general(
        lhs,
        rhs,
        (((1,), (0,)), ((), ())),
        precision=lax.Precision.HIGH,
        preferred_element_type=jnp.float32,
    )


def parent_windows(children, parents, least, most):
    windows = []
    for p in range(parents):
        low = max(least * p, children - most * (parents - p))
        high = min(most * (p + 1), children - least * (parents - 1 - p))
        windows.append((low, high))
    return windows


def fused_body(fields, sizes, *refs):
    tables_h = refs[:8]
    rad_h, incoming_h, theta_h, phi_h, child_ops_h, parent_ops_h = refs[8:14]
    out_ref, local_ref, parent_rad_ref = refs[14:17]
    (theta, phi, phi_t, theta_t, child_ops, parent_ops, near, gathered, spread, rows_in, wide,
     cosine, sine, back, held_rows, partial, other, total, final) = refs[17:36]
    tables = refs[36:44]
    parent_s, octant_s, child_src_s, child_op_s, child_len_s = tables[:5]
    parent_src_s, parent_op_s, parent_len_s = tables[5:]
    (load_sem, pre_send, pre_recv, in_send, in_recv, out_send, out_recv, ring_send,
     ring_recv, parent_send, parent_recv, back_send, back_recv, raw_send, raw_recv, swap_send,
     swap_recv, final_send, final_recv) = refs[44:]
    mesh_ids = pl.DeviceIdType.MESH
    me, box = lax.axis_index("dir"), lax.axis_index("box")
    children = parent_s.shape[0]
    parents, _, rows, width = local_ref.shape
    depth = rad_h.shape[1]
    half = gathered.shape[2]
    chunks, direct, early = len(sizes), 2, 2
    starts = [sum(sizes[:k]) for k in range(chunks)]
    total_rows, total_cols = theta_h.shape[0], width
    z, x = lax.div(me, 2), lax.rem(me, 2)
    side = lax.div(z, 2)
    inner = z == 1 + side
    outer = z != 1 + side

    def at_place(place):
        return {"box": box, "dir": place}

    partner = at_place(2 * z + 1 - x)
    outer_peer = [at_place(6 * side + at) for at in range(2)]
    far_first = (1 - x, x)
    outer_far_first = [at_place(6 * side + at) for at in far_first]
    inner_peers = [at_place(2 * (1 + side) + at) for at in range(2)]
    inner_peer = at_place(2 * (1 + side) + x)
    across_inner = at_place(2 * (2 - side) + x)
    across_inners = [at_place(2 * (2 - side) + at) for at in range(2)]
    across_outers = [at_place(6 * (1 - side) + at) for at in range(2)]
    inner_diagonal = at_place(2 * (1 + side) + 1 - x)
    across_diagonal = at_place(2 * (2 - side) + 1 - x)
    has_lower, has_upper = box > 0, box < fields - 1
    lower, upper = {"box": box - 1, "dir": me}, {"box": box + 1, "dir": me}

    def remote(source, target, send, recv, device):
        return pltpu.make_async_remote_copy(
            src_ref=source, dst_ref=target, send_sem=send, recv_sem=recv,
            device_id=device, device_id_type=mesh_ids,
        )

    def aligned(value, step):
        return pl.ds(pl.multiple_of(value, step), step)

    def part(k):
        return pl.ds(2 * starts[k], 2 * sizes[k])

    own_near = pl.ds(2 * children, 2 * children)
    loads = [
        (rad_h, near.at[own_near]), (theta_h, theta), (phi_h, phi), (incoming_h, local_ref),
        (child_ops_h, child_ops), (parent_ops_h, parent_ops),
    ]
    near_load, theta_load, phi_load, incoming_load, child_load, parent_load = (
        pltpu.make_async_copy(source, target, load_sem.at[at])
        for at, (source, target) in enumerate(loads)
    )
    table_loads = [
        pltpu.make_async_copy(source, target, load_sem.at[6 + at])
        for at, (source, target) in enumerate(zip(tables_h, tables))
    ]
    own_half = pl.ds(pl.multiple_of(x * half, half), half)
    other_half = pl.ds(pl.multiple_of((1 - x) * half, half), half)
    own_depth = aligned(2 * depth * z + depth * x, depth)
    def fill_phases():
        row_at = lax.broadcasted_iota(jnp.int32, (rows, width), 0) + me * rows
        col_at = lax.broadcasted_iota(jnp.int32, (rows, width), 1)
        polar = math.pi * (row_at.astype(jnp.float32) + 0.5) / total_rows
        azimuth = 2.0 * math.pi * col_at.astype(jnp.float32) / total_cols
        sin_polar = jnp.sin(polar)
        along_x = sin_polar * jnp.cos(azimuth)
        along_y = sin_polar * jnp.sin(azimuth)
        along_z = jnp.cos(polar)
        for octant in range(4):
            first, second = 1.0 - 2.0 * (octant % 2), 1.0 - 2.0 * (octant // 2)
            argument = phase_scale * (first * along_x + second * along_y + along_z)
            cosine[octant] = jnp.cos(argument)
            sine[octant] = jnp.sin(argument)

    def greet(device):
        pl.semaphore_signal(barrier, inc=1, device_id=device, device_id_type=mesh_ids)

    barrier = pltpu.get_barrier_semaphore()
    greet(partner)

    @pl.when(inner)
    def _():
        for device in outer_peer + across_inners + across_outers:
            greet(device)

    @pl.when(outer)
    def _():
        for device in inner_peers + across_inners:
            greet(device)

    pl.when(has_lower)(lambda: greet(lower))
    pl.when(has_upper)(lambda: greet(upper))
    for copy in (near_load, *table_loads, theta_load, phi_load):
        copy.start()
    fill_phases()
    near_load.wait()
    pl.semaphore_wait(
        barrier,
        5 + 2 * inner.astype(jnp.int32) + has_lower.astype(jnp.int32) + has_upper.astype(jnp.int32),
    )

    def landed(target, send, recv):
        remote(target, target, send, recv, partner).wait_recv()

    def each(first, count, body):
        for k in range(first, count):
            body(k)

    partner_depth = aligned(2 * depth * z + depth * (1 - x), depth)

    def mine(k, columns):
        return near.at[pl.ds(2 * (children + starts[k]), 2 * sizes[k]), :, columns]

    def trade(k):
        return remote(
            mine(k, other_half), gathered.at[part(k), own_depth], pre_send.at[0], pre_recv.at[k],
            partner,
        )

    def supply(k, relayed, devices):
        target = gathered.at[part(k), own_depth]
        source, device = mine(k, own_half), devices[0]
        if relayed and k < direct:
            source, device = mine(k, other_half), devices[1]
        elif relayed:
            source = target = gathered.at[part(k), partner_depth]
        return remote(source, target, in_send.at[0], in_recv.at[k], device)

    def inner_supply(k, relayed):
        return [supply(k, relayed, (across_inner, across_diagonal))]

    def outer_supply(k, relayed):
        return [
            supply(k, relayed, (across_inner, across_diagonal)),
            supply(k, relayed, (inner_peer, inner_diagonal)),
        ]

    def start(copies):
        for copy in copies:
            copy.start()

    def traded(k):
        landed(gathered.at[part(k), partner_depth], pre_send.at[0], pre_recv.at[k])

    def advance(k, copies):
        traded(k)
        start(copies(k, 1))
        if k + early < chunks:
            trade(k + early).start()
            start(copies(k + early, 0))

    def open_supply(copies):
        for k in range(direct):
            start(copies(k, 0))
            start(copies(k, 1))
        for k in range(direct, direct + early):
            start(copies(k, 0))

    pl.when(inner)(lambda: start([trade(k) for k in range(direct)]))
    start([trade(k) for k in range(direct, direct + early)])
    pl.when(inner)(lambda: open_supply(inner_supply))
    pl.when(outer)(lambda: open_supply(outer_supply))
    rings = ((has_upper, upper, 0), (has_lower, lower, 4 * children))

    def ring_copy(at):
        exists, device, begin = rings[at]
        return remote(
            near.at[own_near], near.at[pl.ds(begin, 2 * children)], ring_send.at[at],
            ring_recv.at[at], device,
        )

    for at in range(2):
        pl.when(rings[at][0])(lambda: ring_copy(at).start())
    pl.when(outer)(lambda: each(direct, chunks, lambda k: advance(k, outer_supply)))
    for copy in (incoming_load, child_load, parent_load):
        copy.start()
    for copy in table_loads:
        copy.wait()
    theta_load.wait()
    phi_load.wait()
    side_rows = aligned(total_rows // 2 * side, total_rows // 2)
    phi_t[...] = phi[...].T
    theta_t[...] = theta[side_rows].T

    def phases(child):
        octant = octant_s[child]
        mirrored = lax.shift_right_logical(octant, 2)
        held = octant + mirrored * (7 - 2 * octant)
        return held, (1 - 2 * mirrored).astype(jnp.float32)

    def out_copy(k, at):
        if at == 0:
            begin, device = 2 * rows * (1 - side) + rows * (1 - x), partner
        else:
            begin, device = 2 * rows * side + rows * far_first[at - 1], outer_far_first[at - 1]
        return remote(
            spread.at[part(k), aligned(begin, rows)], rows_in.at[x, part(k)], out_send.at[0],
            out_recv.at[k], device,
        )

    def theta_stage(k):
        if k < direct:
            traded(k)
        gathered[part(k), own_depth] = near[
            pl.ds(2 * (children + starts[k]), 2 * sizes[k]), :, own_half
        ]
        landed(gathered.at[part(k), pl.ds(0, 6 * depth)], in_send.at[0], in_recv.at[k])
        planes = range(2 * starts[k], 2 * (starts[k] + sizes[k]))
        block = jnp.concatenate([gathered[j] for j in planes], axis=1)
        product = precise(theta[side_rows], block)
        for at, j in enumerate(planes):
            spread[j] = product[:, at * half : (at + 1) * half]
        for at in (1, 2, 0):
            out_copy(k, at).start()
        if direct <= k + early < chunks:
            advance(k + early, inner_supply)
        rows_in[x, part(k)] = spread[
            part(k), aligned(2 * rows * (1 - side) + rows * x, rows)
        ]

    windows = parent_windows(children, parents, 2, 6)

    def parent_copy(at, p):
        return remote(
            wide.at[parents + p], wide.at[2 * parents * at + p], parent_send.at[at, p],
            parent_recv.at[at, p], (upper, lower)[at],
        )

    def shift_stage(k):
        pl.when(inner)(
            lambda: landed(rows_in.at[1 - x, part(k)], out_send.at[0], out_recv.at[k])
        )
        pl.when(outer)(lambda: landed(rows_in.at[:, part(k)], out_send.at[0], out_recv.at[k]))
        block = jnp.concatenate(
            [rows_in[at, part(k)].reshape(2 * sizes[k] * rows, half) for at in range(2)], axis=1
        )
        product = precise(block, phi[...])
        members = range(starts[k], starts[k] + sizes[k])
        angles = [phases(child) for child in members]
        slots = [parent_s[child] - box * parents for child in members]
        belongs = [[(slot == p).astype(jnp.float32) for slot in slots] for p in range(parents)]
        for t in range(0, rows, 8):
            tile = slice(t, t + 8)
            moved = []
            for i, (held, sign) in enumerate(angles):
                real = product[2 * i * rows + t : 2 * i * rows + t + 8]
                imag = product[(2 * i + 1) * rows + t : (2 * i + 1) * rows + t + 8]
                cos, sin = cosine[held, tile], sign * sine[held, tile]
                moved.append((cos * real - sin * imag, sin * real + cos * imag))
            for p, (low, high) in enumerate(windows):
                for plane in range(2):
                    terms = [
                        belongs[p][i] * moved[i][plane]
                        for i, child in enumerate(members) if low <= child < high
                    ]
                    if not terms:
                        continue
                    if low not in members:
                        terms.insert(0, wide[parents + p, plane, tile])
                    wide[parents + p, plane, tile] = functools.reduce(jnp.add, terms)
        for p, (low, high) in enumerate(windows):
            if high - 1 in members:
                for at in range(2):
                    pl.when(rings[at][0])(lambda: parent_copy(at, p).start())

    shift_lag = 1

    def up_step(step):
        if step < chunks:
            pl.when(inner)(lambda: theta_stage(step))
        if step >= shift_lag:
            shift_stage(step - shift_lag)

    each(0, chunks + shift_lag, up_step)

    incoming_load.wait()
    parent_load.wait()
    for at, exists in enumerate((has_lower, has_upper)):
        @pl.when(exists)
        def _():
            for p in range(parents):
                landed(wide.at[2 * parents * at + p], parent_send.at[at, p], parent_recv.at[at, p])

    def translate_parent(p):
        length = parent_len_s[p]
        entries = []
        for column in range(parent_src_s.shape[1]):
            at = within(parent_src_s[p, column] - (box - 1) * parents, 3 * parents)
            entries.append((at, parent_op_s[p, column], (column < length).astype(jnp.float32)))
        for t in range(0, rows, 8):
            tile = slice(t, t + 8)
            real, imag = local_ref[p, 0, tile], local_ref[p, 1, tile]
            for at, op, live in entries:
                op_real, op_imag = live * parent_ops[op, 0, tile], live * parent_ops[op, 1, tile]
                re, im = wide[at, 0, tile], wide[at, 1, tile]
                real = real + (op_real * re - op_imag * im)
                imag = imag + (op_real * im + op_imag * re)
            local_ref[p, 0, tile] = real
            local_ref[p, 1, tile] = imag


    z_local = z - 2 * side
    own_rows = aligned(2 * rows * z_local + rows * x, rows)
    partner_rows = aligned(2 * rows * z_local + rows * (1 - x), rows)

    def back_copy(k):
        return remote(
            back.at[1 - x, part(k)], held_rows.at[part(k), own_rows], back_send.at[0],
            back_recv.at[k], partner,
        )

    def raw_copy(k, relayed):
        source, target, device = back.at[x, part(k)], held_rows.at[part(k), own_rows], inner_peer
        if relayed and k < direct:
            source, device = back.at[1 - x, part(k)], inner_diagonal
        elif relayed:
            source = target = held_rows.at[part(k), partner_rows]
        return remote(source, target, raw_send.at[0], raw_recv.at[k], device)

    def unshift_stage(k):
        fields_in = []
        for child in range(starts[k], starts[k] + sizes[k]):
            held, sign = phases(child)
            slot = within(parent_s[child] - box * parents, parents)
            cos, sin = cosine[held], sign * sine[held]
            real, imag = local_ref[slot, 0], local_ref[slot, 1]
            fields_in += [cos * real + sin * imag, cos * imag - sin * real]
        product = precise(jnp.concatenate(fields_in, axis=0), phi_t[...])
        for at in range(2):
            back[at, part(k)] = product[:, at * half : (at + 1) * half].reshape(
                2 * sizes[k], rows, half
            )
        if k >= direct:
            back_copy(k).start()

        @pl.when(inner)
        def _():
            if k < direct:
                back_copy(k).start()
            held_rows[part(k), own_rows] = back[x, part(k)]

        @pl.when(outer)
        def _():
            raw_copy(k, 0).start()
            if k < direct:
                raw_copy(k, 1).start()

    def raise_stage(k):
        if k >= direct:
            landed(held_rows.at[part(k), partner_rows], back_send.at[0], back_recv.at[k])
            raw_copy(k, 1).start()

    def swap_copy(k):
        return remote(
            partial.at[part(k), aligned(4 * depth * (1 - side), 4 * depth)], other.at[part(k)],
            swap_send.at[0], swap_recv.at[k], across_inner,
        )

    def gather_stage(k):
        landed(held_rows.at[part(k), partner_rows], back_send.at[0], back_recv.at[k])
        landed(
            held_rows.at[part(k), aligned(2 * rows * side, 2 * rows)], raw_send.at[0],
            raw_recv.at[k],
        )
        planes = range(2 * starts[k], 2 * (starts[k] + sizes[k]))
        block = jnp.concatenate([held_rows[j] for j in planes], axis=1)
        product = precise(theta_t[...], block)
        for at, j in enumerate(planes):
            partial[j] = product[:, at * half : (at + 1) * half]
        swap_copy(k).start()

    def final_copy(k, at):
        if at == 0:
            begin, device = 2 * depth * (1 - side) + depth * (1 - x), partner
        else:
            begin, device = 2 * depth * side + depth * far_first[at - 1], outer_far_first[at - 1]
        return remote(
            total.at[part(k), aligned(begin, depth)], final.at[x, part(k)], final_send.at[0],
            final_recv.at[k], device,
        )

    def combine_stage(k):
        landed(other.at[part(k)], swap_send.at[0], swap_recv.at[k])
        total[part(k)] = partial[part(k), aligned(4 * depth * side, 4 * depth)] + other[part(k)]
        for at in (1, 2, 0):
            final_copy(k, at).start()
        final[x, part(k)] = total[
            part(k), aligned(2 * depth * (1 - side) + depth * x, depth)
        ]

    def child_translate(child, carry):
        real = jnp.zeros((depth, out_ref.shape[2]), jnp.float32)
        imag = real
        length = child_len_s[child]
        for column in range(child_src_s.shape[1]):
            at = 2 * within(child_src_s[child, column] - (box - 1) * children, 3 * children)
            op = child_op_s[child, column]
            live = (column < length).astype(jnp.float32)
            op_real, op_imag = live * child_ops[op, 0], live * child_ops[op, 1]
            re, im = near[at], near[at + 1]
            real = real + (op_real * re - op_imag * im)
            imag = imag + (op_real * im + op_imag * re)
        out_ref[2 * child] = real
        out_ref[2 * child + 1] = imag
        return carry

    def finish_stage(k):
        pl.when(inner)(
            lambda: landed(final.at[1 - x, part(k)], final_send.at[0], final_recv.at[k])
        )
        pl.when(outer)(lambda: landed(final.at[:, part(k)], final_send.at[0], final_recv.at[k]))
        for at in range(2):
            columns = slice(at * half, (at + 1) * half)
            out_ref[part(k), :, columns] += final[at, part(k)]

    child_load.wait()
    for at, (exists, start) in enumerate(((has_lower, 0), (has_upper, 4 * children))):
        @pl.when(exists)
        def _():
            landed(near.at[pl.ds(start, 2 * children)], ring_send.at[at], ring_recv.at[at])

    lag, wait_lag, end_lag = 2, 2, 2

    def settled(target, send):
        remote(target, target, send, final_recv.at[0], partner).wait_send()

    everything = pl.ds(0, 2 * children)
    later = pl.ds(2 * starts[direct], 2 * (children - starts[direct]))

    def settle_up_inner():
        settled(gathered.at[everything, pl.ds(0, depth)], pre_send.at[0])
        settled(gathered.at[everything, pl.ds(0, 2 * depth)], in_send.at[0])
        settled(spread.at[everything, pl.ds(0, 3 * rows)], out_send.at[0])

    def settle_up_outer():
        settled(gathered.at[later, pl.ds(0, depth)], pre_send.at[0])
        settled(gathered.at[everything, pl.ds(0, 4 * depth)], in_send.at[0])

    def settle_up():
        pl.when(inner)(settle_up_inner)
        pl.when(outer)(settle_up_outer)
        for at, (exists, device, begin) in enumerate(rings):
            @pl.when(exists)
            def _():
                ring_copy(at).wait_send()
                for p in range(parents):
                    parent_copy(at, p).wait_send()

    def settle_inner():
        settled(held_rows.at[everything, pl.ds(0, rows)], back_send.at[0])
        settled(partial.at[everything, pl.ds(0, 4 * depth)], swap_send.at[0])
        settled(total.at[everything, pl.ds(0, 3 * depth)], final_send.at[0])

    def settle_outer():
        settled(held_rows.at[later, pl.ds(0, rows)], back_send.at[0])
        settled(held_rows.at[everything, pl.ds(0, 2 * rows)], raw_send.at[0])

    def down_step(step):
        if step < chunks:
            reached = starts[step] + sizes[step]
            for p, (low, high) in enumerate(windows):
                if starts[step] <= low < reached:
                    translate_parent(p)
            unshift_stage(step)
        if 1 <= step <= chunks:
            pl.when(outer)(lambda: raise_stage(step - 1))
        if lag <= step < chunks + lag:
            pl.when(inner)(lambda: gather_stage(step - lag))
            if step == lag:
                parent_rad_ref[...] = wide[parents : 2 * parents]
                settle_up()
            first = starts[step - lag]
            lax.fori_loop(first, first + sizes[step - lag], child_translate, 0)
        if step >= lag + wait_lag:
            pl.when(inner)(lambda: combine_stage(step - lag - wait_lag))
        if step >= lag + wait_lag + end_lag:
            finish_stage(step - lag - wait_lag - end_lag)

    each(0, chunks + lag + wait_lag, down_step)
    each(chunks - end_lag, chunks, finish_stage)
    pl.when(inner)(settle_inner)
    pl.when(outer)(settle_outer)


def deliver_body(*refs):
    sems = refs[-1]
    count = (len(refs) - 1) // 2
    copies = [
        pltpu.make_async_copy(refs[at], refs[count + at], sems.at[at]) for at in range(count)
    ]
    for copy in copies:
        copy.start()
    for copy in copies:
        copy.wait()


def deliver(*arrays):
    return pl.pallas_call(
        deliver_body,
        out_shape=tuple(jax.ShapeDtypeStruct(array.shape, array.dtype) for array in arrays),
        in_specs=[pl.BlockSpec(memory_space=pltpu.VMEM)] * len(arrays),
        out_specs=(pl.BlockSpec(memory_space=pltpu.HBM),) * len(arrays),
        scratch_shapes=[pltpu.SemaphoreType.DMA((len(arrays),))],
        compiler_params=pltpu.CompilerParams(vmem_limit_bytes=1024 * 1024),
        name="deliver",
    )(*arrays)


def fused(
    child_rad, parent_incoming, theta_interp, phi_interp, child_ops, parent_ops, *tables
):
    children, _, depth, phi_child = child_rad.shape
    parents, _, rows, width = parent_incoming.shape
    total_rows, total_depth = theta_interp.shape
    sizes = (2,) * (children // 2 - 1) + (1, 1)
    chunks = len(sizes)
    half = phi_child // 2
    planes = 2 * children
    vmem = pl.BlockSpec(memory_space=pltpu.VMEM)
    hbm = pl.BlockSpec(memory_space=pltpu.HBM)

    def room(*shape):
        return pltpu.VMEM(shape, jnp.float32)

    dma = pltpu.SemaphoreType.DMA
    scratch = [
        room(total_rows, total_depth),
        room(phi_child, width),
        room(width, phi_child),
        room(total_depth, total_rows // 2),
        room(*child_ops.shape),
        room(*parent_ops.shape),
        room(3 * planes, depth, phi_child),
        room(planes, total_depth, half),
        room(planes, total_rows // 2, half),
        room(2, planes, rows, half),
        room(3 * parents, 2, rows, width),
        room(4, rows, width),
        room(4, rows, width),
        room(2, planes, rows, half),
        room(planes, total_rows // 2, half),
        room(planes, total_depth, half),
        room(planes, total_depth // 2, half),
        room(planes, total_depth // 2, half),
        room(2, planes, depth, half),
        *(pltpu.SMEM(table.shape, jnp.int32) for table in tables),
        dma((14,)),
        dma((1,)),
        dma((chunks,)),
        dma((1,)),
        dma((chunks,)),
        dma((1,)),
        dma((chunks,)),
        dma((2,)),
        dma((2,)),
        dma((2, parents)),
        dma((2, parents)),
        dma((1,)),
        dma((chunks,)),
        dma((1,)),
        dma((chunks,)),
        dma((1,)),
        dma((chunks,)),
        dma((1,)),
        dma((chunks,)),
    ]
    operands = (
        *tables, child_rad.reshape(planes, depth, phi_child), parent_incoming, theta_interp,
        phi_interp, child_ops, parent_ops,
    )
    anterp, local, rad = pl.pallas_call(
        functools.partial(fused_body, lax.axis_size("box"), sizes),
        out_shape=(
            jax.ShapeDtypeStruct((planes, depth, phi_child), jnp.float32),
            jax.ShapeDtypeStruct(parent_incoming.shape, jnp.float32),
            jax.ShapeDtypeStruct(parent_incoming.shape, jnp.float32),
        ),
        in_specs=[hbm] * len(operands),
        out_specs=(vmem,) * 3,
        scratch_shapes=scratch,
        compiler_params=pltpu.CompilerParams(
            collective_id=0, has_side_effects=True, vmem_limit_bytes=40 * 1024 * 1024
        ),
        name="level_pass",
    )(*(pltpu.with_memory_space_constraint(operand, pltpu.HBM) for operand in operands))
    anterp, local, rad = deliver(anterp, local, rad)
    return anterp.reshape(child_rad.shape), local, rad


def per_device(
    child_rad,
    parent_incoming,
    theta_interp,
    phi_interp,
    child_ops,
    parent_ops,
    child_parent,
    child_octant,
    far_child_src,
    far_child_op,
    far_child_len,
    far_parent_src,
    far_parent_op,
    far_parent_len,
):
    child_count, _, theta_child, phi_child = child_rad.shape
    parent_count, _, theta_parent, phi_parent = parent_incoming.shape
    theta_total = theta_interp.shape[0]
    dir_count = lax.axis_size("dir")
    if dir_count == 8 and theta_child % 8 == 0 and phi_child % 256 == 0 and child_count % 2 == 0 and child_count >= 8:
        return fused(
            child_rad, parent_incoming, theta_interp, phi_interp, child_ops, parent_ops, child_parent,
            child_octant, far_child_src, far_child_op, far_child_len, far_parent_src, far_parent_op,
            far_parent_len,
        )
    planes = child_count * 2 // dir_count
    padded = -(-theta_child // 8) * 8
    dir_index = lax.axis_index("dir")
    grow = ((0, 0), (0, 0), (0, padded - theta_child), (0, 0))
    spread = jnp.pad(
        theta_interp.reshape(theta_total, dir_count, theta_child),
        ((0, 0), (0, 0), (0, padded - theta_child)),
    ).reshape(theta_total, dir_count * padded)
    grown = jnp.pad(child_rad, grow)
    theta_done, before, after = exchange(
        spread, grown.reshape(dir_count, planes, padded, phi_child), True, 0
    )
    before = before.reshape(grown.shape)[:, :, :theta_child]
    after = after.reshape(grown.shape)[:, :, :theta_child]
    child_trans = translate(
        child_rad, before, after, child_ops, far_child_src, far_child_op, far_child_len, None,
        "child_translate",
    )
    theta_done = theta_done.reshape(child_count, 2, theta_parent, phi_child)
    interp = jnp.einsum("ncjf,fg->ncjg", theta_done, phi_interp, precision=lax.Precision.HIGH)
    cosine, sine = phase_block(
        jnp.arange(4, dtype=jnp.int32), dir_index * theta_parent, theta_parent, theta_total,
        0, phi_parent, phi_parent,
    )
    parent_rad = by_child(
        shift_body, child_parent, child_octant, cosine, sine, interp, parent_count, "shift"
    )
    before, after = neighbours(parent_rad)
    parent_local = translate(
        parent_rad, before, after, parent_ops, far_parent_src, far_parent_op, far_parent_len,
        parent_incoming, "parent_translate",
    )
    unshift = by_child(
        unshift_body, child_parent, child_octant, cosine, sine, parent_local, child_count, "unshift"
    )
    back_phi = jnp.einsum("ncjg,fg->ncjf", unshift, phi_interp, precision=lax.Precision.HIGH)
    anterp = exchange(
        spread, back_phi.reshape(dir_count, planes, theta_parent, phi_child), False, 1
    )
    anterp = anterp.reshape(child_count, 2, padded, phi_child)[:, :, :theta_child]
    child_local = child_trans + anterp
    return (child_local, parent_local, parent_rad)


def solution(mesh):
    in_specs = (
        P("box", None, "dir", None),
        P("box", None, "dir", None),
        P(),
        P(),
        P(None, None, "dir", None),
        P(None, None, "dir", None),
        P("box"),
        P("box"),
        P("box", None),
        P("box", None),
        P("box"),
        P("box", None),
        P("box", None),
        P("box"),
    )
    out_specs = (
        P("box", None, "dir", None),
        P("box", None, "dir", None),
        P("box", None, "dir", None),
    )
    return jax.shard_map(
        per_device, mesh=mesh, in_specs=in_specs, out_specs=out_specs, check_vma=False
    )
```

```python
import functools
import math

import jax
import jax.numpy as jnp
from jax import lax
from jax.experimental import pallas as pl
from jax.experimental.pallas import tpu as pltpu
from jax.sharding import PartitionSpec as P

phase_scale = 6.0
highest = lax.Precision.HIGHEST


def neighbours(array):
    size = lax.axis_size("box")
    up = [(i, i + 1) for i in range(size - 1)]
    down = [(i + 1, i) for i in range(size - 1)]
    return lax.ppermute(array, "box", up), lax.ppermute(array, "box", down)


def octant_signs(octant):
    first = 1.0 - 2.0 * (octant % 2).astype(jnp.float32)
    second = 1.0 - 2.0 * (octant // 2 % 2).astype(jnp.float32)
    third = 1.0 - 2.0 * (octant // 4 % 2).astype(jnp.float32)
    return (first, second, third)


def phase_block(octant, row_start, row_count, total_rows, col_start, col_count, total_cols):
    angle_rows = (row_start + jnp.arange(row_count, dtype=jnp.int32)).astype(jnp.float32)
    theta = math.pi * (angle_rows + 0.5) / total_rows
    angle_cols = (col_start + jnp.arange(col_count, dtype=jnp.int32)).astype(jnp.float32)
    azimuth = 2.0 * math.pi * angle_cols / total_cols
    sin_theta = jnp.sin(theta)[:, None]
    along_x = sin_theta * jnp.cos(azimuth)[None, :]
    along_y = sin_theta * jnp.sin(azimuth)[None, :]
    along_z = jnp.cos(theta)[:, None] + 0.0 * azimuth[None, :]
    first, second, third = octant_signs(octant)
    argument = phase_scale * (
        first[:, None, None] * along_x
        + second[:, None, None] * along_y
        + third[:, None, None] * along_z
    )
    return (jnp.cos(argument), jnp.sin(argument))


def flipped(index, mask):
    result = index
    bit = 1
    while bit <= mask:
        if mask & bit:
            result = result + bit - 2 * bit * lax.rem(lax.div(index, bit), 2)
        bit *= 2
    return result


def exchange_body(count, around, fields, matrix_ref, x_ref, *refs):
    refs = list(refs)
    out_ref = refs.pop(0)
    if around:
        below_ref, above_ref = refs.pop(0), refs.pop(0)
    got, ready, landed, send_sem, recv_sem = refs[:5]
    me = lax.axis_index("dir")
    planes, depth, width = got.shape[1:]
    rows = ready.shape[2]
    mesh_ids = pl.DeviceIdType.MESH
    barrier = pltpu.get_barrier_semaphore()
    steps = range(count - 1, 0, -1)

    def partner(step):
        if count & (count - 1):
            return lax.rem(me + step, count), lax.rem(me + count - step, count)
        peer = flipped(me, step)
        return peer, peer

    for step in steps:
        pl.semaphore_signal(
            barrier, inc=1, device_id={"dir": partner(step)[0]}, device_id_type=mesh_ids
        )
    greeted = count - 1
    if around:
        box = lax.axis_index("box")
        upper = lax.rem(box + 1, fields)
        lower = lax.rem(box + fields - 1, fields)
        for other in (upper, lower):
            pl.semaphore_signal(
                barrier, inc=1, device_id={"box": other}, device_id_type=mesh_ids
            )
        greeted += 2
    pl.semaphore_wait(barrier, greeted)

    def push(source, target, leg, plane):
        for step in steps:
            peer, _ = partner(step)
            copy = pltpu.make_async_remote_copy(
                src_ref=source.at[peer, plane],
                dst_ref=target.at[me, plane],
                send_sem=send_sem.at[leg, plane, step],
                recv_sem=recv_sem.at[leg, plane, step],
                device_id={"dir": peer},
                device_id_type=mesh_ids,
            )
            copy.start()
            started.append(copy)

    def settle(target, leg, plane):
        for step in steps:
            _, origin = partner(step)
            pltpu.make_async_remote_copy(
                src_ref=target.at[origin, plane],
                dst_ref=target.at[origin, plane],
                send_sem=send_sem.at[leg, plane, step],
                recv_sem=recv_sem.at[leg, plane, step],
                device_id={"dir": origin},
                device_id_type=mesh_ids,
            ).wait_recv()

    started = []
    for plane in range(planes):
        push(x_ref, got, 0, plane)
    got[me] = x_ref[me]
    for plane in range(planes):
        settle(got, 0, plane)
        product = lax.dot_general(
            matrix_ref[...],
            got[:, plane].reshape(count * depth, width),
            (((1 if around else 0,), (0,)), ((), ())),
            precision=lax.Precision.HIGH,
            preferred_element_type=jnp.float32,
        )
        ready[:, plane] = product.reshape(count, rows, width)
        push(ready, landed, 1, plane)
    ring = []
    if around:
        box_send, box_recv = refs[5:7]
        for at, (other, target) in enumerate(((upper, below_ref), (lower, above_ref))):
            copy = pltpu.make_async_remote_copy(
                src_ref=x_ref,
                dst_ref=target,
                send_sem=box_send.at[at],
                recv_sem=box_recv.at[at],
                device_id={"box": other},
                device_id_type=mesh_ids,
            )
            copy.start()
            ring.append(copy)
    landed[me] = ready[me]
    for plane in range(planes):
        settle(landed, 1, plane)
    out_ref[...] = landed[...].reshape(out_ref.shape)
    for copy in started:
        copy.wait_send()
    for copy in ring:
        copy.wait()


def exchange(matrix, x, around, which):
    count, planes, depth, width = x.shape
    rows = matrix.shape[0 if around else 1] // count
    operands = (matrix, x)
    vmem = pl.BlockSpec(memory_space=pltpu.VMEM)
    result = jax.ShapeDtypeStruct((count * planes, rows, width), jnp.float32)
    ring = jax.ShapeDtypeStruct(x.shape, jnp.float32)
    scratch = [
        pltpu.VMEM((count, planes, depth, width), jnp.float32),
        pltpu.VMEM((count, planes, rows, width), jnp.float32),
        pltpu.VMEM((count, planes, rows, width), jnp.float32),
        pltpu.SemaphoreType.DMA((2, planes, count)),
        pltpu.SemaphoreType.DMA((2, planes, count)),
    ]
    if around:
        scratch += [pltpu.SemaphoreType.DMA((2,)), pltpu.SemaphoreType.DMA((2,))]
    return pl.pallas_call(
        functools.partial(exchange_body, count, around, lax.axis_size("box")),
        out_shape=(result, ring, ring) if around else result,
        in_specs=[vmem] * len(operands),
        out_specs=(vmem,) * 3 if around else vmem,
        scratch_shapes=scratch,
        compiler_params=pltpu.CompilerParams(
            collective_id=which, has_side_effects=True, vmem_limit_bytes=16 * 1024 * 1024
        ),
        name="exchange_" + str(which),
    )(*operands)


def translate_body(has_base, *refs):
    source_ref, which_ref, length_ref, before, own, after, ops_ref = refs[:7]
    base_ref = refs[7] if has_base else None
    out_ref, wide, sems = refs[-3:]
    boxes, _, rows, width = own.shape
    copies = [
        pltpu.make_async_copy(part, wide.at[pl.ds(at * boxes, boxes)], sems.at[at])
        for at, part in enumerate((before, own, after))
    ]
    for copy in copies:
        copy.start()
    for copy in copies:
        copy.wait()
    offset = (lax.axis_index("box") - 1) * boxes
    tall = rows
    while tall % 16 == 0 and tall * width > 4096:
        tall //= 2

    def one_box(box, carry):
        length = length_ref[box]
        for start in range(0, rows, tall):
            part = slice(start, start + tall)

            def entry(column, totals):
                real, imag = totals
                at = source_ref[box, column] - offset
                op = which_ref[box, column]
                op_real, op_imag = ops_ref[op, 0, part], ops_ref[op, 1, part]
                re, im = wide[at, 0, part], wide[at, 1, part]
                real = real + (op_real * re - op_imag * im)
                imag = imag + (op_real * im + op_imag * re)
                return real, imag

            if has_base:
                initial = (base_ref[box, 0, part], base_ref[box, 1, part])
            else:
                initial = (jnp.zeros((tall, width), jnp.float32),) * 2
            real, imag = lax.fori_loop(0, length, entry, initial)
            out_ref[box, 0, part] = real
            out_ref[box, 1, part] = imag
        return carry

    lax.fori_loop(0, boxes, one_box, 0)


def translate(own, before, after, operators, source, which_op, length, base, name):
    boxes = own.shape[0]
    vmem = pl.BlockSpec(memory_space=pltpu.VMEM)
    smem = pl.BlockSpec(memory_space=pltpu.SMEM)
    anywhere = pl.BlockSpec(memory_space=pltpu.HBM)
    operands = [source, which_op, length, before, own, after, operators]
    specs = [smem] * 3 + [anywhere] * 3 + [vmem]
    if base is not None:
        operands.append(base)
        specs.append(vmem)
    return pl.pallas_call(
        functools.partial(translate_body, base is not None),
        out_shape=jax.ShapeDtypeStruct(own.shape, jnp.float32),
        in_specs=specs,
        out_specs=vmem,
        scratch_shapes=[
            pltpu.VMEM((3 * boxes,) + own.shape[1:], jnp.float32),
            pltpu.SemaphoreType.DMA((3,)),
        ],
        compiler_params=pltpu.CompilerParams(vmem_limit_bytes=20 * 1024 * 1024),
        name=name,
    )(*operands)


def shift_body(parent_ref, octant_ref, cosine_ref, sine_ref, interp_ref, out_ref):
    children = interp_ref.shape[0]
    offset = lax.axis_index("box") * out_ref.shape[0]
    out_ref[...] = jnp.zeros_like(out_ref)

    def one_child(child, carry):
        slot, octant = parent_ref[child] - offset, octant_ref[child]
        mirrored = octant // 4
        held = octant + mirrored * (7 - 2 * octant)
        sign = (1 - 2 * mirrored).astype(jnp.float32)
        cosine, sine = cosine_ref[held], sign * sine_ref[held]
        real, imag = interp_ref[child, 0], interp_ref[child, 1]
        out_ref[slot, 0] += cosine * real - sine * imag
        out_ref[slot, 1] += sine * real + cosine * imag
        return carry

    lax.fori_loop(0, children, one_child, 0)


def unshift_body(parent_ref, octant_ref, cosine_ref, sine_ref, field_ref, out_ref):
    children = out_ref.shape[0]
    offset = lax.axis_index("box") * field_ref.shape[0]

    def one_child(child, carry):
        slot, octant = parent_ref[child] - offset, octant_ref[child]
        mirrored = octant // 4
        held = octant + mirrored * (7 - 2 * octant)
        sign = (1 - 2 * mirrored).astype(jnp.float32)
        cosine, sine = cosine_ref[held], sign * sine_ref[held]
        real, imag = field_ref[slot, 0], field_ref[slot, 1]
        out_ref[child, 0] = cosine * real + sine * imag
        out_ref[child, 1] = cosine * imag - sine * real
        return carry

    lax.fori_loop(0, children, one_child, 0)


def by_child(body, parent, octant, cosine, sine, values, boxes, name):
    vmem = pl.BlockSpec(memory_space=pltpu.VMEM)
    smem = pl.BlockSpec(memory_space=pltpu.SMEM)
    return pl.pallas_call(
        body,
        out_shape=jax.ShapeDtypeStruct((boxes,) + values.shape[1:], jnp.float32),
        in_specs=[smem] * 2 + [vmem] * 3,
        out_specs=vmem,
        compiler_params=pltpu.CompilerParams(vmem_limit_bytes=16 * 1024 * 1024),
        name=name,
    )(parent, octant, cosine, sine, values)


def within(index, size):
    return jnp.minimum(jnp.maximum(index, 0), size - 1)


def precise(lhs, rhs):
    return lax.dot_general(
        lhs,
        rhs,
        (((1,), (0,)), ((), ())),
        precision=lax.Precision.HIGH,
        preferred_element_type=jnp.float32,
    )


def parent_windows(children, parents, least, most):
    windows = []
    for p in range(parents):
        low = max(least * p, children - most * (parents - p))
        high = min(most * (p + 1), children - least * (parents - 1 - p))
        windows.append((low, high))
    return windows


def fused_body(fields, sizes, *refs):
    tables_h = refs[:8]
    rad_h, incoming_h, theta_h, phi_h, child_ops_h, parent_ops_h = refs[8:14]
    out_ref, local_ref, parent_rad_ref = refs[14:17]
    (theta, phi, phi_t, theta_t, child_ops, parent_ops, near, gathered, spread, rows_in, wide,
     cosine, sine, back, held_rows, partial, other, total, final) = refs[17:36]
    tables = refs[36:44]
    parent_s, octant_s, child_src_s, child_op_s, child_len_s = tables[:5]
    parent_src_s, parent_op_s, parent_len_s = tables[5:]
    (load_sem, pre_send, pre_recv, in_send, in_recv, out_send, out_recv, ring_send,
     ring_recv, parent_send, parent_recv, back_send, back_recv, raw_send, raw_recv, swap_send,
     swap_recv, final_send, final_recv) = refs[44:]
    mesh_ids = pl.DeviceIdType.MESH
    me, box = lax.axis_index("dir"), lax.axis_index("box")
    children = parent_s.shape[0]
    parents, _, rows, width = local_ref.shape
    depth = rad_h.shape[1]
    half = gathered.shape[2]
    chunks, direct, early = len(sizes), 2, 2
    starts = [sum(sizes[:k]) for k in range(chunks)]
    total_rows, total_cols = theta_h.shape[0], width
    z, x = lax.div(me, 2), lax.rem(me, 2)
    side = lax.div(z, 2)
    inner = z == 1 + side
    outer = z != 1 + side

    def at_place(place):
        return {"box": box, "dir": place}

    partner = at_place(2 * z + 1 - x)
    outer_peer = [at_place(6 * side + at) for at in range(2)]
    far_first = (1 - x, x)
    outer_far_first = [at_place(6 * side + at) for at in far_first]
    inner_peers = [at_place(2 * (1 + side) + at) for at in range(2)]
    inner_peer = at_place(2 * (1 + side) + x)
    across_inner = at_place(2 * (2 - side) + x)
    across_inners = [at_place(2 * (2 - side) + at) for at in range(2)]
    across_outers = [at_place(6 * (1 - side) + at) for at in range(2)]
    inner_diagonal = at_place(2 * (1 + side) + 1 - x)
    across_diagonal = at_place(2 * (2 - side) + 1 - x)
    has_lower, has_upper = box > 0, box < fields - 1
    lower, upper = {"box": box - 1, "dir": me}, {"box": box + 1, "dir": me}

    def remote(source, target, send, recv, device):
        return pltpu.make_async_remote_copy(
            src_ref=source, dst_ref=target, send_sem=send, recv_sem=recv,
            device_id=device, device_id_type=mesh_ids,
        )

    def aligned(value, step):
        return pl.ds(pl.multiple_of(value, step), step)

    def part(k):
        return pl.ds(2 * starts[k], 2 * sizes[k])

    own_near = pl.ds(2 * children, 2 * children)
    loads = [
        (rad_h, near.at[own_near]), (theta_h, theta), (phi_h, phi), (incoming_h, local_ref),
        (child_ops_h, child_ops), (parent_ops_h, parent_ops),
    ]
    near_load, theta_load, phi_load, incoming_load, child_load, parent_load = (
        pltpu.make_async_copy(source, target, load_sem.at[at])
        for at, (source, target) in enumerate(loads)
    )
    table_loads = [
        pltpu.make_async_copy(source, target, load_sem.at[6 + at])
        for at, (source, target) in enumerate(zip(tables_h, tables))
    ]
    own_half = pl.ds(pl.multiple_of(x * half, half), half)
    other_half = pl.ds(pl.multiple_of((1 - x) * half, half), half)
    own_depth = aligned(2 * depth * z + depth * x, depth)
    def fill_phases():
        row_at = lax.broadcasted_iota(jnp.int32, (rows, width), 0) + me * rows
        col_at = lax.broadcasted_iota(jnp.int32, (rows, width), 1)
        polar = math.pi * (row_at.astype(jnp.float32) + 0.5) / total_rows
        azimuth = 2.0 * math.pi * col_at.astype(jnp.float32) / total_cols
        sin_polar = jnp.sin(polar)
        along_x = sin_polar * jnp.cos(azimuth)
        along_y = sin_polar * jnp.sin(azimuth)
        along_z = jnp.cos(polar)
        for octant in range(4):
            first, second = 1.0 - 2.0 * (octant % 2), 1.0 - 2.0 * (octant // 2)
            argument = phase_scale * (first * along_x + second * along_y + along_z)
            cosine[octant] = jnp.cos(argument)
            sine[octant] = jnp.sin(argument)

    def greet(device):
        pl.semaphore_signal(barrier, inc=1, device_id=device, device_id_type=mesh_ids)

    barrier = pltpu.get_barrier_semaphore()
    greet(partner)

    @pl.when(inner)
    def _():
        for device in outer_peer + across_inners + across_outers:
            greet(device)

    @pl.when(outer)
    def _():
        for device in inner_peers + across_inners:
            greet(device)

    pl.when(has_lower)(lambda: greet(lower))
    pl.when(has_upper)(lambda: greet(upper))
    for copy in (near_load, *table_loads, theta_load, phi_load):
        copy.start()
    fill_phases()
    near_load.wait()
    pl.semaphore_wait(
        barrier,
        5 + 2 * inner.astype(jnp.int32) + has_lower.astype(jnp.int32) + has_upper.astype(jnp.int32),
    )

    def landed(target, send, recv):
        remote(target, target, send, recv, partner).wait_recv()

    def each(first, count, body):
        for k in range(first, count):
            body(k)

    partner_depth = aligned(2 * depth * z + depth * (1 - x), depth)

    def mine(k, columns):
        return near.at[pl.ds(2 * (children + starts[k]), 2 * sizes[k]), :, columns]

    def trade(k):
        return remote(
            mine(k, other_half), gathered.at[part(k), own_depth], pre_send.at[0], pre_recv.at[k],
            partner,
        )

    def supply(k, relayed, devices):
        target = gathered.at[part(k), own_depth]
        source, device = mine(k, own_half), devices[0]
        if relayed and k < direct:
            source, device = mine(k, other_half), devices[1]
        elif relayed:
            source = target = gathered.at[part(k), partner_depth]
        return remote(source, target, in_send.at[0], in_recv.at[k], device)

    def inner_supply(k, relayed):
        return [supply(k, relayed, (across_inner, across_diagonal))]

    def outer_supply(k, relayed):
        return [
            supply(k, relayed, (across_inner, across_diagonal)),
            supply(k, relayed, (inner_peer, inner_diagonal)),
        ]

    def start(copies):
        for copy in copies:
            copy.start()

    def traded(k):
        landed(gathered.at[part(k), partner_depth], pre_send.at[0], pre_recv.at[k])

    def advance(k, copies):
        traded(k)
        start(copies(k, 1))
        if k + early < chunks:
            trade(k + early).start()
            start(copies(k + early, 0))

    def open_supply(copies):
        for k in range(1, direct):
            start(copies(k, 0))
            start(copies(k, 1))
        for k in range(direct, direct + early):
            start(copies(k, 0))

    def open_first(copies):
        start(copies(0, 0))
        start(copies(0, 1))

    pl.when(inner)(lambda: open_first(inner_supply))
    pl.when(outer)(lambda: open_first(outer_supply))
    pl.when(inner)(lambda: start([trade(k) for k in range(direct)]))
    start([trade(k) for k in range(direct, direct + early)])
    pl.when(inner)(lambda: open_supply(inner_supply))
    pl.when(outer)(lambda: open_supply(outer_supply))
    rings = ((has_upper, upper, 0), (has_lower, lower, 4 * children))

    def ring_copy(at):
        exists, device, begin = rings[at]
        return remote(
            near.at[own_near], near.at[pl.ds(begin, 2 * children)], ring_send.at[at],
            ring_recv.at[at], device,
        )

    for at in range(2):
        pl.when(rings[at][0])(lambda: ring_copy(at).start())
    pl.when(outer)(lambda: each(direct, chunks, lambda k: advance(k, outer_supply)))
    for copy in (incoming_load, child_load, parent_load):
        copy.start()
    for copy in table_loads:
        copy.wait()
    theta_load.wait()
    phi_load.wait()
    side_rows = aligned(total_rows // 2 * side, total_rows // 2)
    phi_t[...] = phi[...].T
    theta_t[...] = theta[side_rows].T

    def phases(child):
        octant = octant_s[child]
        mirrored = lax.shift_right_logical(octant, 2)
        held = octant + mirrored * (7 - 2 * octant)
        return held, (1 - 2 * mirrored).astype(jnp.float32)

    def out_copy(k, at):
        if at == 0:
            begin, device = 2 * rows * (1 - side) + rows * (1 - x), partner
        else:
            begin, device = 2 * rows * side + rows * far_first[at - 1], outer_far_first[at - 1]
        return remote(
            spread.at[part(k), aligned(begin, rows)], rows_in.at[x, part(k)], out_send.at[0],
            out_recv.at[k], device,
        )

    def theta_stage(k):
        if k < direct:
            traded(k)
        gathered[part(k), own_depth] = near[
            pl.ds(2 * (children + starts[k]), 2 * sizes[k]), :, own_half
        ]
        landed(gathered.at[part(k), pl.ds(0, 6 * depth)], in_send.at[0], in_recv.at[k])
        planes = range(2 * starts[k], 2 * (starts[k] + sizes[k]))
        block = jnp.concatenate([gathered[j] for j in planes], axis=1)
        product = precise(theta[side_rows], block)
        for at, j in enumerate(planes):
            spread[j] = product[:, at * half : (at + 1) * half]
        for at in (1, 2, 0):
            out_copy(k, at).start()
        if direct <= k + early < chunks:
            advance(k + early, inner_supply)
        rows_in[x, part(k)] = spread[
            part(k), aligned(2 * rows * (1 - side) + rows * x, rows)
        ]

    windows = parent_windows(children, parents, 2, 6)

    def parent_copy(at, p):
        return remote(
            wide.at[parents + p], wide.at[2 * parents * at + p], parent_send.at[at, p],
            parent_recv.at[at, p], (upper, lower)[at],
        )

    def shift_stage(k):
        pl.when(inner)(
            lambda: landed(rows_in.at[1 - x, part(k)], out_send.at[0], out_recv.at[k])
        )
        pl.when(outer)(lambda: landed(rows_in.at[:, part(k)], out_send.at[0], out_recv.at[k]))
        block = jnp.concatenate(
            [rows_in[at, part(k)].reshape(2 * sizes[k] * rows, half) for at in range(2)], axis=1
        )
        product = precise(block, phi[...])
        members = range(starts[k], starts[k] + sizes[k])
        angles = [phases(child) for child in members]
        slots = [parent_s[child] - box * parents for child in members]
        belongs = [[(slot == p).astype(jnp.float32) for slot in slots] for p in range(parents)]
        for t in range(0, rows, 8):
            tile = slice(t, t + 8)
            moved = []
            for i, (held, sign) in enumerate(angles):
                real = product[2 * i * rows + t : 2 * i * rows + t + 8]
                imag = product[(2 * i + 1) * rows + t : (2 * i + 1) * rows + t + 8]
                cos, sin = cosine[held, tile], sign * sine[held, tile]
                moved.append((cos * real - sin * imag, sin * real + cos * imag))
            for p, (low, high) in enumerate(windows):
                for plane in range(2):
                    terms = [
                        belongs[p][i] * moved[i][plane]
                        for i, child in enumerate(members) if low <= child < high
                    ]
                    if not terms:
                        continue
                    if low not in members:
                        terms.insert(0, wide[parents + p, plane, tile])
                    wide[parents + p, plane, tile] = functools.reduce(jnp.add, terms)
        for p, (low, high) in enumerate(windows):
            if high - 1 in members:
                for at in range(2):
                    pl.when(rings[at][0])(lambda: parent_copy(at, p).start())

    shift_lag = 1

    def up_step(step):
        if step < chunks:
            pl.when(inner)(lambda: theta_stage(step))
        if step >= shift_lag:
            shift_stage(step - shift_lag)

    each(0, chunks + shift_lag, up_step)

    incoming_load.wait()
    parent_load.wait()
    for at, exists in enumerate((has_lower, has_upper)):
        @pl.when(exists)
        def _():
            for p in range(parents):
                landed(wide.at[2 * parents * at + p], parent_send.at[at, p], parent_recv.at[at, p])

    def translate_parent(p):
        length = parent_len_s[p]
        entries = []
        for column in range(parent_src_s.shape[1]):
            at = within(parent_src_s[p, column] - (box - 1) * parents, 3 * parents)
            entries.append((at, parent_op_s[p, column], (column < length).astype(jnp.float32)))
        for t in range(0, rows, 8):
            tile = slice(t, t + 8)
            real, imag = local_ref[p, 0, tile], local_ref[p, 1, tile]
            for at, op, live in entries:
                op_real, op_imag = live * parent_ops[op, 0, tile], live * parent_ops[op, 1, tile]
                re, im = wide[at, 0, tile], wide[at, 1, tile]
                real = real + (op_real * re - op_imag * im)
                imag = imag + (op_real * im + op_imag * re)
            local_ref[p, 0, tile] = real
            local_ref[p, 1, tile] = imag


    z_local = z - 2 * side
    own_rows = aligned(2 * rows * z_local + rows * x, rows)
    partner_rows = aligned(2 * rows * z_local + rows * (1 - x), rows)

    def back_copy(k):
        return remote(
            back.at[1 - x, part(k)], held_rows.at[part(k), own_rows], back_send.at[0],
            back_recv.at[k], partner,
        )

    def raw_copy(k, relayed):
        source, target, device = back.at[x, part(k)], held_rows.at[part(k), own_rows], inner_peer
        if relayed and k < direct:
            source, device = back.at[1 - x, part(k)], inner_diagonal
        elif relayed:
            source = target = held_rows.at[part(k), partner_rows]
        return remote(source, target, raw_send.at[0], raw_recv.at[k], device)

    def unshift_stage(k):
        fields_in = []
        for child in range(starts[k], starts[k] + sizes[k]):
            held, sign = phases(child)
            slot = within(parent_s[child] - box * parents, parents)
            cos, sin = cosine[held], sign * sine[held]
            real, imag = local_ref[slot, 0], local_ref[slot, 1]
            fields_in += [cos * real + sin * imag, cos * imag - sin * real]
        product = precise(jnp.concatenate(fields_in, axis=0), phi_t[...])
        for at in range(2):
            back[at, part(k)] = product[:, at * half : (at + 1) * half].reshape(
                2 * sizes[k], rows, half
            )
        if k >= direct:
            back_copy(k).start()

        @pl.when(inner)
        def _():
            if k < direct:
                back_copy(k).start()
            held_rows[part(k), own_rows] = back[x, part(k)]

        @pl.when(outer)
        def _():
            raw_copy(k, 0).start()
            if k < direct:
                raw_copy(k, 1).start()

    def raise_stage(k):
        if k >= direct:
            landed(held_rows.at[part(k), partner_rows], back_send.at[0], back_recv.at[k])
            raw_copy(k, 1).start()

    def swap_copy(k):
        return remote(
            partial.at[part(k), aligned(4 * depth * (1 - side), 4 * depth)], other.at[part(k)],
            swap_send.at[0], swap_recv.at[k], across_inner,
        )

    def gather_stage(k):
        landed(held_rows.at[part(k), partner_rows], back_send.at[0], back_recv.at[k])
        landed(
            held_rows.at[part(k), aligned(2 * rows * side, 2 * rows)], raw_send.at[0],
            raw_recv.at[k],
        )
        planes = range(2 * starts[k], 2 * (starts[k] + sizes[k]))
        block = jnp.concatenate([held_rows[j] for j in planes], axis=1)
        product = precise(theta_t[...], block)
        for at, j in enumerate(planes):
            partial[j] = product[:, at * half : (at + 1) * half]
        swap_copy(k).start()

    def final_copy(k, at):
        if at == 0:
            begin, device = 2 * depth * (1 - side) + depth * (1 - x), partner
        else:
            begin, device = 2 * depth * side + depth * far_first[at - 1], outer_far_first[at - 1]
        return remote(
            total.at[part(k), aligned(begin, depth)], final.at[x, part(k)], final_send.at[0],
            final_recv.at[k], device,
        )

    def combine_stage(k):
        landed(other.at[part(k)], swap_send.at[0], swap_recv.at[k])
        total[part(k)] = partial[part(k), aligned(4 * depth * side, 4 * depth)] + other[part(k)]
        for at in (1, 2, 0):
            final_copy(k, at).start()
        final[x, part(k)] = total[
            part(k), aligned(2 * depth * (1 - side) + depth * x, depth)
        ]

    def child_translate(child, carry):
        real = jnp.zeros((depth, out_ref.shape[2]), jnp.float32)
        imag = real
        length = child_len_s[child]
        for column in range(child_src_s.shape[1]):
            at = 2 * within(child_src_s[child, column] - (box - 1) * children, 3 * children)
            op = child_op_s[child, column]
            live = (column < length).astype(jnp.float32)
            op_real, op_imag = live * child_ops[op, 0], live * child_ops[op, 1]
            re, im = near[at], near[at + 1]
            real = real + (op_real * re - op_imag * im)
            imag = imag + (op_real * im + op_imag * re)
        out_ref[2 * child] = real
        out_ref[2 * child + 1] = imag
        return carry

    def finish_stage(k):
        pl.when(inner)(
            lambda: landed(final.at[1 - x, part(k)], final_send.at[0], final_recv.at[k])
        )
        pl.when(outer)(lambda: landed(final.at[:, part(k)], final_send.at[0], final_recv.at[k]))
        for at in range(2):
            columns = slice(at * half, (at + 1) * half)
            out_ref[part(k), :, columns] += final[at, part(k)]

    child_load.wait()
    for at, (exists, start) in enumerate(((has_lower, 0), (has_upper, 4 * children))):
        @pl.when(exists)
        def _():
            landed(near.at[pl.ds(start, 2 * children)], ring_send.at[at], ring_recv.at[at])

    lag, wait_lag, end_lag = 2, 2, 2

    def settled(target, send):
        remote(target, target, send, final_recv.at[0], partner).wait_send()

    everything = pl.ds(0, 2 * children)
    later = pl.ds(2 * starts[direct], 2 * (children - starts[direct]))

    def settle_up_inner():
        settled(gathered.at[everything, pl.ds(0, depth)], pre_send.at[0])
        settled(gathered.at[everything, pl.ds(0, 2 * depth)], in_send.at[0])
        settled(spread.at[everything, pl.ds(0, 3 * rows)], out_send.at[0])

    def settle_up_outer():
        settled(gathered.at[later, pl.ds(0, depth)], pre_send.at[0])
        settled(gathered.at[everything, pl.ds(0, 4 * depth)], in_send.at[0])

    def settle_up():
        pl.when(inner)(settle_up_inner)
        pl.when(outer)(settle_up_outer)
        for at, (exists, device, begin) in enumerate(rings):
            @pl.when(exists)
            def _():
                ring_copy(at).wait_send()
                for p in range(parents):
                    parent_copy(at, p).wait_send()

    def settle_inner():
        settled(held_rows.at[everything, pl.ds(0, rows)], back_send.at[0])
        settled(partial.at[everything, pl.ds(0, 4 * depth)], swap_send.at[0])
        settled(total.at[everything, pl.ds(0, 3 * depth)], final_send.at[0])

    def settle_outer():
        settled(held_rows.at[later, pl.ds(0, rows)], back_send.at[0])
        settled(held_rows.at[everything, pl.ds(0, 2 * rows)], raw_send.at[0])

    def down_step(step):
        if step < chunks:
            reached = starts[step] + sizes[step]
            for p, (low, high) in enumerate(windows):
                if starts[step] <= low < reached:
                    translate_parent(p)
            unshift_stage(step)
        if 1 <= step <= chunks:
            pl.when(outer)(lambda: raise_stage(step - 1))
        if lag <= step < chunks + lag:
            pl.when(inner)(lambda: gather_stage(step - lag))
            if step == lag:
                parent_rad_ref[...] = wide[parents : 2 * parents]
                settle_up()
            first = starts[step - lag]
            lax.fori_loop(first, first + sizes[step - lag], child_translate, 0)
        if step >= lag + wait_lag:
            pl.when(inner)(lambda: combine_stage(step - lag - wait_lag))
        if step >= lag + wait_lag + end_lag:
            finish_stage(step - lag - wait_lag - end_lag)

    each(0, chunks + lag + wait_lag, down_step)
    each(chunks - end_lag, chunks, finish_stage)
    pl.when(inner)(settle_inner)
    pl.when(outer)(settle_outer)


def deliver_body(*refs):
    sems = refs[-1]
    count = (len(refs) - 1) // 2
    copies = [
        pltpu.make_async_copy(refs[at], refs[count + at], sems.at[at]) for at in range(count)
    ]
    for copy in copies:
        copy.start()
    for copy in copies:
        copy.wait()


def deliver(*arrays):
    return pl.pallas_call(
        deliver_body,
        out_shape=tuple(jax.ShapeDtypeStruct(array.shape, array.dtype) for array in arrays),
        in_specs=[pl.BlockSpec(memory_space=pltpu.VMEM)] * len(arrays),
        out_specs=(pl.BlockSpec(memory_space=pltpu.HBM),) * len(arrays),
        scratch_shapes=[pltpu.SemaphoreType.DMA((len(arrays),))],
        compiler_params=pltpu.CompilerParams(vmem_limit_bytes=1024 * 1024),
        name="deliver",
    )(*arrays)


def fused(
    child_rad, parent_incoming, theta_interp, phi_interp, child_ops, parent_ops, *tables
):
    children, _, depth, phi_child = child_rad.shape
    parents, _, rows, width = parent_incoming.shape
    total_rows, total_depth = theta_interp.shape
    sizes = (2,) * (children // 2 - 1) + (1, 1)
    chunks = len(sizes)
    half = phi_child // 2
    planes = 2 * children
    vmem = pl.BlockSpec(memory_space=pltpu.VMEM)
    hbm = pl.BlockSpec(memory_space=pltpu.HBM)

    def room(*shape):
        return pltpu.VMEM(shape, jnp.float32)

    dma = pltpu.SemaphoreType.DMA
    scratch = [
        room(total_rows, total_depth),
        room(phi_child, width),
        room(width, phi_child),
        room(total_depth, total_rows // 2),
        room(*child_ops.shape),
        room(*parent_ops.shape),
        room(3 * planes, depth, phi_child),
        room(planes, total_depth, half),
        room(planes, total_rows // 2, half),
        room(2, planes, rows, half),
        room(3 * parents, 2, rows, width),
        room(4, rows, width),
        room(4, rows, width),
        room(2, planes, rows, half),
        room(planes, total_rows // 2, half),
        room(planes, total_depth, half),
        room(planes, total_depth // 2, half),
        room(planes, total_depth // 2, half),
        room(2, planes, depth, half),
        *(pltpu.SMEM(table.shape, jnp.int32) for table in tables),
        dma((14,)),
        dma((1,)),
        dma((chunks,)),
        dma((1,)),
        dma((chunks,)),
        dma((1,)),
        dma((chunks,)),
        dma((2,)),
        dma((2,)),
        dma((2, parents)),
        dma((2, parents)),
        dma((1,)),
        dma((chunks,)),
        dma((1,)),
        dma((chunks,)),
        dma((1,)),
        dma((chunks,)),
        dma((1,)),
        dma((chunks,)),
    ]
    operands = (
        *tables, child_rad.reshape(planes, depth, phi_child), parent_incoming, theta_interp,
        phi_interp, child_ops, parent_ops,
    )
    anterp, local, rad = pl.pallas_call(
        functools.partial(fused_body, lax.axis_size("box"), sizes),
        out_shape=(
            jax.ShapeDtypeStruct((planes, depth, phi_child), jnp.float32),
            jax.ShapeDtypeStruct(parent_incoming.shape, jnp.float32),
            jax.ShapeDtypeStruct(parent_incoming.shape, jnp.float32),
        ),
        in_specs=[hbm] * len(operands),
        out_specs=(vmem,) * 3,
        scratch_shapes=scratch,
        compiler_params=pltpu.CompilerParams(
            collective_id=0, has_side_effects=True, vmem_limit_bytes=40 * 1024 * 1024
        ),
        name="level_pass",
    )(*(pltpu.with_memory_space_constraint(operand, pltpu.HBM) for operand in operands))
    anterp, local, rad = deliver(anterp, local, rad)
    return anterp.reshape(child_rad.shape), local, rad


def per_device(
    child_rad,
    parent_incoming,
    theta_interp,
    phi_interp,
    child_ops,
    parent_ops,
    child_parent,
    child_octant,
    far_child_src,
    far_child_op,
    far_child_len,
    far_parent_src,
    far_parent_op,
    far_parent_len,
):
    child_count, _, theta_child, phi_child = child_rad.shape
    parent_count, _, theta_parent, phi_parent = parent_incoming.shape
    theta_total = theta_interp.shape[0]
    dir_count = lax.axis_size("dir")
    if dir_count == 8 and theta_child % 8 == 0 and phi_child % 256 == 0 and child_count % 2 == 0 and child_count >= 8:
        return fused(
            child_rad, parent_incoming, theta_interp, phi_interp, child_ops, parent_ops, child_parent,
            child_octant, far_child_src, far_child_op, far_child_len, far_parent_src, far_parent_op,
            far_parent_len,
        )
    planes = child_count * 2 // dir_count
    padded = -(-theta_child // 8) * 8
    dir_index = lax.axis_index("dir")
    grow = ((0, 0), (0, 0), (0, padded - theta_child), (0, 0))
    spread = jnp.pad(
        theta_interp.reshape(theta_total, dir_count, theta_child),
        ((0, 0), (0, 0), (0, padded - theta_child)),
    ).reshape(theta_total, dir_count * padded)
    grown = jnp.pad(child_rad, grow)
    theta_done, before, after = exchange(
        spread, grown.reshape(dir_count, planes, padded, phi_child), True, 0
    )
    before = before.reshape(grown.shape)[:, :, :theta_child]
    after = after.reshape(grown.shape)[:, :, :theta_child]
    child_trans = translate(
        child_rad, before, after, child_ops, far_child_src, far_child_op, far_child_len, None,
        "child_translate",
    )
    theta_done = theta_done.reshape(child_count, 2, theta_parent, phi_child)
    interp = jnp.einsum("ncjf,fg->ncjg", theta_done, phi_interp, precision=lax.Precision.HIGH)
    cosine, sine = phase_block(
        jnp.arange(4, dtype=jnp.int32), dir_index * theta_parent, theta_parent, theta_total,
        0, phi_parent, phi_parent,
    )
    parent_rad = by_child(
        shift_body, child_parent, child_octant, cosine, sine, interp, parent_count, "shift"
    )
    before, after = neighbours(parent_rad)
    parent_local = translate(
        parent_rad, before, after, parent_ops, far_parent_src, far_parent_op, far_parent_len,
        parent_incoming, "parent_translate",
    )
    unshift = by_child(
        unshift_body, child_parent, child_octant, cosine, sine, parent_local, child_count, "unshift"
    )
    back_phi = jnp.einsum("ncjg,fg->ncjf", unshift, phi_interp, precision=lax.Precision.HIGH)
    anterp = exchange(
        spread, back_phi.reshape(dir_count, planes, theta_parent, phi_child), False, 1
    )
    anterp = anterp.reshape(child_count, 2, padded, phi_child)[:, :, :theta_child]
    child_local = child_trans + anterp
    return (child_local, parent_local, parent_rad)


def solution(mesh):
    in_specs = (
        P("box", None, "dir", None),
        P("box", None, "dir", None),
        P(),
        P(),
        P(None, None, "dir", None),
        P(None, None, "dir", None),
        P("box"),
        P("box"),
        P("box", None),
        P("box", None),
        P("box"),
        P("box", None),
        P("box", None),
        P("box"),
    )
    out_specs = (
        P("box", None, "dir", None),
        P("box", None, "dir", None),
        P("box", None, "dir", None),
    )
    return jax.shard_map(
        per_device, mesh=mesh, in_specs=in_specs, out_specs=out_specs, check_vma=False
    )
```
